32 devices in a mesh: groups: 2 (over y), cells: 4 (over z), corners: 2 (over x), kern: 2 (over core).
Axes of the slice: x: 2, y: 2, z: 4, core: 2. Of those that a mesh axis runs over, the one named last changes fastest.
Arguments:
- theta: float32 [64, 128, 128], P(('groups', 'cells')), parts along dimension 0, may hold values from -8 to 8
- target: bfloat16 [16, 128, 128], P(('groups', 'cells')), parts along dimension 0, may hold values from 0 to 1
- kernels: float32 [2, 2, 24, 35, 35], P(None, 'corners', 'kern'), may hold values from -25.33743 to 25.33743
- dose: float32 [2], P('corners'), may hold values from 0.6 to 1
- inst_owner: int32 [128, 1], P(('groups', 'cells')), parts along dimension 0, may hold values from 0 to 3; in each aligned block of 16 rows (0 to 15, 16 to 31, ...) at most 8 rows name the same one
- inst_local: int32 [128], P(('groups', 'cells')), parts along dimension 0, may hold values from 0 to 7
- inst_shift: int32 [128], P(('groups', 'cells')), parts along dimension 0, may hold values from 0 to 127
Outputs:
- theta_out: float32 [64, 128, 128], P(('groups', 'cells'), ('corners', 'kern')), parts along dimension 0
The draws below stay inside these ranges and needn't reach their ends.
There are 2 independent parts, one for each index of `groups`. The reference program is written for one: setup_inputs(seed, part) draws one part's arguments, and reference() takes and returns one part's arrays. A program takes and returns all parts, laid end to end along the dimension named above; an argument that names none is the same for every part. Nothing has to cross between parts.
Inputs may be any that keep to these rules, and one draw needn't show every extreme that they name: `inst_owner`: within the rows of one device (aligned blocks of 16 rows) no owner is named by more than 8 rows, and in some block one owner is named by exactly 8.
All inputs are finite; a program needn't handle non-finite values.
Results may differ from the reference program's by a relative error of at most 0.003.
Values may be sent and summed in bfloat16 or wider, within the bound.
No kernel may reach another device: no remote copies, remote signals or barrier semaphores. Data moves between devices by JAX's collectives and lax.ppermute only.
A program may use at most 64 MiB of HBM per device.

```python
import math
import jax
import jax.numpy as jnp
import numpy as np
from jax import lax

CELL = 128
FREQ = 35
CELLS_DEV = 8
SLOTS = 8
ITERS = 2
KERNELS = 24
CORNERS = 2
CELLS = 32
TILES = 8
INST_DEV = 16
INSTANCES = 64
CAP = 8
N_CELLS = 4


def with_ends(array, own_key, low, largest):
    extent = array.shape
    spot = [jax.random.randint(jax.random.fold_in(own_key, axis), (), 0, extent[axis]) for axis in range(len(extent))]
    array = array.at[tuple(spot)].set(low)
    longest = extent.index(max(extent))
    spot[longest] = (spot[longest] + 1) % extent[longest]
    return array.at[tuple(spot)].set(largest)


def level_of(rng, extent, cuts, smallest, high):
    factor_of, own = 1.0, jax.random.fold_in(rng, 6)
    for axis_at, shards_of in cuts:
        draws = jnp.exp(jax.random.uniform(jax.random.fold_in(own, axis_at), (shards_of,), jnp.float32, smallest / len(cuts), high / len(cuts)))
        factor_of = factor_of * jnp.repeat(draws, extent[axis_at] // shards_of).reshape([-1 if axis == axis_at else 1 for axis in range(len(extent))])
    return factor_of


def deal_out(key, own, number, rows, amount, top, reach, lean):
    order = jax.random.permutation(key, amount)
    heavy_load, common = portions_of(amount, rows * top, reach, lean, True), portions_of(amount, rows * top, reach, lean, False)
    places = jnp.arange(amount)

    def named(sizes, offset_by):
        used = int((sizes > 0).sum())
        fixed = max(1, used // 4)
        passed = fixed + (places - fixed + offset_by * (used - fixed)) % max(1, amount - fixed)
        return jnp.zeros((amount,), jnp.int32).at[order[jnp.where(places < fixed, places, passed)]].set(jnp.asarray(sizes, jnp.int32))

    sizes = jnp.where(number % 4 == 0, named(heavy_load, number // 4), named(common, number - number // 4 - 1))
    mixed = jax.random.permutation(jax.random.fold_in(own, 3), amount)
    donor, receiver = mixed[0:amount // 2 * 2:2], mixed[1:amount // 2 * 2:2]
    slack = jnp.minimum(sizes[donor] - 1, reach - sizes[receiver]) // 2
    slack = jnp.where((donor == order[0]) | (receiver == order[0]) | (sizes[receiver] == 0), 0, jnp.maximum(slack, 0))
    passed = jax.random.randint(jax.random.fold_in(own, 4), (amount // 2,), 0, 1 << 20) % (slack + 1)
    sizes = sizes.at[donor].add(-passed).at[receiver].add(passed)
    items = jnp.searchsorted(jnp.cumsum(sizes), jnp.arange(rows * top), side="right").astype(jnp.int32)
    table = items.reshape(top, rows).T
    table = table[jax.random.permutation(jax.random.fold_in(own, 1), rows)]
    offset_by = jax.random.randint(jax.random.fold_in(own, 2), (rows, 1), 0, top)
    return jnp.take_along_axis(table, (jnp.arange(top)[None, :] + offset_by) % top, axis=1)


def portions_of(amount, total, most, slope, full):
    weights = [(1 << 20) // math.isqrt(rank ** slope) + 1 for rank in range(1, amount + 1)]
    largest = most if full else min(most, max(-(-total // amount), total * weights[0] // sum(weights)))
    least = 1 if total - largest >= amount - 1 else 0
    counts, surplus = [largest] + [least] * (amount - 1), total - largest - least * (amount - 1)
    while surplus > 0:
        movable = [i for i in range(1, amount) if counts[i] < largest] or [i for i in range(1, amount) if counts[i] < most]
        whole, budget = sum([weights[i] for i in movable]), surplus
        for i in movable:
            extra = min(most - counts[i], max(1, budget * weights[i] // whole), surplus)
            counts[i] = counts[i] + extra
            surplus = surplus - extra
    return np.array(counts)


def scatter_about(key, dims, spread, limit, cuts=(), held_as=jnp.bfloat16):
    array = jax.random.normal(key, dims, jnp.float32) * spread
    if len(cuts) > 0:
        array = level_of(key, dims, cuts, -0.22, 0.18) * array
    return jnp.clip(array, min=-limit, max=limit).astype(held_as)


def setup_inputs(seed: int = 0, part: int = 0) -> dict:
    seeds = jax.random.split(jax.random.key(seed), 8)
    part_keys = jax.random.split(jax.random.fold_in(seeds[7], part), 8)
    theta = scatter_about(part_keys[0], (CELLS, CELL, CELL), 2.0, 8.0, ((0, 4),), jnp.float32)
    target = jnp.clip(1.0 * jax.random.uniform(part_keys[1], (TILES, CELL, CELL), jnp.float32) ** level_of(part_keys[1], (TILES, CELL, CELL), ((0, 4),), -0.2, 0.2), 0.0, 1.0).astype(jnp.bfloat16)
    kernels = scatter_about(seeds[2], (2, CORNERS, KERNELS, FREQ, FREQ), (2.0 * CELL * SLOTS ** 0.5 / (FREQ * KERNELS ** 0.5)), 25.33743, ((1, 2), (2, 2)), jnp.float32)
    dose = jnp.clip(0.6 + 0.39999998 * jax.random.uniform(seeds[3], (CORNERS,), jnp.float32) ** level_of(seeds[3], (CORNERS,), ((0, 2),), -0.2, 0.2), 0.6, 1.0)
    inst_owner_keys = jax.random.split(jax.random.fold_in(part_keys[4], 1), INSTANCES // INST_DEV)
    inst_owner_turns = jax.random.permutation(jax.random.fold_in(part_keys[4], 3), INSTANCES // INST_DEV)
    inst_owner = jax.vmap(lambda own, number: deal_out(jax.random.fold_in(part_keys[4], 2), own, number, INST_DEV, N_CELLS, 1, CAP, 2))(inst_owner_keys, inst_owner_turns).reshape((INSTANCES, 1))
    inst_local = with_ends(jax.random.randint(part_keys[5], (INSTANCES,), 0, CELLS_DEV), jax.random.fold_in(part_keys[5], 1), 0, CELLS_DEV - 1).astype(jnp.int32)
    inst_shift = with_ends(jax.random.randint(part_keys[6], (INSTANCES,), 0, CELL), jax.random.fold_in(part_keys[6], 1), 0, CELL - 1).astype(jnp.int32)
    return {"theta": theta, "target": target, "kernels": kernels, "dose": dose, "inst_owner": inst_owner, "inst_local": inst_local, "inst_shift": inst_shift}


LR = 0.25
EPS = 1e-06
STEEP = 3.0

def tables(cell_size, freq_count):
    freqs = jnp.arange(freq_count, dtype=jnp.int32) - freq_count // 2
    pixels = jnp.arange(cell_size, dtype=jnp.int32)
    phase = (freqs[:, None] * pixels[None, :] % cell_size).astype(jnp.float32) * (2.0 * math.pi / cell_size)
    fwd_real = jnp.cos(phase)
    fwd_imag = -jnp.sin(phase)
    inv_real = fwd_real.T / cell_size
    inv_imag = -fwd_imag.T / cell_size
    return (fwd_real, fwd_imag, inv_real, inv_imag)

def spectrum(field, tabs):
    fwd_real, fwd_imag = (tabs[0], tabs[1])
    hp = lax.Precision.HIGHEST
    left_real = jnp.einsum('fx,txy->tfy', fwd_real, field, precision=hp)
    left_imag = jnp.einsum('fx,txy->tfy', fwd_imag, field, precision=hp)
    spec_real = jnp.einsum('tfy,gy->tfg', left_real, fwd_real, precision=hp) - jnp.einsum('tfy,gy->tfg', left_imag, fwd_imag, precision=hp)
    spec_imag = jnp.einsum('tfy,gy->tfg', left_real, fwd_imag, precision=hp) + jnp.einsum('tfy,gy->tfg', left_imag, fwd_real, precision=hp)
    return (spec_real, spec_imag)

def intensity(field, kern_real, kern_imag, tabs):
    inv_real, inv_imag = (tabs[2], tabs[3])
    hp = lax.Precision.HIGHEST
    spec_real, spec_imag = spectrum(field, tabs)

    def add_kernel(running, pair):
        resp_real = pair[0] * spec_real - pair[1] * spec_imag
        resp_imag = pair[0] * spec_imag + pair[1] * spec_real
        half_real = jnp.einsum('tfg,yg->tfy', resp_real, inv_real, precision=hp) - jnp.einsum('tfg,yg->tfy', resp_imag, inv_imag, precision=hp)
        half_imag = jnp.einsum('tfg,yg->tfy', resp_real, inv_imag, precision=hp) + jnp.einsum('tfg,yg->tfy', resp_imag, inv_real, precision=hp)
        near_real = jnp.einsum('xf,tfy->txy', inv_real, half_real, precision=hp) - jnp.einsum('xf,tfy->txy', inv_imag, half_imag, precision=hp)
        near_imag = jnp.einsum('xf,tfy->txy', inv_real, half_imag, precision=hp) + jnp.einsum('xf,tfy->txy', inv_imag, half_real, precision=hp)
        return (running + near_real * near_real + near_imag * near_imag, None)
    start = jnp.zeros(field.shape, jnp.float32)
    result, unused = lax.scan(add_kernel, start, (kern_real, kern_imag))
    return result

def reference(theta, target, kernels, dose, inst_owner, inst_local, inst_shift):
    tabs = tables(CELL, FREQ)
    cell_ids = (inst_owner[:, 0] * CELLS_DEV + inst_local).astype(jnp.int32)
    wanted = target.astype(jnp.float32)

    def build(cell_params):
        rounded = jax.nn.sigmoid(cell_params).astype(jnp.bfloat16)
        mask_vals = lax.optimization_barrier(rounded).astype(jnp.float32)
        placed = jnp.take(2.0 * mask_vals - 1.0, cell_ids, axis=0)
        rolled = jax.vmap(lambda plane, offset: jnp.roll(plane, offset, axis=1))(placed, inst_shift)
        return lax.optimization_barrier(jnp.sum(rolled.reshape(TILES, SLOTS, CELL, CELL), axis=1)) / SLOTS
    cell_params = theta
    for iteration in range(ITERS):
        field = build(cell_params)

        def corner_grad(inputs):
            kern_real, kern_imag, dose_now = inputs
            image, pullback = jax.vjp(lambda plane: intensity(plane, kern_real, kern_imag, tabs), field)
            resist = jax.nn.sigmoid(STEEP * (dose_now * image - 1.0))
            pressure = 2.0 * (resist - wanted) * resist * (1.0 - resist) * STEEP * dose_now
            return pullback(pressure)[0]
        tile_grads = lax.optimization_barrier(jnp.sum(lax.map(corner_grad, (kernels[0], kernels[1], dose)), axis=0))
        inst_grads = jnp.repeat(tile_grads, SLOTS, axis=0)
        unrolled = jax.vmap(lambda plane, offset: jnp.roll(plane, -offset, axis=1))(inst_grads, inst_shift)
        cell_sums = jax.ops.segment_sum(unrolled, cell_ids, num_segments=CELLS)
        squash = jax.nn.sigmoid(cell_params)
        gradient = cell_sums * (2.0 / SLOTS) * squash * (1.0 - squash)
        squares = lax.optimization_barrier(jnp.sum(gradient * gradient, axis=(1, 2)))
        cell_params = cell_params - LR * gradient / jnp.sqrt(squares / (CELL * CELL) + EPS)[:, None, None]
    return cell_params
```

```python
import functools

import jax
import jax.numpy as jnp
import numpy as np
from jax import lax
from jax.experimental import pallas as pl
from jax.experimental.pallas import tpu as pltpu
from jax.sharding import PartitionSpec as P

ITERS = 2
LR = 0.25
EPS = 1e-06
STEEP = 3.0
LANES = 128
HALF = LANES // 2
INFO = 16
BF = jnp.bfloat16
F32 = jnp.float32


def up(value, step):
    return -(-value // step) * step


def split(array):
    high = np.asarray(array, np.float32).astype(BF)
    low = (np.asarray(array, np.float32) - high.astype(np.float32)).astype(BF)
    return high, low


class Tables:
    def __init__(self, cell, freq):
        self.cell, self.freq = cell, freq
        self.mid = freq // 2
        self.rows = up(self.mid + 1, 8)
        self.grid = min(cell, up(4 * self.mid + 1, 8))
        rows, grid, mid = self.rows, self.grid, self.mid
        turn = 2.0 * np.pi / cell
        f = np.arange(mid + 1)
        g = np.arange(freq) - mid
        pixels = np.arange(cell)
        fy = np.zeros((cell, LANES))
        phase = (pixels[:, None] * g[None, :] % cell) * turn
        fy[:, :freq] = np.cos(phase)
        fy[:, HALF : HALF + freq] = -np.sin(phase)
        self.fy = np.concatenate(split(fy), axis=1)
        fx = np.zeros((2 * rows, cell))
        phase = (f[:, None] * pixels[None, :] % cell) * turn
        fx[: mid + 1] = np.cos(phase)
        fx[rows : rows + mid + 1] = np.sin(phase)
        self.fx = np.concatenate(split(fx), axis=0)
        ex = np.concatenate([fx[:rows].T, -fx[rows:].T], axis=1)
        self.ex = ex.astype(np.float32)
        gy = np.zeros((LANES, 2 * cell))
        phase = (g[:, None] * pixels[None, :] % cell) * turn
        gy[:freq, :cell] = np.cos(phase)
        gy[:freq, cell:] = np.sin(phase)
        gy[HALF : HALF + freq, :cell] = -np.sin(phase)
        gy[HALF : HALF + freq, cell:] = np.cos(phase)
        self.gy = gy.astype(np.float32)
        both = np.concatenate([gy, np.roll(gy, HALF, axis=0)], axis=0)
        self.gyy = both.astype(np.float32).astype(BF)
        self.gyy_t = self.gyy.T.copy()
        gx = np.zeros((2 * grid, 4 * rows))
        phase = (f[None, :] * np.arange(grid)[:, None] % grid) * (2.0 * np.pi / grid)
        cos, sin = np.zeros((grid, rows)), np.zeros((grid, rows))
        cos[:, : mid + 1], sin[:, : mid + 1] = np.cos(phase), np.sin(phase)
        gx[:grid] = np.concatenate([cos, cos, -sin, -sin], axis=1)
        gx[grid:] = np.concatenate([sin, -sin, cos, -cos], axis=1)
        self.gx = gx.astype(np.float32).astype(BF)
        self.gx_t = self.gx.T.copy()
        u = np.arange(-2 * mid, 2 * mid + 1)
        if grid == cell:
            weights = np.eye(cell)
        else:
            diff = pixels[:, None] / cell - np.arange(grid)[None, :] / grid
            weights = np.cos(2.0 * np.pi * diff[:, :, None] * u).sum(-1) / grid
        self.w = weights.astype(np.float32)
        self.w_t = self.w.T.copy()
        ph = np.zeros((cell, 2 * LANES))
        phase = (pixels[:, None] * g[None, :] % cell) * turn
        ph[:, :freq] = ph[:, HALF : HALF + freq] = np.cos(phase)
        ph[:, LANES : LANES + freq] = np.sin(phase)
        ph[:, LANES + HALF : LANES + HALF + freq] = -np.sin(phase)
        self.ph = ph.astype(np.float32)
        self.ph_split = np.concatenate(split(ph), axis=1)
        pick_u, pick_v = np.zeros((rows, freq)), np.zeros((rows, freq))
        for row in range(mid + 1):
            pick_u[row, mid + row] = 1.0
            if row > 0:
                pick_v[row, mid - row] = 1.0
        self.pick = np.stack([pick_u, pick_v]).astype(np.float32).astype(BF)
        lane = np.zeros((4, freq, LANES))
        for col in range(freq):
            lane[0, col, col] = 1.0
            lane[1, col, HALF + col] = 1.0
            lane[2, col, freq - 1 - col] = 1.0
            lane[3, col, HALF + freq - 1 - col] = -1.0
        self.lane = lane.astype(np.float32).astype(BF)


def dot(a, b, **kw):
    return jnp.dot(a, b, preferred_element_type=F32, **kw)


def exact(a, b):
    return dot(a, b, precision=lax.Precision.HIGHEST)


def swap(x):
    return pltpu.roll(x, HALF, 1)


def lane_of(shape):
    return lax.broadcasted_iota(jnp.int32, shape, len(shape) - 1)


def arrange_body(dose, kern, pick, lane, out):
    root = jnp.sqrt(jnp.full((1, 1), dose[0], F32))
    for k in range(out.shape[0]):
        real = (kern[0, 0, k] * root).astype(BF)
        imag = (kern[1, 0, k] * root).astype(BF)
        upper = (dot(real, lane[0]) + dot(imag, lane[1])).astype(BF)
        lower = (dot(real, lane[2]) + dot(imag, lane[3])).astype(BF)
        both = jnp.concatenate([dot(pick[0], upper), dot(pick[1], lower)], axis=0)
        out[k] = both.astype(BF)


def spectra(tabs, slots, theta, fy, fx, out):
    cells, cell, rows = theta.shape[0], tabs.cell, tabs.rows
    mask = jax.nn.sigmoid(theta).astype(BF).reshape(cells * cell, cell)
    along = dot(mask, fy[...])
    along = along[:, :LANES] + along[:, LANES:]
    sign = jnp.where(lane_of((rows, LANES)) < HALF, 1.0, -1.0)
    row_at = lax.broadcasted_iota(jnp.int32, (rows, LANES), 0)
    centre = jnp.where((row_at == 0) & (lane_of((rows, LANES)) == tabs.mid), 1.0 / slots, 0.0)
    scale = 2.0 / (slots * cell * cell)
    for c in range(cells):
        part = along[c * cell : (c + 1) * cell]
        high = part.astype(BF)
        low = (part - high.astype(F32)).astype(BF)
        res = dot(fx[...], jnp.concatenate([high, low], axis=1))
        res = res[: 2 * rows, :LANES] + res[: 2 * rows, LANES:] + res[2 * rows :, :LANES]
        spec = res[:rows] + swap(res[rows:]) * sign
        out[c * rows : (c + 1) * rows] = (spec * scale - centre).astype(BF)


def first_body(tabs, slots, owner, local, shift, theta, fy, fx, out):
    spectra(tabs, slots, theta[...], fy, fx, out)
    base = theta.shape[0] * tabs.rows
    row = lax.broadcasted_iota(jnp.int32, (INFO, LANES), 0)
    col = lane_of((INFO, LANES))
    info = jnp.zeros((INFO, LANES), jnp.int32)
    for i in range(local.shape[0]):
        value = jnp.where(row == 0, owner[i, 0], jnp.where(row == 1, local[i], shift[i]))
        info = jnp.where((col == i) & (row < 3), value, info)
    out[base : base + INFO] = info.astype(F32).astype(BF)


def counts_body(tabs, n, tiles, cells, slots, at, ph, *refs):
    out = refs[-1]
    z = at[0]
    base = cells * tabs.rows
    row = lax.broadcasted_iota(jnp.int32, (tiles * cells, LANES), 0)
    col = lane_of((tiles * cells, LANES))
    shift_at = lax.broadcasted_iota(jnp.int32, (tabs.cell, LANES), 0)
    for k in range(n):
        info = refs[k][base : base + INFO].astype(F32).astype(jnp.int32)
        owner, local, shift = info[0:1], info[1:2], info[2:3]
        mine = (owner == z) & (local == row % cells) & (col // slots == row // cells)
        mine = mine & (col < tiles * slots)
        chosen = jnp.where(mine, 1.0, 0.0).astype(BF)
        hot = jnp.where(shift == shift_at, 1.0, 0.0).astype(BF)
        number = lax.dot_general(
            chosen, hot, (((1,), (1,)), ((), ())), preferred_element_type=F32
        ).astype(BF)
        sums = dot(number, ph[...])
        sums = sums[:, : 2 * LANES] + sums[:, 2 * LANES :]
        source = lax.rem(z - k + n, n)
        out[pl.ds(source * tiles, tiles)] = sums.reshape(tiles, cells, 2 * LANES)


def tile_body(tabs, n, groups, cells, tiles, copies, at, owner, local, shift, *refs):
    n_kern = sum(len(group) for group in groups)
    payload, refs = refs[:n], refs[n:]
    arranged, refs = refs[:n_kern], refs[n_kern:]
    target, ph, gyy, gyy_t, gx, gx_t, w, w_t, out, held, near = refs
    rows, cell, grid, mid = tabs.rows, tabs.cell, tabs.grid, tabs.mid
    slots = local.shape[0] // tiles
    z, j = at[0], at[1]
    for k in range(n):
        held[pl.ds(k * cells, cells)] = (
            payload[k][0 : cells * rows].astype(F32).reshape(cells, rows, LANES)
        )
    spec = jnp.zeros((rows, LANES), F32)
    for s in range(slots):
        i = j * slots + s
        which = lax.rem(z - owner[i, 0] + n, n) * cells + local[i]
        one = held[which]
        turn = ph[pl.ds(shift[i], 1)]
        spec = spec + one * turn[:, :LANES] + swap(one) * turn[:, LANES:]
    left = lane_of((rows, LANES)) < HALF
    other = swap(spec)
    real = jnp.where(left, spec, other)
    imag = jnp.where(left, other, -spec)
    real = jnp.concatenate([real, real], axis=0)
    imag = jnp.concatenate([imag, imag], axis=0)
    wanted = target[j].astype(F32)
    sum_real = jnp.zeros((2 * rows, LANES), F32)
    sum_imag = jnp.zeros((2 * rows, LANES), F32)
    span = 2 * rows
    for group in groups:
        members = [(arranged[a], k) for a in group for k in range(arranged[a].shape[0])]
        pairs = [members[m : m + 2] for m in range(0, len(members), 2)]
        total = jnp.zeros((grid, 2 * cell), F32)
        for number, pair in enumerate(pairs):
            wide = []
            for ref, k in pair:
                kern = ref[k].astype(F32)
                wide.append(
                    jnp.concatenate([(kern * real).astype(BF), (kern * imag).astype(BF)], axis=1)
                )
            rowed = dot(jnp.concatenate(wide, axis=0), gyy[...])
            cols = [
                jnp.concatenate(
                    [rowed[p * span : (p + 1) * span, :cell], rowed[p * span : (p + 1) * span, cell:]],
                    axis=0,
                )
                for p in range(len(pair))
            ]
            fields = dot(gx[...], jnp.concatenate(cols, axis=1).astype(BF))
            near[number] = fields
            total = total + fields[:grid] * fields[:grid] + fields[grid:] * fields[grid:]
        image = exact(w[...], total[:, :cell] + total[:, cell:])
        resist = jax.nn.sigmoid(STEEP * (image - 1.0))
        pressure = 4.0 * STEEP * (resist - wanted) * resist * (1.0 - resist)
        push = exact(w_t[...], pressure)
        push = jnp.concatenate([push, push], axis=0)
        push = jnp.concatenate([push, push], axis=1)
        for number, pair in enumerate(pairs):
            back = dot(gx_t[...], (near[number] * push).astype(BF)).astype(BF)
            rowed = jnp.concatenate(
                [
                    jnp.concatenate(
                        [back[:span, p * cell : (p + 1) * cell], back[span:, p * cell : (p + 1) * cell]],
                        axis=1,
                    )
                    for p in range(len(pair))
                ],
                axis=0,
            )
            wide = dot(rowed, gyy_t[...])
            for p, (ref, k) in enumerate(pair):
                kern = ref[k].astype(F32)
                sum_real = sum_real + kern * wide[p * span : (p + 1) * span, :LANES]
                sum_imag = sum_imag + kern * wide[p * span : (p + 1) * span, LANES:]
    sum_real = sum_real[:rows] + sum_real[rows:]
    sum_imag = sum_imag[:rows] + sum_imag[rows:]
    grad = jnp.where(left, sum_real + swap(sum_real), swap(sum_imag - swap(sum_imag)))
    for copy in range(copies):
        out[copy] = grad


def gradients(tabs, slots, theta, grads, sums, gy, ex):
    tiles, cells = grads.shape[0], theta.shape[0]
    rows, cell = tabs.rows, tabs.cell
    pieces = []
    own = [grads[t] for t in range(tiles)]
    swapped = [swap(grad) for grad in own]
    for c in range(cells):
        total = jnp.zeros((rows, LANES), F32)
        for t in range(tiles):
            turn = sums[t, c : c + 1]
            total = total + own[t] * turn[:, :LANES] - swapped[t] * turn[:, LANES:]
        pieces.append(total * (2.0 / (slots * cell * cell)))
    rowed = exact(jnp.concatenate(pieces, axis=0), gy[...])
    result = []
    for c in range(cells):
        part = rowed[c * rows : (c + 1) * rows]
        part = jnp.concatenate([part[:, :cell], part[:, cell:]], axis=0)
        squash = jax.nn.sigmoid(theta[c])
        gradient = exact(ex[...], part) * squash * (1.0 - squash)
        power = jnp.sum(jnp.sum(gradient * gradient, axis=0, keepdims=True), axis=1, keepdims=True)
        result.append((gradient, LR * lax.rsqrt(power / (cell * cell) + EPS)))
    return result


def update_body(tabs, slots, theta, grads, sums, gy, ex, fy, fx, out, payload):
    moved = []
    for c, (gradient, rate) in enumerate(gradients(tabs, slots, theta, grads, sums, gy, ex)):
        value = theta[c] - rate * gradient
        out[c] = value
    spectra(tabs, slots, out[...], fy, fx, payload)


def last_body(tabs, slots, at, theta, grads, sums, gy, ex, out, held):
    band = out.shape[1]
    start = pl.multiple_of(at[2] * band, band)
    for c, (gradient, rate) in enumerate(gradients(tabs, slots, theta, grads, sums, gy, ex)):
        held[c] = rate * gradient
    out[...] = theta[:, pl.ds(start, band)] - held[:, pl.ds(start, band)]


VMEM = pl.BlockSpec(memory_space=pltpu.VMEM)
SMEM = pl.BlockSpec(memory_space=pltpu.SMEM)


def call(body, scalars, arrays, outs, scratch=(), name=None):
    many = isinstance(outs, list)
    return pl.pallas_call(
        body,
        out_shape=outs,
        in_specs=[SMEM] * len(scalars) + [VMEM] * len(arrays),
        out_specs=[VMEM] * len(outs) if many else VMEM,
        scratch_shapes=list(scratch),
        name=name,
    )(*scalars, *arrays)


def shape(dims, dtype):
    return jax.ShapeDtypeStruct(dims, dtype)


def shifted(array, axis, step):
    n = lax.axis_size(axis)
    return lax.ppermute(array, axis, [(i, (i + step) % n) for i in range(n)])


def per_device(theta, target, kernels, dose, inst_owner, inst_local, inst_shift):
    n = lax.axis_size("cells")
    n_kern = lax.axis_size("kern")
    n_corners = lax.axis_size("corners")
    cells, cell = theta.shape[0], theta.shape[1]
    tiles = target.shape[0]
    slots = inst_local.shape[0] // tiles
    assert tiles == n_kern
    tabs = Tables(cell, kernels.shape[3])
    rows = tabs.rows
    at = jnp.stack(
        [lax.axis_index("cells"), lax.axis_index("kern"), lax.axis_index(("corners", "kern"))]
    ).astype(jnp.int32)
    band = cell // (n_kern * n_corners)
    own = call(
        arrange_body,
        [dose],
        [kernels, tabs.pick, tabs.lane],
        shape((kernels.shape[2], 2 * rows, LANES), BF),
        name="arrange",
    )
    payload = call(
        functools.partial(first_body, tabs, slots),
        [inst_owner, inst_local, inst_shift],
        [theta, tabs.fy, tabs.fx],
        shape((cells * rows + INFO, LANES), BF),
        name="first",
    )
    both = n_corners == 2
    sets = [own]
    if both:
        sets.append(shifted(own, "corners", 1))
    arranged, groups = [], []
    for held in sets:
        groups.append([len(arranged) + k for k in range(n_kern)])
        arranged.append(held)
        arranged.extend(shifted(held, "kern", k) for k in range(1, n_kern))
    payloads = [payload] + [shifted(payload, "cells", k) for k in range(1, n)]
    sums = call(
        functools.partial(counts_body, tabs, n, tiles, cells, slots),
        [at],
        [tabs.ph_split] + payloads,
        shape((n * tiles, cells, 2 * LANES), F32),
        name="counts",
    )
    copies = n * n_kern
    for iteration in range(ITERS):
        grads = call(
            functools.partial(tile_body, tabs, n, groups, cells, tiles, copies),
            [at, inst_owner, inst_local, inst_shift],
            payloads
            + arranged
            + [target, tabs.ph, tabs.gyy, tabs.gyy_t, tabs.gx, tabs.gx_t, tabs.w, tabs.w_t],
            shape((copies, rows, LANES), F32),
            scratch=[
                pltpu.VMEM((n * cells, rows, LANES), F32),
                pltpu.VMEM(
                    ((n_kern * kernels.shape[2] + 1) // 2, 2 * tabs.grid, 2 * cell), F32
                ),
            ],
            name="tile",
        )
        if not both:
            grads = lax.psum(grads, "corners")
        grads = lax.all_to_all(grads, ("cells", "kern"), 0, 0, tiled=True)
        if iteration == ITERS - 1:
            return call(
                functools.partial(last_body, tabs, slots),
                [at],
                [theta, grads, sums, tabs.gy, tabs.ex],
                shape((cells, band, cell), F32),
                scratch=[pltpu.VMEM((cells, cell, cell), F32)],
                name="last",
            )
        theta, payload = call(
            functools.partial(update_body, tabs, slots),
            [],
            [theta, grads, sums, tabs.gy, tabs.ex, tabs.fy, tabs.fx],
            [shape(theta.shape, F32), shape((cells * rows, LANES), BF)],
            name="update",
        )
        payloads = [payload] + [shifted(payload, "cells", k) for k in range(1, n)]


def solution(mesh):
    in_specs = (
        P(("groups", "cells"), None, None),
        P(("groups", "cells"), None, None),
        P(None, "corners", "kern", None, None),
        P("corners"),
        P(("groups", "cells"), None),
        P(("groups", "cells")),
        P(("groups", "cells")),
    )
    out_specs = P(("groups", "cells"), ("corners", "kern"), None)
    return jax.shard_map(
        per_device, mesh=mesh, in_specs=in_specs, out_specs=out_specs, check_vma=False
    )
```

```python
import functools

import jax
import jax.numpy as jnp
import numpy as np
from jax import lax
from jax.experimental import pallas as pl
from jax.experimental.pallas import tpu as pltpu
from jax.sharding import PartitionSpec as P

ITERS = 2
LR = 0.25
EPS = 1e-06
STEEP = 3.0
LANES = 128
HALF = LANES // 2
INFO = 16
BF = jnp.bfloat16
F32 = jnp.float32


def up(value, step):
    return -(-value // step) * step


def split(array):
    high = np.asarray(array, np.float32).astype(BF)
    low = (np.asarray(array, np.float32) - high.astype(np.float32)).astype(BF)
    return high, low


class Tables:
    def __init__(self, cell, freq):
        self.cell, self.freq = cell, freq
        self.mid = freq // 2
        self.rows = up(self.mid + 1, 8)
        self.grid = min(cell, up(4 * self.mid + 1, 8))
        rows, grid, mid = self.rows, self.grid, self.mid
        turn = 2.0 * np.pi / cell
        f = np.arange(mid + 1)
        g = np.arange(freq) - mid
        pixels = np.arange(cell)
        fy = np.zeros((cell, LANES))
        phase = (pixels[:, None] * g[None, :] % cell) * turn
        fy[:, :freq] = np.cos(phase)
        fy[:, HALF : HALF + freq] = -np.sin(phase)
        self.fy = np.concatenate(split(fy), axis=1)
        fx = np.zeros((2 * rows, cell))
        phase = (f[:, None] * pixels[None, :] % cell) * turn
        fx[: mid + 1] = np.cos(phase)
        fx[rows : rows + mid + 1] = np.sin(phase)
        self.fx = np.concatenate(split(fx), axis=0)
        ex = np.concatenate([fx[:rows].T, -fx[rows:].T], axis=1)
        self.ex = ex.astype(np.float32)
        gy = np.zeros((LANES, 2 * cell))
        phase = (g[:, None] * pixels[None, :] % cell) * turn
        gy[:freq, :cell] = np.cos(phase)
        gy[:freq, cell:] = np.sin(phase)
        gy[HALF : HALF + freq, :cell] = -np.sin(phase)
        gy[HALF : HALF + freq, cell:] = np.cos(phase)
        self.gy = gy.astype(np.float32)
        both = np.concatenate([gy, np.roll(gy, HALF, axis=0)], axis=0)
        self.gyy = both.astype(np.float32).astype(BF)
        self.gyy_t = self.gyy.T.copy()
        gx = np.zeros((2 * grid, 4 * rows))
        phase = (f[None, :] * np.arange(grid)[:, None] % grid) * (2.0 * np.pi / grid)
        cos, sin = np.zeros((grid, rows)), np.zeros((grid, rows))
        cos[:, : mid + 1], sin[:, : mid + 1] = np.cos(phase), np.sin(phase)
        gx[:grid] = np.concatenate([cos, cos, -sin, -sin], axis=1)
        gx[grid:] = np.concatenate([sin, -sin, cos, -cos], axis=1)
        self.gx = gx.astype(np.float32).astype(BF)
        self.gx_t = self.gx.T.copy()
        u = np.arange(-2 * mid, 2 * mid + 1)
        if grid == cell:
            weights = np.eye(cell)
        else:
            diff = pixels[:, None] / cell - np.arange(grid)[None, :] / grid
            weights = np.cos(2.0 * np.pi * diff[:, :, None] * u).sum(-1) / grid
        self.w = weights.astype(np.float32)
        self.w_t = self.w.T.copy()
        ph = np.zeros((cell, 2 * LANES))
        phase = (pixels[:, None] * g[None, :] % cell) * turn
        ph[:, :freq] = ph[:, HALF : HALF + freq] = np.cos(phase)
        ph[:, LANES : LANES + freq] = np.sin(phase)
        ph[:, LANES + HALF : LANES + HALF + freq] = -np.sin(phase)
        self.ph = ph.astype(np.float32)
        self.ph_split = np.concatenate(split(ph), axis=1)
        pick_u, pick_v = np.zeros((rows, freq)), np.zeros((rows, freq))
        for row in range(mid + 1):
            pick_u[row, mid + row] = 1.0
            if row > 0:
                pick_v[row, mid - row] = 1.0
        self.pick = np.stack([pick_u, pick_v]).astype(np.float32).astype(BF)
        lane = np.zeros((4, freq, LANES))
        for col in range(freq):
            lane[0, col, col] = 1.0
            lane[1, col, HALF + col] = 1.0
            lane[2, col, freq - 1 - col] = 1.0
            lane[3, col, HALF + freq - 1 - col] = -1.0
        self.lane = lane.astype(np.float32).astype(BF)


def dot(a, b, **kw):
    return jnp.dot(a, b, preferred_element_type=F32, **kw)


def exact(a, b):
    return dot(a, b, precision=lax.Precision.HIGHEST)


def swap(x):
    return pltpu.roll(x, HALF, 1)


def lane_of(shape):
    return lax.broadcasted_iota(jnp.int32, shape, len(shape) - 1)


def arrange_body(dose, kern, pick, lane, out):
    root = jnp.sqrt(jnp.full((1, 1), dose[0], F32))
    for k in range(out.shape[0]):
        real = (kern[0, 0, k] * root).astype(BF)
        imag = (kern[1, 0, k] * root).astype(BF)
        upper = (dot(real, lane[0]) + dot(imag, lane[1])).astype(BF)
        lower = (dot(real, lane[2]) + dot(imag, lane[3])).astype(BF)
        both = jnp.concatenate([dot(pick[0], upper), dot(pick[1], lower)], axis=0)
        out[k] = both.astype(BF)


def spectra(tabs, slots, theta, fy, fx, out):
    cells, cell, rows = theta.shape[0], tabs.cell, tabs.rows
    mask = jax.nn.sigmoid(theta).astype(BF).reshape(cells * cell, cell)
    along = dot(mask, fy[...])
    along = along[:, :LANES] + along[:, LANES:]
    sign = jnp.where(lane_of((rows, LANES)) < HALF, 1.0, -1.0)
    row_at = lax.broadcasted_iota(jnp.int32, (rows, LANES), 0)
    centre = jnp.where((row_at == 0) & (lane_of((rows, LANES)) == tabs.mid), 1.0 / slots, 0.0)
    scale = 2.0 / (slots * cell * cell)
    for c in range(cells):
        part = along[c * cell : (c + 1) * cell]
        high = part.astype(BF)
        low = (part - high.astype(F32)).astype(BF)
        res = dot(fx[...], jnp.concatenate([high, low], axis=1))
        res = res[: 2 * rows, :LANES] + res[: 2 * rows, LANES:] + res[2 * rows :, :LANES]
        spec = res[:rows] + swap(res[rows:]) * sign
        out[c * rows : (c + 1) * rows] = (spec * scale - centre).astype(BF)


def first_body(tabs, slots, owner, local, shift, theta, fy, fx, out):
    spectra(tabs, slots, theta[...], fy, fx, out)
    base = theta.shape[0] * tabs.rows
    row = lax.broadcasted_iota(jnp.int32, (INFO, LANES), 0)
    col = lane_of((INFO, LANES))
    info = jnp.zeros((INFO, LANES), jnp.int32)
    for i in range(local.shape[0]):
        value = jnp.where(row == 0, owner[i], jnp.where(row == 1, local[i], shift[i]))
        info = jnp.where((col == i) & (row < 3), value, info)
    out[base : base + INFO] = info.astype(F32).astype(BF)


def counts_body(tabs, n, tiles, cells, slots, at, ph, *refs):
    out = refs[-1]
    z = at[0]
    base = cells * tabs.rows
    row = lax.broadcasted_iota(jnp.int32, (tiles * cells, LANES), 0)
    col = lane_of((tiles * cells, LANES))
    shift_at = lax.broadcasted_iota(jnp.int32, (tabs.cell, LANES), 0)
    for k in range(n):
        info = refs[k][base : base + INFO].astype(F32).astype(jnp.int32)
        owner, local, shift = info[0:1], info[1:2], info[2:3]
        mine = (owner == z) & (local == row % cells) & (col // slots == row // cells)
        mine = mine & (col < tiles * slots)
        chosen = jnp.where(mine, 1.0, 0.0).astype(BF)
        hot = jnp.where(shift == shift_at, 1.0, 0.0).astype(BF)
        number = lax.dot_general(
            chosen, hot, (((1,), (1,)), ((), ())), preferred_element_type=F32
        ).astype(BF)
        sums = dot(number, ph[...])
        sums = sums[:, : 2 * LANES] + sums[:, 2 * LANES :]
        source = lax.rem(z - k + n, n)
        out[pl.ds(source * tiles, tiles)] = sums.reshape(tiles, cells, 2 * LANES)


def tile_body(tabs, n, cells, tiles, copies, at, owner, local, shift, *refs):
    payload, refs = refs[:n], refs[n:]
    arranged, refs = refs[:tiles], refs[tiles:]
    target, ph, gyy, gyy_t, gx, gx_t, w, w_t, out, held, near = refs
    rows, cell, grid, mid = tabs.rows, tabs.cell, tabs.grid, tabs.mid
    slots = local.shape[0] // tiles
    z, j = at[0], at[1]
    for k in range(n):
        held[pl.ds(k * cells, cells)] = (
            payload[k][0 : cells * rows].astype(F32).reshape(cells, rows, LANES)
        )
    spec = jnp.zeros((rows, LANES), F32)
    for s in range(slots):
        i = j * slots + s
        which = lax.rem(z - owner[i] + n, n) * cells + local[i]
        one = held[which]
        turn = ph[pl.ds(shift[i], 1)]
        spec = spec + one * turn[:, :LANES] + swap(one) * turn[:, LANES:]
    left = lane_of((rows, LANES)) < HALF
    other = swap(spec)
    real = jnp.where(left, spec, other)
    imag = jnp.where(left, other, -spec)
    real = jnp.concatenate([real, real], axis=0)
    imag = jnp.concatenate([imag, imag], axis=0)
    wanted = target[j].astype(F32)
    sum_real = jnp.zeros((2 * rows, LANES), F32)
    sum_imag = jnp.zeros((2 * rows, LANES), F32)
    span = 2 * rows
    members = [(ref, k) for ref in arranged for k in range(ref.shape[0])]
    pairs = [members[m : m + 2] for m in range(0, len(members), 2)]
    total = jnp.zeros((grid, 2 * cell), F32)
    for number, pair in enumerate(pairs):
        wide = []
        for ref, k in pair:
            kern = ref[k].astype(F32)
            wide.append(
                jnp.concatenate([(kern * real).astype(BF), (kern * imag).astype(BF)], axis=1)
            )
        rowed = dot(jnp.concatenate(wide, axis=0), gyy[...])
        cols = [
            jnp.concatenate(
                [rowed[p * span : (p + 1) * span, :cell], rowed[p * span : (p + 1) * span, cell:]],
                axis=0,
            )
            for p in range(len(pair))
        ]
        fields = dot(gx[...], jnp.concatenate(cols, axis=1).astype(BF))
        near[number] = fields
        total = total + fields[:grid] * fields[:grid] + fields[grid:] * fields[grid:]
    image = exact(w[...], total[:, :cell] + total[:, cell:])
    resist = jax.nn.sigmoid(STEEP * (image - 1.0))
    pressure = 4.0 * STEEP * (resist - wanted) * resist * (1.0 - resist)
    push = exact(w_t[...], pressure)
    push = jnp.concatenate([push, push], axis=0)
    push = jnp.concatenate([push, push], axis=1)
    for number, pair in enumerate(pairs):
        back = dot(gx_t[...], (near[number] * push).astype(BF)).astype(BF)
        rowed = jnp.concatenate(
            [
                jnp.concatenate(
                    [back[:span, p * cell : (p + 1) * cell], back[span:, p * cell : (p + 1) * cell]],
                    axis=1,
                )
                for p in range(len(pair))
            ],
            axis=0,
        )
        wide = dot(rowed, gyy_t[...])
        for p, (ref, k) in enumerate(pair):
            kern = ref[k].astype(F32)
            sum_real = sum_real + kern * wide[p * span : (p + 1) * span, :LANES]
            sum_imag = sum_imag + kern * wide[p * span : (p + 1) * span, LANES:]
    sum_real = sum_real[:rows] + sum_real[rows:]
    sum_imag = sum_imag[:rows] + sum_imag[rows:]
    grad = jnp.where(left, sum_real + swap(sum_real), swap(sum_imag - swap(sum_imag)))
    for copy in range(copies):
        out[copy] = grad.astype(BF)


def gradients(tabs, slots, corners, kern, theta, grads, sums, gy, ex):
    tiles, cells = sums.shape[0], theta.shape[0]
    rows, cell = tabs.rows, tabs.cell
    pieces = []
    own = []
    for t in range(tiles):
        z, j = t // kern, t % kern
        parts = [grads[(z * corners + x) * kern + j].astype(F32) for x in range(corners)]
        own.append(sum(parts[1:], parts[0]))
    swapped = [swap(grad) for grad in own]
    for c in range(cells):
        total = jnp.zeros((rows, LANES), F32)
        for t in range(tiles):
            turn = sums[t, c : c + 1]
            total = total + own[t] * turn[:, :LANES] - swapped[t] * turn[:, LANES:]
        pieces.append(total * (2.0 / (slots * cell * cell)))
    rowed = exact(jnp.concatenate(pieces, axis=0), gy[...])
    result = []
    for c in range(cells):
        part = rowed[c * rows : (c + 1) * rows]
        part = jnp.concatenate([part[:, :cell], part[:, cell:]], axis=0)
        squash = jax.nn.sigmoid(theta[c])
        gradient = exact(ex[...], part) * squash * (1.0 - squash)
        power = jnp.sum(jnp.sum(gradient * gradient, axis=0, keepdims=True), axis=1, keepdims=True)
        result.append((gradient, LR * lax.rsqrt(power / (cell * cell) + EPS)))
    return result


def update_body(tabs, slots, corners, kern, theta, grads, sums, gy, ex, fy, fx, out, payload):
    for c, (gradient, rate) in enumerate(
        gradients(tabs, slots, corners, kern, theta, grads, sums, gy, ex)
    ):
        value = theta[c] - rate * gradient
        out[c] = value
    spectra(tabs, slots, out[...], fy, fx, payload)


def last_body(tabs, slots, corners, kern, at, theta, grads, sums, gy, ex, out, held):
    band = out.shape[1]
    start = pl.multiple_of(at[2] * band, band)
    for c, (gradient, rate) in enumerate(
        gradients(tabs, slots, corners, kern, theta, grads, sums, gy, ex)
    ):
        held[c] = rate * gradient
    out[...] = theta[:, pl.ds(start, band)] - held[:, pl.ds(start, band)]


VMEM = pl.BlockSpec(memory_space=pltpu.VMEM)
SMEM = pl.BlockSpec(memory_space=pltpu.SMEM)


def call(body, scalars, arrays, outs, scratch=(), name=None):
    many = isinstance(outs, list)
    arrays = [pltpu.with_memory_space_constraint(array, pltpu.VMEM) for array in arrays]
    return pl.pallas_call(
        body,
        out_shape=outs,
        in_specs=[SMEM] * len(scalars) + [VMEM] * len(arrays),
        out_specs=[VMEM] * len(outs) if many else VMEM,
        scratch_shapes=list(scratch),
        name=name,
    )(*scalars, *arrays)


def shape(dims, dtype):
    return pltpu.VMEM(dims, dtype)


def shifted(array, axis, step):
    n = lax.axis_size(axis)
    return lax.ppermute(array, axis, [(i, (i + step) % n) for i in range(n)])


def per_device(theta, target, kernels, dose, inst_owner, inst_local, inst_shift):
    n = lax.axis_size("cells")
    n_kern = lax.axis_size("kern")
    n_corners = lax.axis_size("corners")
    cells, cell = theta.shape[0], theta.shape[1]
    tiles = target.shape[0]
    slots = inst_local.shape[0] // tiles
    assert tiles == n_kern
    tabs = Tables(cell, kernels.shape[3])
    inst_owner = inst_owner[:, 0]
    rows = tabs.rows
    at = jnp.stack(
        [lax.axis_index("cells"), lax.axis_index("kern"), lax.axis_index(("corners", "kern"))]
    ).astype(jnp.int32)
    band = cell // (n_kern * n_corners)
    payload = call(
        functools.partial(first_body, tabs, slots),
        [inst_owner, inst_local, inst_shift],
        [theta, tabs.fy, tabs.fx],
        shape((cells * rows + INFO, LANES), BF),
        name="first",
    )
    payload, kernels = lax.optimization_barrier((payload, kernels))
    payloads = [payload] + [shifted(payload, "cells", k) for k in range(1, n)]
    own = call(
        arrange_body,
        [dose],
        [kernels, tabs.pick, tabs.lane],
        shape((kernels.shape[2], 2 * rows, LANES), BF),
        name="arrange",
    )
    arranged = [own] + [shifted(own, "kern", k) for k in range(1, n_kern)]
    sums = call(
        functools.partial(counts_body, tabs, n, tiles, cells, slots),
        [at],
        [tabs.ph_split] + payloads,
        shape((n * tiles, cells, 2 * LANES), F32),
        name="counts",
    )
    copies = n * n_corners * n_kern
    for iteration in range(ITERS):
        grads = call(
            functools.partial(tile_body, tabs, n, cells, tiles, copies),
            [at, inst_owner, inst_local, inst_shift],
            payloads
            + arranged
            + [target, tabs.ph, tabs.gyy, tabs.gyy_t, tabs.gx, tabs.gx_t, tabs.w, tabs.w_t],
            shape((copies, rows, LANES), BF),
            scratch=[
                pltpu.VMEM((n * cells, rows, LANES), F32),
                pltpu.VMEM(
                    ((n_kern * kernels.shape[2] + 1) // 2, 2 * tabs.grid, 2 * cell), F32
                ),
            ],
            name="tile",
        )
        grads = lax.all_to_all(grads, ("cells", "corners", "kern"), 0, 0, tiled=True)
        if iteration == ITERS - 1:
            return call(
                functools.partial(last_body, tabs, slots, n_corners, n_kern),
                [at],
                [theta, grads, sums, tabs.gy, tabs.ex],
                shape((cells, band, cell), F32),
                scratch=[pltpu.VMEM((cells, cell, cell), F32)],
                name="last",
            )
        theta, payload = call(
            functools.partial(update_body, tabs, slots, n_corners, n_kern),
            [],
            [theta, grads, sums, tabs.gy, tabs.ex, tabs.fy, tabs.fx],
            [shape(theta.shape, F32), shape((cells * rows, LANES), BF)],
            name="update",
        )
        payloads = [payload] + [shifted(payload, "cells", k) for k in range(1, n)]


def solution(mesh):
    in_specs = (
        P(("groups", "cells"), None, None),
        P(("groups", "cells"), None, None),
        P(None, "corners", "kern", None, None),
        P("corners"),
        P(("groups", "cells"), None),
        P(("groups", "cells")),
        P(("groups", "cells")),
    )
    out_specs = P(("groups", "cells"), ("corners", "kern"), None)
    return jax.shard_map(
        per_device, mesh=mesh, in_specs=in_specs, out_specs=out_specs, check_vma=False
    )
```

```python
import functools

import jax
import jax.numpy as jnp
import numpy as np
from jax import lax
from jax.experimental import pallas as pl
from jax.experimental.pallas import tpu as pltpu
from jax.sharding import PartitionSpec as P


ITERS = 2
LR = 0.25
EPS = 1e-06
STEEP = 3.0
LANES = 128
HALF = LANES // 2
INFO = 16
BF = jnp.bfloat16
F32 = jnp.float32


def up(value, step):
    return -(-value // step) * step


def split(array):
    high = np.asarray(array, np.float32).astype(BF)
    low = (np.asarray(array, np.float32) - high.astype(np.float32)).astype(BF)
    return high, low


class Tables:
    def __init__(self, cell, freq):
        self.cell, self.freq = cell, freq
        self.mid = freq // 2
        self.rows = up(self.mid + 1, 8)
        self.grid = min(cell, up(4 * self.mid + 1, 8))
        rows, grid, mid = self.rows, self.grid, self.mid
        turn = 2.0 * np.pi / cell
        f = np.arange(mid + 1)
        g = np.arange(freq) - mid
        pixels = np.arange(cell)
        fy = np.zeros((cell, LANES))
        phase = (pixels[:, None] * g[None, :] % cell) * turn
        fy[:, :freq] = np.cos(phase)
        fy[:, HALF : HALF + freq] = -np.sin(phase)
        self.fy = np.concatenate(split(fy), axis=1)
        fx = np.zeros((2 * rows, cell))
        phase = (f[:, None] * pixels[None, :] % cell) * turn
        fx[: mid + 1] = np.cos(phase)
        fx[rows : rows + mid + 1] = np.sin(phase)
        self.fx = np.concatenate(split(fx), axis=0)
        ex = np.concatenate([fx[:rows].T, -fx[rows:].T], axis=1)
        self.ex = ex.astype(np.float32)
        gy = np.zeros((LANES, 2 * cell))
        phase = (g[:, None] * pixels[None, :] % cell) * turn
        gy[:freq, :cell] = np.cos(phase)
        gy[:freq, cell:] = np.sin(phase)
        gy[HALF : HALF + freq, :cell] = -np.sin(phase)
        gy[HALF : HALF + freq, cell:] = np.cos(phase)
        self.gy = gy.astype(np.float32)
        both = np.concatenate([gy, np.roll(gy, HALF, axis=0)], axis=0)
        self.gyy = both.astype(np.float32).astype(BF)
        self.gyy_t = self.gyy.T.copy()
        gx = np.zeros((2 * grid, 4 * rows))
        phase = (f[None, :] * np.arange(grid)[:, None] % grid) * (2.0 * np.pi / grid)
        cos, sin = np.zeros((grid, rows)), np.zeros((grid, rows))
        cos[:, : mid + 1], sin[:, : mid + 1] = np.cos(phase), np.sin(phase)
        gx[:grid] = np.concatenate([cos, cos, -sin, -sin], axis=1)
        gx[grid:] = np.concatenate([sin, -sin, cos, -cos], axis=1)
        self.gx = gx.astype(np.float32).astype(BF)
        self.gx_t = self.gx.T.copy()
        u = np.arange(-2 * mid, 2 * mid + 1)
        if grid == cell:
            weights = np.eye(cell)
        else:
            diff = pixels[:, None] / cell - np.arange(grid)[None, :] / grid
            weights = np.cos(2.0 * np.pi * diff[:, :, None] * u).sum(-1) / grid
        self.w = weights.astype(np.float32)
        self.w_t = self.w.T.copy()
        ph = np.zeros((cell, 2 * LANES))
        phase = (pixels[:, None] * g[None, :] % cell) * turn
        ph[:, :freq] = ph[:, HALF : HALF + freq] = np.cos(phase)
        ph[:, LANES : LANES + freq] = np.sin(phase)
        ph[:, LANES + HALF : LANES + HALF + freq] = -np.sin(phase)
        self.ph = ph.astype(np.float32)
        self.ph_split = np.concatenate(split(ph), axis=1)
        pick_u, pick_v = np.zeros((rows, freq)), np.zeros((rows, freq))
        for row in range(mid + 1):
            pick_u[row, mid + row] = 1.0
            if row > 0:
                pick_v[row, mid - row] = 1.0
        self.pick = np.stack([pick_u, pick_v]).astype(np.float32).astype(BF)
        lane = np.zeros((4, freq, LANES))
        for col in range(freq):
            lane[0, col, col] = 1.0
            lane[1, col, HALF + col] = 1.0
            lane[2, col, freq - 1 - col] = 1.0
            lane[3, col, HALF + freq - 1 - col] = -1.0
        self.lane = lane.astype(np.float32).astype(BF)


def packing(tabs):
    sent = tabs.rows - 8
    free = HALF - tabs.freq
    extra = tabs.mid + 1 - sent
    pieces = -(-tabs.freq // free) if free > 0 else 0
    if sent % 16 or free < 8 or extra < 1 or extra * pieces > 8:
        return up(tabs.rows, 16), []
    steps = []
    for p in range(pieces):
        begin = p * free
        steps.append((begin, min(free, tabs.freq - begin), p * extra, extra))
    return sent, steps


def inside(first, count, value):
    return (value >= first) & (value < first + count)


def pack(tabs, spec):
    sent, steps = packing(tabs)
    if not steps:
        return jnp.concatenate([spec, jnp.zeros((sent - tabs.rows, LANES), F32)], axis=0).astype(BF)
    row = lax.broadcasted_iota(jnp.int32, (8, LANES), 0)
    col = lane_of((8, LANES)) % HALF
    top, rest = spec[:8], spec[sent:]
    for begin, width, where, extra in steps:
        moved = pltpu.roll(rest, tabs.freq - begin, 1)
        if where:
            moved = pltpu.roll(moved, where, 0)
        here = inside(where, extra, row) & inside(tabs.freq, width, col)
        top = jnp.where(here, moved, top)
    return jnp.concatenate([top, spec[8:sent]], axis=0).astype(BF)


def unpack(tabs, sent_spec):
    _, steps = packing(tabs)
    if not steps:
        return sent_spec[: tabs.rows].astype(F32)
    spec = sent_spec.astype(F32)
    row = lax.broadcasted_iota(jnp.int32, (8, LANES), 0)
    col = lane_of((8, LANES)) % HALF
    rest = jnp.zeros((8, LANES), F32)
    for begin, width, where, extra in steps:
        moved = pltpu.roll(spec[:8], LANES - (tabs.freq - begin), 1)
        if where:
            moved = pltpu.roll(moved, 8 - where, 0)
        here = inside(0, extra, row) & inside(begin, width, col)
        rest = jnp.where(here, moved, rest)
    return jnp.concatenate([spec, rest], axis=0)


def dot(a, b, **kw):
    return jnp.dot(a, b, preferred_element_type=F32, **kw)


def exact(a, b):
    return dot(a, b, precision=lax.Precision.HIGHEST)


def swap(x):
    return pltpu.roll(x, HALF, 1)


def lane_of(shape):
    return lax.broadcasted_iota(jnp.int32, shape, len(shape) - 1)


def arrange_body(dose, kern, pick, lane, out):
    root = jnp.sqrt(jnp.full((1, 1), dose[0], F32))
    for k in range(out.shape[0]):
        real = (kern[0, 0, k] * root).astype(BF)
        imag = (kern[1, 0, k] * root).astype(BF)
        upper = (dot(real, lane[0]) + dot(imag, lane[1])).astype(BF)
        lower = (dot(real, lane[2]) + dot(imag, lane[3])).astype(BF)
        both = jnp.concatenate([dot(pick[0], upper), dot(pick[1], lower)], axis=0)
        out[k] = both.astype(BF)


def spectra(tabs, slots, theta, fy, fx, out):
    cells, cell, rows = theta.shape[0], tabs.cell, tabs.rows
    mask = jax.nn.sigmoid(theta).astype(BF).reshape(cells * cell, cell)
    along = dot(mask, fy[...])
    along = along[:, :LANES] + along[:, LANES:]
    sign = jnp.where(lane_of((rows, LANES)) < HALF, 1.0, -1.0)
    row_at = lax.broadcasted_iota(jnp.int32, (rows, LANES), 0)
    centre = jnp.where((row_at == 0) & (lane_of((rows, LANES)) == tabs.mid), 1.0 / slots, 0.0)
    scale = 2.0 / (slots * cell * cell)
    for c in range(cells):
        part = along[c * cell : (c + 1) * cell]
        high = part.astype(BF)
        low = (part - high.astype(F32)).astype(BF)
        res = dot(fx[...], jnp.concatenate([high, low], axis=1))
        res = res[: 2 * rows, :LANES] + res[: 2 * rows, LANES:] + res[2 * rows :, :LANES]
        spec = res[:rows] + swap(res[rows:]) * sign
        sent = packing(tabs)[0]
        out[c * sent : (c + 1) * sent] = pack(tabs, spec * scale - centre)


def first_body(tabs, slots, owner, local, shift, theta, fy, fx, out):
    spectra(tabs, slots, theta[...], fy, fx, out)
    base = theta.shape[0] * packing(tabs)[0]
    row = lax.broadcasted_iota(jnp.int32, (INFO, LANES), 0)
    col = lane_of((INFO, LANES))
    info = jnp.zeros((INFO, LANES), jnp.int32)
    for i in range(local.shape[0]):
        value = jnp.where(row == 0, owner[i], jnp.where(row == 1, local[i], shift[i]))
        info = jnp.where((col == i) & (row < 3), value, info)
    out[base : base + INFO] = info.astype(F32).astype(BF)


def counts(tabs, n, tiles, cells, slots, at, ph, payload, out):
    z = at[0]
    base = cells * packing(tabs)[0]
    row = lax.broadcasted_iota(jnp.int32, (tiles * cells, LANES), 0)
    col = lane_of((tiles * cells, LANES))
    shift_at = lax.broadcasted_iota(jnp.int32, (tabs.cell, LANES), 0)
    for k in range(n):
        info = payload[k][base : base + INFO].astype(F32).astype(jnp.int32)
        owner, local, shift = info[0:1], info[1:2], info[2:3]
        mine = (owner == z) & (local == row % cells) & (col // slots == row // cells)
        mine = mine & (col < tiles * slots)
        chosen = jnp.where(mine, 1.0, 0.0).astype(BF)
        hot = jnp.where(shift == shift_at, 1.0, 0.0).astype(BF)
        number = lax.dot_general(
            chosen, hot, (((1,), (1,)), ((), ())), preferred_element_type=F32
        ).astype(BF)
        sums = dot(number, ph[...])
        sums = sums[:, : 2 * LANES] + sums[:, 2 * LANES :]
        source = lax.rem(z - k + n, n)
        out[pl.ds(source * tiles, tiles)] = sums.reshape(tiles, cells, 2 * LANES)


def tile_body(tabs, n, cells, tiles, copies, at, owner, local, shift, *refs):
    payload, refs = refs[:n], refs[n:]
    arranged, refs = refs[:tiles], refs[tiles:]
    target, ph, gyy, gyy_t, gx, gx_t, w, w_t, out, held, near = refs
    rows, cell, grid = tabs.rows, tabs.cell, tabs.grid
    slots = local.shape[0] // tiles
    z, j = at[0], at[1]
    for k in range(n):
        sent = packing(tabs)[0]
        held[pl.ds(k * cells, cells)] = payload[k][0 : cells * sent].reshape(cells, sent, LANES)
    spec = jnp.zeros((rows, LANES), F32)
    for s in range(slots):
        i = j * slots + s
        which = lax.rem(z - owner[i] + n, n) * cells + local[i]
        one = unpack(tabs, held[which])
        turn = ph[pl.ds(shift[i], 1)]
        spec = spec + one * turn[:, :LANES] + swap(one) * turn[:, LANES:]
    left = lane_of((rows, LANES)) < HALF
    other = swap(spec)
    real = jnp.where(left, spec, other)
    imag = jnp.where(left, other, -spec)
    real = jnp.concatenate([real, real], axis=0)
    imag = jnp.concatenate([imag, imag], axis=0)
    wanted = target[j].astype(F32)
    sum_real = jnp.zeros((2 * rows, LANES), F32)
    sum_imag = jnp.zeros((2 * rows, LANES), F32)
    span = 2 * rows
    members = [(ref, k) for ref in arranged for k in range(ref.shape[0])]
    pairs = [members[m : m + 2] for m in range(0, len(members), 2)]
    total = jnp.zeros((grid, 2 * cell), F32)
    for number, pair in enumerate(pairs):
        wide = []
        for ref, k in pair:
            kern = ref[k].astype(F32)
            wide.append(
                jnp.concatenate([(kern * real).astype(BF), (kern * imag).astype(BF)], axis=1)
            )
        rowed = dot(jnp.concatenate(wide, axis=0), gyy[...])
        cols = [
            jnp.concatenate(
                [rowed[p * span : (p + 1) * span, :cell], rowed[p * span : (p + 1) * span, cell:]],
                axis=0,
            )
            for p in range(len(pair))
        ]
        fields = dot(gx[...], jnp.concatenate(cols, axis=1).astype(BF))
        near[number] = fields
        total = total + fields[:grid] * fields[:grid] + fields[grid:] * fields[grid:]
    image = exact(w[...], total[:, :cell] + total[:, cell:])
    resist = jax.nn.sigmoid(STEEP * (image - 1.0))
    pressure = 4.0 * STEEP * (resist - wanted) * resist * (1.0 - resist)
    push = exact(w_t[...], pressure)
    push = jnp.concatenate([push, push], axis=0)
    push = jnp.concatenate([push, push], axis=1)
    for number, pair in enumerate(pairs):
        back = dot(gx_t[...], (near[number] * push).astype(BF)).astype(BF)
        rowed = jnp.concatenate(
            [
                jnp.concatenate(
                    [back[:span, p * cell : (p + 1) * cell], back[span:, p * cell : (p + 1) * cell]],
                    axis=1,
                )
                for p in range(len(pair))
            ],
            axis=0,
        )
        wide = dot(rowed, gyy_t[...])
        for p, (ref, k) in enumerate(pair):
            kern = ref[k].astype(F32)
            sum_real = sum_real + kern * wide[p * span : (p + 1) * span, :LANES]
            sum_imag = sum_imag + kern * wide[p * span : (p + 1) * span, LANES:]
    sum_real = sum_real[:rows] + sum_real[rows:]
    sum_imag = sum_imag[:rows] + sum_imag[rows:]
    grad = jnp.where(left, sum_real + swap(sum_real), swap(sum_imag - swap(sum_imag)))
    grad = pack(tabs, grad)
    for copy in range(copies):
        out[copy] = grad


def gradients(tabs, slots, corners, kern, theta, grads, sums, gy, ex):
    tiles, cells = sums.shape[0], theta.shape[0]
    rows, cell = tabs.rows, tabs.cell
    pieces = []
    own = []
    for t in range(tiles):
        z, j = t // kern, t % kern
        parts = [unpack(tabs, grads[(z * corners + x) * kern + j]) for x in range(corners)]
        own.append(sum(parts[1:], parts[0]))
    swapped = [swap(grad) for grad in own]
    for c in range(cells):
        total = jnp.zeros((rows, LANES), F32)
        for t in range(tiles):
            turn = sums[t, c : c + 1]
            total = total + own[t] * turn[:, :LANES] - swapped[t] * turn[:, LANES:]
        pieces.append(total * (2.0 / (slots * cell * cell)))
    rowed = exact(jnp.concatenate(pieces, axis=0), gy[...])
    result = []
    for c in range(cells):
        part = rowed[c * rows : (c + 1) * rows]
        part = jnp.concatenate([part[:, :cell], part[:, cell:]], axis=0)
        squash = jax.nn.sigmoid(theta[c])
        gradient = exact(ex[...], part) * squash * (1.0 - squash)
        power = jnp.sum(jnp.sum(gradient * gradient, axis=0, keepdims=True), axis=1, keepdims=True)
        result.append((gradient, LR * lax.rsqrt(power / (cell * cell) + EPS)))
    return result


def update_body(tabs, slots, corners, kern, n, at, theta, grads, ph, gy, ex, fy, fx, *refs):
    heard, (out, sums, payload) = refs[:n], refs[n:]
    counts(tabs, n, kern, theta.shape[0], slots, at, ph, heard, sums)
    for c, (gradient, rate) in enumerate(
        gradients(tabs, slots, corners, kern, theta, grads, sums, gy, ex)
    ):
        out[c] = theta[c] - rate * gradient
    spectra(tabs, slots, out[...], fy, fx, payload)


def last_body(tabs, slots, corners, kern, at, theta, grads, sums, gy, ex, out, held, ready, sem):
    band = out.shape[1]
    start = pl.multiple_of(at[2] * band, band)
    copies = []
    for c, (gradient, rate) in enumerate(
        gradients(tabs, slots, corners, kern, theta, grads, sums, gy, ex)
    ):
        held[c] = rate * gradient
        ready[c] = theta[c, pl.ds(start, band)] - held[c, pl.ds(start, band)]
        copies.append(pltpu.make_async_copy(ready.at[c], out.at[c], sem.at[c]))
        copies[-1].start()
    for copy in copies:
        copy.wait()


VMEM = pl.BlockSpec(memory_space=pltpu.VMEM)
SMEM = pl.BlockSpec(memory_space=pltpu.SMEM)


def call(body, scalars, arrays, outs, scratch=(), far=(), out_far=False):
    many = isinstance(outs, list)
    arrays = [
        array if place in far else pltpu.with_memory_space_constraint(array, pltpu.VMEM)
        for place, array in enumerate(arrays)
    ]
    out_spec = pl.BlockSpec(memory_space=pl.ANY) if out_far else VMEM
    return pl.pallas_call(
        body,
        out_shape=outs,
        in_specs=[SMEM] * len(scalars) + [VMEM] * len(arrays),
        out_specs=[VMEM] * len(outs) if many else out_spec,
        scratch_shapes=list(scratch),
    )(*scalars, *arrays)


def shape(dims, dtype):
    return pltpu.VMEM(dims, dtype)


def shifted(array, axis, step):
    n = lax.axis_size(axis)
    return lax.ppermute(array, axis, [(i, (i + step) % n) for i in range(n)])


def per_device(theta, target, kernels, dose, inst_owner, inst_local, inst_shift):
    n = lax.axis_size("cells")
    n_kern = lax.axis_size("kern")
    n_corners = lax.axis_size("corners")
    cells, cell = theta.shape[0], theta.shape[1]
    tiles = target.shape[0]
    slots = inst_local.shape[0] // tiles
    assert tiles == n_kern
    tabs = Tables(cell, kernels.shape[3])
    inst_owner = inst_owner[:, 0]
    rows, sent = tabs.rows, packing(tabs)[0]
    at = jnp.stack(
        [lax.axis_index("cells"), lax.axis_index("kern"), lax.axis_index(("corners", "kern"))]
    ).astype(jnp.int32)
    band = cell // (n_kern * n_corners)
    payload = call(
        functools.partial(first_body, tabs, slots),
        [inst_owner, inst_local, inst_shift],
        [theta, tabs.fy, tabs.fx],
        shape((cells * sent + INFO, LANES), BF),
        far=(0, 1, 2),
    )
    payloads = [payload]
    for k in range(1, n):
        payloads.append(shifted(payload, "cells", k))
    own = call(
        arrange_body,
        [dose],
        [kernels, tabs.pick, tabs.lane],
        shape((kernels.shape[2], 2 * rows, LANES), BF),
    )
    arranged = [own] + [shifted(own, "kern", k) for k in range(1, n_kern)]
    copies = n * n_corners * n_kern
    for iteration in range(ITERS):
        grads = call(
            functools.partial(tile_body, tabs, n, cells, tiles, copies),
            [at, inst_owner, inst_local, inst_shift],
            payloads
            + arranged
            + [target, tabs.ph, tabs.gyy, tabs.gyy_t, tabs.gx, tabs.gx_t, tabs.w, tabs.w_t],
            shape((copies, sent, LANES), BF),
            scratch=[
                pltpu.VMEM((n * cells, sent, LANES), BF),
                pltpu.VMEM(
                    ((n_kern * kernels.shape[2] + 1) // 2, 2 * tabs.grid, 2 * cell), F32
                ),
            ],
        )
        grads = lax.all_to_all(grads, ("cells", "corners", "kern"), 0, 0, tiled=True)
        if iteration == ITERS - 1:
            return call(
                functools.partial(last_body, tabs, slots, n_corners, n_kern),
                [at],
                [theta, grads, sums, tabs.gy, tabs.ex],
                jax.ShapeDtypeStruct((cells, band, cell), F32),
                scratch=[
                    pltpu.VMEM((cells, cell, cell), F32),
                    pltpu.VMEM((cells, band, cell), F32),
                    pltpu.SemaphoreType.DMA((cells,)),
                ],
                out_far=True,
            )
        theta, sums, payload = call(
            functools.partial(update_body, tabs, slots, n_corners, n_kern, n),
            [at],
            [theta, grads, tabs.ph_split, tabs.gy, tabs.ex, tabs.fy, tabs.fx] + payloads,
            [
                shape(theta.shape, F32),
                shape((n * tiles, cells, 2 * LANES), F32),
                shape((cells * sent, LANES), BF),
            ],
        )
        payloads = [payload] + [shifted(payload, "cells", k) for k in range(1, n)]


def solution(mesh):
    in_specs = (
        P(("groups", "cells"), None, None),
        P(("groups", "cells"), None, None),
        P(None, "corners", "kern", None, None),
        P("corners"),
        P(("groups", "cells"), None),
        P(("groups", "cells")),
        P(("groups", "cells")),
    )
    out_specs = P(("groups", "cells"), ("corners", "kern"), None)
    return jax.shard_map(
        per_device, mesh=mesh, in_specs=in_specs, out_specs=out_specs, check_vma=False
    )
```

```python
import functools

import jax
import jax.numpy as jnp
import numpy as np
from jax import lax
from jax.experimental import pallas as pl
from jax.experimental.pallas import tpu as pltpu
from jax.sharding import PartitionSpec as P


ITERS = 2
LR = 0.25
EPS = 1e-06
STEEP = 3.0
LANES = 128
HALF = LANES // 2
INFO = 16
CHUNK = 8
BF = jnp.bfloat16
F32 = jnp.float32


def up(value, step):
    return -(-value // step) * step


def split(array):
    high = np.asarray(array, np.float32).astype(BF)
    low = (np.asarray(array, np.float32) - high.astype(np.float32)).astype(BF)
    return high, low


class Tables:
    def __init__(self, cell, freq):
        self.cell, self.freq = cell, freq
        self.mid = freq // 2
        self.rows = up(self.mid + 1, 8)
        self.grid = min(cell, up(4 * self.mid + 1, 8))
        rows, grid, mid = self.rows, self.grid, self.mid
        turn = 2.0 * np.pi / cell
        f = np.arange(mid + 1)
        g = np.arange(freq) - mid
        pixels = np.arange(cell)
        fy = np.zeros((cell, LANES))
        phase = (pixels[:, None] * g[None, :] % cell) * turn
        fy[:, :freq] = np.cos(phase)
        fy[:, HALF : HALF + freq] = -np.sin(phase)
        self.fy = np.concatenate(split(fy), axis=1)
        fx = np.zeros((2 * rows, cell))
        phase = (f[:, None] * pixels[None, :] % cell) * turn
        fx[: mid + 1] = np.cos(phase)
        fx[rows : rows + mid + 1] = np.sin(phase)
        self.fx = np.concatenate(split(fx), axis=0)
        ex = np.concatenate([fx[:rows].T, -fx[rows:].T], axis=1)
        self.ex = ex.astype(np.float32).astype(BF)
        gy = np.zeros((LANES, 2 * cell))
        phase = (g[:, None] * pixels[None, :] % cell) * turn
        gy[:freq, :cell] = np.cos(phase)
        gy[:freq, cell:] = np.sin(phase)
        gy[HALF : HALF + freq, :cell] = -np.sin(phase)
        gy[HALF : HALF + freq, cell:] = np.cos(phase)
        self.gy = gy.astype(np.float32).astype(BF)
        both = np.concatenate([gy, np.roll(gy, HALF, axis=0)], axis=0)
        self.gyy = both.astype(np.float32).astype(BF)
        self.gyy_t = self.gyy.T.copy()
        gx = np.zeros((2 * grid, 4 * rows))
        phase = (f[None, :] * np.arange(grid)[:, None] % grid) * (2.0 * np.pi / grid)
        cos, sin = np.zeros((grid, rows)), np.zeros((grid, rows))
        cos[:, : mid + 1], sin[:, : mid + 1] = np.cos(phase), np.sin(phase)
        gx[:grid] = np.concatenate([cos, cos, -sin, -sin], axis=1)
        gx[grid:] = np.concatenate([sin, -sin, cos, -cos], axis=1)
        self.gx = gx.astype(np.float32).astype(BF)
        self.gx_t = self.gx.T.copy()
        u = np.arange(-2 * mid, 2 * mid + 1)
        if grid == cell:
            weights = np.eye(cell)
        else:
            diff = pixels[:, None] / cell - np.arange(grid)[None, :] / grid
            weights = np.cos(2.0 * np.pi * diff[:, :, None] * u).sum(-1) / grid
        high, low = split(weights)
        self.w = np.zeros((cell, up(3 * grid, 16)), np.float32).astype(BF)
        self.w[:, : 3 * grid] = np.concatenate([high, high, low], axis=1)
        self.w_t = high.T.copy()
        ph = np.zeros((cell, 2 * LANES))
        phase = (pixels[:, None] * g[None, :] % cell) * turn
        ph[:, :freq] = ph[:, HALF : HALF + freq] = np.cos(phase)
        ph[:, LANES : LANES + freq] = np.sin(phase)
        ph[:, LANES + HALF : LANES + HALF + freq] = -np.sin(phase)
        self.ph = ph.astype(np.float32)
        self.ph_split = np.concatenate(split(ph), axis=1)
        pick_u, pick_v = np.zeros((rows, freq)), np.zeros((rows, freq))
        for row in range(mid + 1):
            pick_u[row, mid + row] = 1.0
            if row > 0:
                pick_v[row, mid - row] = 1.0
        self.pick = np.stack([pick_u, pick_v]).astype(np.float32).astype(BF)
        lane = np.zeros((4, freq, LANES))
        for col in range(freq):
            lane[0, col, col] = 1.0
            lane[1, col, HALF + col] = 1.0
            lane[2, col, freq - 1 - col] = 1.0
            lane[3, col, HALF + freq - 1 - col] = -1.0
        self.lane = lane.astype(np.float32).astype(BF)


def packing(tabs):
    sent = tabs.rows - 8
    free = HALF - tabs.freq
    extra = tabs.mid + 1 - sent
    pieces = -(-tabs.freq // free) if free > 0 else 0
    if sent % 16 or free < 8 or extra < 1 or extra * pieces > 8:
        return up(tabs.rows, 16), []
    steps = []
    for p in range(pieces):
        begin = p * free
        steps.append((begin, min(free, tabs.freq - begin), p * extra, extra))
    return sent, steps


def inside(first, count, value):
    return (value >= first) & (value < first + count)


def pack(tabs, spec):
    sent, steps = packing(tabs)
    if not steps:
        return jnp.concatenate([spec, jnp.zeros((sent - tabs.rows, LANES), F32)], axis=0).astype(BF)
    row = lax.broadcasted_iota(jnp.int32, (8, LANES), 0)
    col = lane_of((8, LANES)) % HALF
    top, rest = spec[:8], spec[sent:]
    for begin, width, where, extra in steps:
        moved = pltpu.roll(rest, tabs.freq - begin, 1)
        if where:
            moved = pltpu.roll(moved, where, 0)
        here = inside(where, extra, row) & inside(tabs.freq, width, col)
        top = jnp.where(here, moved, top)
    return jnp.concatenate([top, spec[8:sent]], axis=0).astype(BF)


def unpack(tabs, sent_spec):
    _, steps = packing(tabs)
    if not steps:
        return sent_spec[: tabs.rows].astype(F32)
    spec = sent_spec.astype(F32)
    row = lax.broadcasted_iota(jnp.int32, (8, LANES), 0)
    col = lane_of((8, LANES)) % HALF
    rest = jnp.zeros((8, LANES), F32)
    for begin, width, where, extra in steps:
        moved = pltpu.roll(spec[:8], LANES - (tabs.freq - begin), 1)
        if where:
            moved = pltpu.roll(moved, 8 - where, 0)
        here = inside(0, extra, row) & inside(begin, width, col)
        rest = jnp.where(here, moved, rest)
    return jnp.concatenate([spec, rest], axis=0)


def dot(a, b, **kw):
    return jnp.dot(a, b, preferred_element_type=F32, **kw)


def swap(x):
    return pltpu.roll(x, HALF, 1)


def lane_of(shape):
    return lax.broadcasted_iota(jnp.int32, shape, len(shape) - 1)


def arrange_body(dose, kern, pick, lane, out):
    root = jnp.sqrt(jnp.full((1, 1), dose[0], F32))
    for k in range(out.shape[0]):
        real = (kern[0, 0, k] * root).astype(BF)
        imag = (kern[1, 0, k] * root).astype(BF)
        upper = (dot(real, lane[0]) + dot(imag, lane[1])).astype(BF)
        lower = (dot(real, lane[2]) + dot(imag, lane[3])).astype(BF)
        both = jnp.concatenate([dot(pick[0], upper), dot(pick[1], lower)], axis=0)
        out[k] = both.astype(BF)


def spectra(tabs, slots, theta, fy, fx, out):
    cells, cell, rows = theta.shape[0], tabs.cell, tabs.rows
    mask = jax.nn.sigmoid(theta).astype(BF).reshape(cells * cell, cell)
    along = dot(mask, fy[...])
    along = along[:, :LANES] + along[:, LANES:]
    sign = jnp.where(lane_of((rows, LANES)) < HALF, 1.0, -1.0)
    row_at = lax.broadcasted_iota(jnp.int32, (rows, LANES), 0)
    centre = jnp.where((row_at == 0) & (lane_of((rows, LANES)) == tabs.mid), 1.0 / slots, 0.0)
    scale = 2.0 / (slots * cell * cell)
    for c in range(cells):
        part = along[c * cell : (c + 1) * cell]
        high = part.astype(BF)
        low = (part - high.astype(F32)).astype(BF)
        res = dot(fx[...], jnp.concatenate([high, low], axis=1))
        res = res[: 2 * rows, :LANES] + res[: 2 * rows, LANES:] + res[2 * rows :, :LANES]
        spec = res[:rows] + swap(res[rows:]) * sign
        sent = packing(tabs)[0]
        out[c * sent : (c + 1) * sent] = pack(tabs, spec * scale - centre)


def first_body(tabs, slots, owner, local, shift, theta, fy, fx, out):
    spectra(tabs, slots, theta[...], fy, fx, out)
    base = theta.shape[0] * packing(tabs)[0]
    row = lax.broadcasted_iota(jnp.int32, (INFO, LANES), 0)
    col = lane_of((INFO, LANES))
    info = jnp.zeros((INFO, LANES), jnp.int32)
    for i in range(local.shape[0]):
        value = jnp.where(row == 0, owner[i], jnp.where(row == 1, local[i], shift[i]))
        info = jnp.where((col == i) & (row < 3), value, info)
    out[base : base + INFO] = info.astype(F32).astype(BF)


def counts(tabs, n, tiles, cells, slots, at, ph, payload, out):
    z = at[0]
    base = cells * packing(tabs)[0]
    row = lax.broadcasted_iota(jnp.int32, (tiles * cells, LANES), 0)
    col = lane_of((tiles * cells, LANES))
    shift_at = lax.broadcasted_iota(jnp.int32, (tabs.cell, LANES), 0)
    numbers = []
    for k in range(n):
        info = payload[k][base : base + INFO].astype(F32).astype(jnp.int32)
        owner, local, shift = info[0:1], info[1:2], info[2:3]
        mine = (owner == z) & (local == row % cells) & (col // slots == row // cells)
        mine = mine & (col < tiles * slots)
        chosen = jnp.where(mine, 1.0, 0.0).astype(BF)
        hot = jnp.where(shift == shift_at, 1.0, 0.0).astype(BF)
        numbers.append(
            lax.dot_general(chosen, hot, (((1,), (1,)), ((), ())), preferred_element_type=F32)
        )
    sums = dot(jnp.concatenate(numbers, axis=0).astype(BF), ph[...])
    sums = sums[:, : 2 * LANES] + sums[:, 2 * LANES :]
    for k in range(n):
        source = lax.rem(z - k + n, n)
        part = sums[k * tiles * cells : (k + 1) * tiles * cells]
        out[pl.ds(source * tiles, tiles)] = part.reshape(tiles, cells, 2 * LANES)


def tile_body(tabs, n, cells, tiles, copies, at, owner, local, shift, *refs):
    payload, refs = refs[:n], refs[n:]
    arranged, refs = refs[:tiles], refs[tiles:]
    target, ph, gyy, gyy_t, gx, gx_t, w, w_t, out, held, wide, tall, near = refs
    rows, cell, grid = tabs.rows, tabs.cell, tabs.grid
    slots = local.shape[0] // tiles
    z, j = at[0], at[1]
    for k in range(n):
        sent = packing(tabs)[0]
        held[pl.ds(k * cells, cells)] = payload[k][0 : cells * sent].reshape(cells, sent, LANES)
    spec = jnp.zeros((rows, LANES), F32)
    for s in range(slots):
        i = j * slots + s
        which = lax.rem(z - owner[i] + n, n) * cells + local[i]
        one = unpack(tabs, held[which])
        turn = ph[pl.ds(shift[i], 1)]
        spec = spec + one * turn[:, :LANES] + swap(one) * turn[:, LANES:]
    left = lane_of((rows, LANES)) < HALF
    other = swap(spec)
    real = jnp.where(left, spec, other)
    imag = jnp.where(left, other, -spec)
    real = jnp.concatenate([real, real], axis=0)
    imag = jnp.concatenate([imag, imag], axis=0)
    wanted = target[j].astype(F32)
    span = 2 * rows
    members = [(ref, k) for ref in arranged for k in range(ref.shape[0])]
    number = len(members)
    for m, (ref, k) in enumerate(members):
        kern = ref[k].astype(F32)
        wide[m * span : (m + 1) * span, :LANES] = (kern * real).astype(BF)
        wide[m * span : (m + 1) * span, LANES:] = (kern * imag).astype(BF)
    for first in range(0, number, CHUNK):
        last = min(first + CHUNK, number)
        res = dot(wide[first * span : last * span], gyy[...])
        for m in range(first, last):
            part = res[(m - first) * span : (m - first + 1) * span]
            tall[m] = jnp.concatenate([part[:, :cell], part[:, cell:]], axis=0).astype(BF)
    total = jnp.zeros((grid, cell), F32)
    for m in range(0, number, 2):
        pair = [tall[m + p] for p in range(min(2, number - m))]
        fields = dot(gx[...], jnp.concatenate(pair, axis=1))
        for p in range(len(pair)):
            one = fields[:, p * cell : (p + 1) * cell]
            near[m + p] = one
            total = total + (one[:grid] * one[:grid] + one[grid:] * one[grid:])
    high = total.astype(BF).astype(F32)
    stack = [high, total - high, high]
    if w.shape[1] > 3 * grid:
        stack.append(jnp.zeros((w.shape[1] - 3 * grid, cell), F32))
    image = dot(w[...], jnp.concatenate(stack, axis=0).astype(BF))
    resist = jax.nn.sigmoid(STEEP * (image - 1.0))
    pressure = 4.0 * STEEP * (resist - wanted) * resist * (1.0 - resist)
    push = dot(w_t[...], pressure.astype(BF))
    for m in range(0, number, 2):
        pair = []
        for p in range(min(2, number - m)):
            one = near[m + p]
            pair.append(jnp.concatenate([one[:grid] * push, one[grid:] * push], axis=0))
        back = dot(gx_t[...], jnp.concatenate(pair, axis=1).astype(BF)).astype(BF)
        for p in range(len(pair)):
            at_row = (m + p) * span
            wide[at_row : at_row + span, :LANES] = back[:span, p * cell : (p + 1) * cell]
            wide[at_row : at_row + span, LANES:] = back[span:, p * cell : (p + 1) * cell]
    sum_real = jnp.zeros((span, LANES), F32)
    sum_imag = jnp.zeros((span, LANES), F32)
    for first in range(0, number, CHUNK):
        last = min(first + CHUNK, number)
        res = dot(wide[first * span : last * span], gyy_t[...])
        for m in range(first, last):
            ref, k = members[m]
            kern = ref[k].astype(F32)
            part = res[(m - first) * span : (m - first + 1) * span]
            sum_real = sum_real + kern * part[:, :LANES]
            sum_imag = sum_imag + kern * part[:, LANES:]
    sum_real = sum_real[:rows] + sum_real[rows:]
    sum_imag = sum_imag[:rows] + sum_imag[rows:]
    grad = jnp.where(left, sum_real + swap(sum_real), swap(sum_imag - swap(sum_imag)))
    grad = pack(tabs, grad)
    for copy in range(copies):
        out[copy] = grad


def gradients(tabs, slots, corners, kern, theta, grads, sums, gy, ex):
    tiles, cells = sums.shape[0], theta.shape[0]
    rows, cell = tabs.rows, tabs.cell
    pieces = []
    own = []
    for t in range(tiles):
        z, j = t // kern, t % kern
        parts = [grads[(z * corners + x) * kern + j].astype(F32) for x in range(corners)]
        own.append(unpack(tabs, sum(parts[1:], parts[0])))
    swapped = [swap(grad) for grad in own]
    for c in range(cells):
        total = jnp.zeros((rows, LANES), F32)
        for t in range(tiles):
            turn = sums[t, c : c + 1]
            total = total + own[t] * turn[:, :LANES] - swapped[t] * turn[:, LANES:]
        pieces.append(total * (2.0 / (slots * cell * cell)))
    rowed = dot(jnp.concatenate(pieces, axis=0).astype(BF), gy[...])
    result = []
    for first in range(0, cells, 2):
        columns = []
        for c in range(first, min(first + 2, cells)):
            part = rowed[c * rows : (c + 1) * rows]
            columns.append(jnp.concatenate([part[:, :cell], part[:, cell:]], axis=0))
        planes = dot(ex[...], jnp.concatenate(columns, axis=1).astype(BF))
        for p in range(len(columns)):
            squash = jax.nn.sigmoid(theta[first + p])
            gradient = planes[:, p * cell : (p + 1) * cell] * squash * (1.0 - squash)
            power = jnp.sum(gradient * gradient, axis=0, keepdims=True)
            power = jnp.sum(power, axis=1, keepdims=True)
            result.append((gradient, LR * lax.rsqrt(power / (cell * cell) + EPS)))
    return result


def update_body(tabs, slots, corners, kern, n, at, theta, grads, ph, gy, ex, fy, fx, *refs):
    heard, (out, sums, payload) = refs[:n], refs[n:]
    counts(tabs, n, kern, theta.shape[0], slots, at, ph, heard, sums)
    for c, (gradient, rate) in enumerate(
        gradients(tabs, slots, corners, kern, theta, grads, sums, gy, ex)
    ):
        out[c] = theta[c] - rate * gradient
    spectra(tabs, slots, out[...], fy, fx, payload)


def last_body(tabs, slots, corners, kern, at, theta, grads, sums, gy, ex, out, held, ready, sem):
    band = out.shape[1]
    start = pl.multiple_of(at[2] * band, band)
    copies = []
    for c, (gradient, rate) in enumerate(
        gradients(tabs, slots, corners, kern, theta, grads, sums, gy, ex)
    ):
        held[c] = rate * gradient
        ready[c] = theta[c, pl.ds(start, band)] - held[c, pl.ds(start, band)]
        copies.append(pltpu.make_async_copy(ready.at[c], out.at[c], sem.at[c]))
        copies[-1].start()
    for copy in copies:
        copy.wait()


VMEM = pl.BlockSpec(memory_space=pltpu.VMEM)
SMEM = pl.BlockSpec(memory_space=pltpu.SMEM)


def call(body, scalars, arrays, outs, scratch=(), far=(), out_far=False):
    many = isinstance(outs, list)
    arrays = [
        array if place in far else pltpu.with_memory_space_constraint(array, pltpu.VMEM)
        for place, array in enumerate(arrays)
    ]
    out_spec = pl.BlockSpec(memory_space=pl.ANY) if out_far else VMEM
    return pl.pallas_call(
        body,
        out_shape=outs,
        in_specs=[SMEM] * len(scalars) + [VMEM] * len(arrays),
        out_specs=[VMEM] * len(outs) if many else out_spec,
        scratch_shapes=list(scratch),
    )(*scalars, *arrays)


def shape(dims, dtype):
    return pltpu.VMEM(dims, dtype)


def shifted(array, axis, step):
    n = lax.axis_size(axis)
    return lax.ppermute(array, axis, [(i, (i + step) % n) for i in range(n)])


def per_device(theta, target, kernels, dose, inst_owner, inst_local, inst_shift):
    n = lax.axis_size("cells")
    n_kern = lax.axis_size("kern")
    n_corners = lax.axis_size("corners")
    cells, cell = theta.shape[0], theta.shape[1]
    tiles = target.shape[0]
    slots = inst_local.shape[0] // tiles
    assert tiles == n_kern
    tabs = Tables(cell, kernels.shape[3])
    inst_owner = inst_owner[:, 0]
    rows, sent = tabs.rows, packing(tabs)[0]
    at = jnp.stack(
        [lax.axis_index("cells"), lax.axis_index("kern"), lax.axis_index(("corners", "kern"))]
    ).astype(jnp.int32)
    band = cell // (n_kern * n_corners)
    payload = call(
        functools.partial(first_body, tabs, slots),
        [inst_owner, inst_local, inst_shift],
        [theta, tabs.fy, tabs.fx],
        shape((cells * sent + INFO, LANES), BF),
        far=(0, 1, 2),
    )
    payloads = [payload]
    for k in range(1, n):
        payloads.append(shifted(payload, "cells", k))
    own = call(
        arrange_body,
        [dose],
        [kernels, tabs.pick, tabs.lane],
        shape((kernels.shape[2], 2 * rows, LANES), BF),
    )
    arranged = [own] + [shifted(own, "kern", k) for k in range(1, n_kern)]
    copies = n * n_corners * n_kern
    for iteration in range(ITERS):
        grads = call(
            functools.partial(tile_body, tabs, n, cells, tiles, copies),
            [at, inst_owner, inst_local, inst_shift],
            payloads
            + arranged
            + [target, tabs.ph, tabs.gyy, tabs.gyy_t, tabs.gx, tabs.gx_t, tabs.w, tabs.w_t],
            shape((copies, sent, LANES), BF),
            scratch=[
                pltpu.VMEM((n * cells, sent, LANES), BF),
                pltpu.VMEM((n_kern * kernels.shape[2] * 2 * rows, 2 * LANES), BF),
                pltpu.VMEM((n_kern * kernels.shape[2], 4 * rows, cell), BF),
                pltpu.VMEM((n_kern * kernels.shape[2], 2 * tabs.grid, cell), F32),
            ],
        )
        grads = lax.all_to_all(grads, ("cells", "corners", "kern"), 0, 0, tiled=True)
        if iteration == ITERS - 1:
            return call(
                functools.partial(last_body, tabs, slots, n_corners, n_kern),
                [at],
                [theta, grads, sums, tabs.gy, tabs.ex],
                jax.ShapeDtypeStruct((cells, band, cell), F32),
                scratch=[
                    pltpu.VMEM((cells, cell, cell), F32),
                    pltpu.VMEM((cells, band, cell), F32),
                    pltpu.SemaphoreType.DMA((cells,)),
                ],
                out_far=True,
            )
        theta, sums, payload = call(
            functools.partial(update_body, tabs, slots, n_corners, n_kern, n),
            [at],
            [theta, grads, tabs.ph_split, tabs.gy, tabs.ex, tabs.fy, tabs.fx] + payloads,
            [
                shape(theta.shape, F32),
                shape((n * tiles, cells, 2 * LANES), F32),
                shape((cells * sent, LANES), BF),
            ],
        )
        payloads = [payload] + [shifted(payload, "cells", k) for k in range(1, n)]


def solution(mesh):
    in_specs = (
        P(("groups", "cells"), None, None),
        P(("groups", "cells"), None, None),
        P(None, "corners", "kern", None, None),
        P("corners"),
        P(("groups", "cells"), None),
        P(("groups", "cells")),
        P(("groups", "cells")),
    )
    out_specs = P(("groups", "cells"), ("corners", "kern"), None)
    return jax.shard_map(
        per_device, mesh=mesh, in_specs=in_specs, out_specs=out_specs, check_vma=False
    )
```

```python
import functools

import jax
import jax.numpy as jnp
import numpy as np
from jax import lax
from jax.experimental import pallas as pl
from jax.experimental.pallas import tpu as pltpu
from jax.sharding import PartitionSpec as P


ITERS = 2
LR = 0.25
EPS = 1e-06
STEEP = 3.0
LANES = 128
HALF = LANES // 2
INFO = 16
CHUNK = 8
BF = jnp.bfloat16
F32 = jnp.float32


def up(value, step):
    return -(-value // step) * step


def split(array):
    high = np.asarray(array, np.float32).astype(BF)
    low = (np.asarray(array, np.float32) - high.astype(np.float32)).astype(BF)
    return high, low


class Tables:
    def __init__(self, cell, freq):
        self.cell, self.freq = cell, freq
        self.mid = freq // 2
        self.rows = up(self.mid + 1, 8)
        self.grid = min(cell, up(4 * self.mid + 1, 8))
        rows, grid, mid = self.rows, self.grid, self.mid
        turn = 2.0 * np.pi / cell
        f = np.arange(mid + 1)
        g = np.arange(freq) - mid
        pixels = np.arange(cell)
        fy = np.zeros((cell, LANES))
        phase = (pixels[:, None] * g[None, :] % cell) * turn
        fy[:, :freq] = np.cos(phase)
        fy[:, HALF : HALF + freq] = -np.sin(phase)
        self.fy = np.concatenate(split(fy), axis=1)
        fx = np.zeros((2 * rows, cell))
        phase = (f[:, None] * pixels[None, :] % cell) * turn
        fx[: mid + 1] = np.cos(phase)
        fx[rows : rows + mid + 1] = np.sin(phase)
        self.fx = np.concatenate(split(fx), axis=0)
        ex = np.concatenate([fx[:rows].T, -fx[rows:].T], axis=1)
        self.ex = ex.astype(np.float32).astype(BF)
        gy = np.zeros((LANES, 2 * cell))
        phase = (g[:, None] * pixels[None, :] % cell) * turn
        gy[:freq, :cell] = np.cos(phase)
        gy[:freq, cell:] = np.sin(phase)
        gy[HALF : HALF + freq, :cell] = -np.sin(phase)
        gy[HALF : HALF + freq, cell:] = np.cos(phase)
        self.gy = gy.astype(np.float32).astype(BF)
        both = np.concatenate([gy, np.roll(gy, HALF, axis=0)], axis=0)
        self.gyy = both.astype(np.float32).astype(BF)
        self.gyy_t = self.gyy.T.copy()
        gx = np.zeros((2 * grid, 4 * rows))
        phase = (f[None, :] * np.arange(grid)[:, None] % grid) * (2.0 * np.pi / grid)
        cos, sin = np.zeros((grid, rows)), np.zeros((grid, rows))
        cos[:, : mid + 1], sin[:, : mid + 1] = np.cos(phase), np.sin(phase)
        gx[:grid] = np.concatenate([cos, cos, -sin, -sin], axis=1)
        gx[grid:] = np.concatenate([sin, -sin, cos, -cos], axis=1)
        self.gx = gx.astype(np.float32).astype(BF)
        self.gx_t = self.gx.T.copy()
        u = np.arange(-2 * mid, 2 * mid + 1)
        if grid == cell:
            weights = np.eye(cell)
        else:
            diff = pixels[:, None] / cell - np.arange(grid)[None, :] / grid
            weights = np.cos(2.0 * np.pi * diff[:, :, None] * u).sum(-1) / grid
        high, low = split(weights)
        self.w = np.zeros((cell, up(3 * grid, 16)), np.float32).astype(BF)
        self.w[:, : 3 * grid] = np.concatenate([high, high, low], axis=1)
        self.w_t = high.T.copy()
        ph = np.zeros((cell, 2 * LANES))
        phase = (pixels[:, None] * g[None, :] % cell) * turn
        ph[:, :freq] = ph[:, HALF : HALF + freq] = np.cos(phase)
        ph[:, LANES : LANES + freq] = np.sin(phase)
        ph[:, LANES + HALF : LANES + HALF + freq] = -np.sin(phase)
        self.ph = ph.astype(np.float32)
        self.ph_split = np.concatenate(split(ph), axis=1)


def packing(tabs):
    sent = tabs.rows - 8
    free = HALF - tabs.freq
    extra = tabs.mid + 1 - sent
    pieces = -(-tabs.freq // free) if free > 0 else 0
    if sent % 16 or free < 8 or extra < 1 or extra * pieces > 8:
        return up(tabs.rows, 16), []
    steps = []
    for p in range(pieces):
        begin = p * free
        steps.append((begin, min(free, tabs.freq - begin), p * extra, extra))
    return sent, steps


def inside(first, count, value):
    return (value >= first) & (value < first + count)


def pack(tabs, spec):
    sent, steps = packing(tabs)
    if not steps:
        return jnp.concatenate([spec, jnp.zeros((sent - tabs.rows, LANES), F32)], axis=0).astype(BF)
    row = lax.broadcasted_iota(jnp.int32, (8, LANES), 0)
    col = lane_of((8, LANES)) % HALF
    top, rest = spec[:8], spec[sent:]
    for begin, width, where, extra in steps:
        moved = pltpu.roll(rest, tabs.freq - begin, 1)
        if where:
            moved = pltpu.roll(moved, where, 0)
        here = inside(where, extra, row) & inside(tabs.freq, width, col)
        top = jnp.where(here, moved, top)
    return jnp.concatenate([top, spec[8:sent]], axis=0).astype(BF)


def unpack(tabs, sent_spec):
    _, steps = packing(tabs)
    if not steps:
        return sent_spec[: tabs.rows].astype(F32)
    spec = sent_spec.astype(F32)
    row = lax.broadcasted_iota(jnp.int32, (8, LANES), 0)
    col = lane_of((8, LANES)) % HALF
    rest = jnp.zeros((8, LANES), F32)
    for begin, width, where, extra in steps:
        moved = pltpu.roll(spec[:8], LANES - (tabs.freq - begin), 1)
        if where:
            moved = pltpu.roll(moved, 8 - where, 0)
        here = inside(0, extra, row) & inside(begin, width, col)
        rest = jnp.where(here, moved, rest)
    return jnp.concatenate([spec, rest], axis=0)


def dot(a, b, **kw):
    return jnp.dot(a, b, preferred_element_type=F32, **kw)


def swap(x):
    return pltpu.roll(x, HALF, 1)


def lane_of(shape):
    return lax.broadcasted_iota(jnp.int32, shape, len(shape) - 1)


def arrange_body(tabs, dose, kern, out):
    freq, mid, rows = tabs.freq, tabs.mid, tabs.rows
    number, tall = out.shape[0], up(freq, 8)
    root = jnp.sqrt(jnp.full((1, 1), dose[0], F32))
    side = jnp.zeros((freq, HALF - freq), F32)
    below = jnp.zeros((tall - freq, LANES), F32)
    rights = []
    for k in range(number):
        both = jnp.concatenate([kern[0, 0, k] * root, side, kern[1, 0, k] * root, side], axis=1)
        rights.append(jnp.concatenate([both, below], axis=0))
    rights = jnp.concatenate(rights, axis=0).astype(BF)
    row = lax.broadcasted_iota(jnp.int32, (LANES, LANES), 0)
    col = lane_of((LANES, LANES))
    same = (row // HALF == col // HALF) & (row % HALF + col % HALF == freq - 1)
    turned = jnp.where(same, jnp.where(row < HALF, 1.0, -1.0), 0.0).astype(BF)
    lefts = dot(rights, turned)
    rights = rights.astype(F32)
    row = lax.broadcasted_iota(jnp.int32, (2 * rows, 2 * tall), 0)
    col = lane_of((2 * rows, 2 * tall))
    upper = (row <= mid) & (col == mid + row)
    lower = (row > rows) & (row <= rows + mid) & (col == tall + mid - (row - rows))
    pick = jnp.where(upper | lower, 1.0, 0.0).astype(BF)
    for k in range(0, number, 2):
        columns = [
            jnp.concatenate(
                [rights[m * tall : (m + 1) * tall], lefts[m * tall : (m + 1) * tall]], axis=0
            )
            for m in range(k, min(k + 2, number))
        ]
        res = dot(pick, jnp.concatenate(columns, axis=1).astype(BF)).astype(BF)
        for p in range(len(columns)):
            out[k + p] = res[:, p * LANES : (p + 1) * LANES]


def spectra(tabs, slots, theta, fy, fx, out):
    cells, cell, rows = theta.shape[0], tabs.cell, tabs.rows
    mask = jax.nn.sigmoid(theta).astype(BF).reshape(cells * cell, cell)
    along = dot(mask, fy[...])
    along = along[:, :LANES] + along[:, LANES:]
    sign = jnp.where(lane_of((rows, LANES)) < HALF, 1.0, -1.0)
    row_at = lax.broadcasted_iota(jnp.int32, (rows, LANES), 0)
    centre = jnp.where((row_at == 0) & (lane_of((rows, LANES)) == tabs.mid), 1.0 / slots, 0.0)
    scale = 2.0 / (slots * cell * cell)
    for c in range(cells):
        part = along[c * cell : (c + 1) * cell]
        high = part.astype(BF)
        low = (part - high.astype(F32)).astype(BF)
        res = dot(fx[...], jnp.concatenate([high, low], axis=1))
        res = res[: 2 * rows, :LANES] + res[: 2 * rows, LANES:] + res[2 * rows :, :LANES]
        spec = res[:rows] + swap(res[rows:]) * sign
        sent = packing(tabs)[0]
        out[c * sent : (c + 1) * sent] = pack(tabs, spec * scale - centre)


def first_body(tabs, slots, owner, local, shift, theta, fy, fx, out):
    spectra(tabs, slots, theta[...], fy, fx, out)
    base = theta.shape[0] * packing(tabs)[0]
    row = lax.broadcasted_iota(jnp.int32, (INFO, LANES), 0)
    col = lane_of((INFO, LANES))
    info = jnp.zeros((INFO, LANES), jnp.int32)
    for i in range(local.shape[0]):
        value = jnp.where(row == 0, owner[i], jnp.where(row == 1, local[i], shift[i]))
        info = jnp.where((col == i) & (row < 3), value, info)
    out[base : base + INFO] = info.astype(F32).astype(BF)


def counts(tabs, n, tiles, cells, slots, ph, payload, out):
    z = lax.axis_index("cells")
    base = cells * packing(tabs)[0]
    row = lax.broadcasted_iota(jnp.int32, (tiles * cells, LANES), 0)
    col = lane_of((tiles * cells, LANES))
    shift_at = lax.broadcasted_iota(jnp.int32, (tabs.cell, LANES), 0)
    numbers = []
    for k in range(n):
        info = payload[k][base : base + INFO].astype(F32).astype(jnp.int32)
        owner, local, shift = info[0:1], info[1:2], info[2:3]
        mine = (owner == z) & (local == row % cells) & (col // slots == row // cells)
        mine = mine & (col < tiles * slots)
        chosen = jnp.where(mine, 1.0, 0.0).astype(BF)
        hot = jnp.where(shift == shift_at, 1.0, 0.0).astype(BF)
        numbers.append(
            lax.dot_general(chosen, hot, (((1,), (1,)), ((), ())), preferred_element_type=F32)
        )
    sums = dot(jnp.concatenate(numbers, axis=0).astype(BF), ph[...])
    sums = sums[:, : 2 * LANES] + sums[:, 2 * LANES :]
    for k in range(n):
        place = source(n, z, k)
        part = sums[k * tiles * cells : (k + 1) * tiles * cells]
        out[pl.ds(place * tiles, tiles)] = part.reshape(tiles, cells, 2 * LANES)


def tile_body(tabs, n, cells, tiles, copies, owner, local, shift, *refs):
    payload, refs = refs[:n], refs[n:]
    arranged, refs = refs[:tiles], refs[tiles:]
    target, ph, gyy, gyy_t, gx, gx_t, w, w_t, out, held, wide, tall, near = refs
    rows, cell, grid = tabs.rows, tabs.cell, tabs.grid
    slots = local.shape[0] // tiles
    z, j = lax.axis_index("cells"), lax.axis_index("kern")
    for k in range(n):
        sent = packing(tabs)[0]
        held[pl.ds(k * cells, cells)] = payload[k][0 : cells * sent].reshape(cells, sent, LANES)
    spec = jnp.zeros((rows, LANES), F32)
    for s in range(slots):
        i = j * slots + s
        which = source(n, z, owner[i]) * cells + local[i]
        one = unpack(tabs, held[which])
        turn = ph[pl.ds(shift[i], 1)]
        spec = spec + one * turn[:, :LANES] + swap(one) * turn[:, LANES:]
    left = lane_of((rows, LANES)) < HALF
    other = swap(spec)
    real = jnp.where(left, spec, other)
    imag = jnp.where(left, other, -spec)
    real = jnp.concatenate([real, real], axis=0)
    imag = jnp.concatenate([imag, imag], axis=0)
    wanted = target[j].astype(F32)
    span = 2 * rows
    members = [(ref, k) for ref in arranged for k in range(ref.shape[0])]
    number = len(members)
    for m, (ref, k) in enumerate(members):
        kern = ref[k].astype(F32)
        wide[m * span : (m + 1) * span, :LANES] = (kern * real).astype(BF)
        wide[m * span : (m + 1) * span, LANES:] = (kern * imag).astype(BF)
    for first in range(0, number, CHUNK):
        last = min(first + CHUNK, number)
        res = dot(wide[first * span : last * span], gyy[...])
        for m in range(first, last):
            part = res[(m - first) * span : (m - first + 1) * span]
            tall[m] = jnp.concatenate([part[:, :cell], part[:, cell:]], axis=0).astype(BF)
    total = jnp.zeros((grid, cell), F32)
    for m in range(0, number, 2):
        pair = [tall[m + p] for p in range(min(2, number - m))]
        fields = dot(gx[...], jnp.concatenate(pair, axis=1))
        for p in range(len(pair)):
            one = fields[:, p * cell : (p + 1) * cell]
            near[m + p] = one
            total = total + (one[:grid] * one[:grid] + one[grid:] * one[grid:])
    high = total.astype(BF).astype(F32)
    stack = [high, total - high, high]
    if w.shape[1] > 3 * grid:
        stack.append(jnp.zeros((w.shape[1] - 3 * grid, cell), F32))
    image = dot(w[...], jnp.concatenate(stack, axis=0).astype(BF))
    resist = jax.nn.sigmoid(STEEP * (image - 1.0))
    pressure = 4.0 * STEEP * (resist - wanted) * resist * (1.0 - resist)
    push = dot(w_t[...], pressure.astype(BF))
    for m in range(0, number, 2):
        pair = []
        for p in range(min(2, number - m)):
            one = near[m + p]
            pair.append(jnp.concatenate([one[:grid] * push, one[grid:] * push], axis=0))
        back = dot(gx_t[...], jnp.concatenate(pair, axis=1).astype(BF)).astype(BF)
        for p in range(len(pair)):
            at_row = (m + p) * span
            wide[at_row : at_row + span, :LANES] = back[:span, p * cell : (p + 1) * cell]
            wide[at_row : at_row + span, LANES:] = back[span:, p * cell : (p + 1) * cell]
    sum_real = jnp.zeros((span, LANES), F32)
    sum_imag = jnp.zeros((span, LANES), F32)
    for first in range(0, number, CHUNK):
        last = min(first + CHUNK, number)
        res = dot(wide[first * span : last * span], gyy_t[...])
        for m in range(first, last):
            ref, k = members[m]
            kern = ref[k].astype(F32)
            part = res[(m - first) * span : (m - first + 1) * span]
            sum_real = sum_real + kern * part[:, :LANES]
            sum_imag = sum_imag + kern * part[:, LANES:]
    sum_real = sum_real[:rows] + sum_real[rows:]
    sum_imag = sum_imag[:rows] + sum_imag[rows:]
    grad = jnp.where(left, sum_real + swap(sum_real), swap(sum_imag - swap(sum_imag)))
    grad = pack(tabs, grad)
    for copy in range(copies):
        out[copy] = grad


def gradients(tabs, slots, corners, kern, theta, grads, sums, gy, ex):
    tiles, cells = sums.shape[0], theta.shape[0]
    rows, cell = tabs.rows, tabs.cell
    pieces = []
    own = []
    for t in range(tiles):
        z, j = t // kern, t % kern
        parts = [grads[(z * corners + x) * kern + j].astype(F32) for x in range(corners)]
        own.append(unpack(tabs, sum(parts[1:], parts[0])))
    swapped = [swap(grad) for grad in own]
    for c in range(cells):
        total = jnp.zeros((rows, LANES), F32)
        for t in range(tiles):
            turn = sums[t, c : c + 1]
            total = total + own[t] * turn[:, :LANES] - swapped[t] * turn[:, LANES:]
        pieces.append(total * (2.0 / (slots * cell * cell)))
    rowed = dot(jnp.concatenate(pieces, axis=0).astype(BF), gy[...])
    result = []
    for first in range(0, cells, 2):
        columns = []
        for c in range(first, min(first + 2, cells)):
            part = rowed[c * rows : (c + 1) * rows]
            columns.append(jnp.concatenate([part[:, :cell], part[:, cell:]], axis=0))
        planes = dot(ex[...], jnp.concatenate(columns, axis=1).astype(BF))
        for p in range(len(columns)):
            squash = jax.nn.sigmoid(theta[first + p])
            gradient = planes[:, p * cell : (p + 1) * cell] * squash * (1.0 - squash)
            power = jnp.sum(gradient * gradient, axis=0, keepdims=True)
            power = jnp.sum(power, axis=1, keepdims=True)
            result.append((gradient, LR * lax.rsqrt(power / (cell * cell) + EPS)))
    return result


def update_body(tabs, slots, corners, kern, n, theta, grads, ph, gy, ex, fy, fx, *refs):
    heard, (out, sums, payload) = refs[:n], refs[n:]
    counts(tabs, n, kern, theta.shape[0], slots, ph, heard, sums)
    for c, (gradient, rate) in enumerate(
        gradients(tabs, slots, corners, kern, theta, grads, sums, gy, ex)
    ):
        out[c] = theta[c] - rate * gradient
    spectra(tabs, slots, out[...], fy, fx, payload)


def last_body(tabs, slots, corners, kern, theta, grads, sums, gy, ex, out, held, ready, sem):
    band = out.shape[1]
    start = pl.multiple_of(lax.axis_index(("corners", "kern")) * band, band)
    copies = []
    for c, (gradient, rate) in enumerate(
        gradients(tabs, slots, corners, kern, theta, grads, sums, gy, ex)
    ):
        held[c] = rate * gradient
        ready[c] = theta[c, pl.ds(start, band)] - held[c, pl.ds(start, band)]
        copies.append(pltpu.make_async_copy(ready.at[c], out.at[c], sem.at[c]))
        copies[-1].start()
    for copy in copies:
        copy.wait()


VMEM = pl.BlockSpec(memory_space=pltpu.VMEM)
SMEM = pl.BlockSpec(memory_space=pltpu.SMEM)


def call(body, scalars, arrays, outs, scratch=(), far=(), out_far=False):
    many = isinstance(outs, list)
    arrays = [
        array if place in far else pltpu.with_memory_space_constraint(array, pltpu.VMEM)
        for place, array in enumerate(arrays)
    ]
    out_spec = pl.BlockSpec(memory_space=pl.ANY) if out_far else VMEM
    return pl.pallas_call(
        body,
        out_shape=outs,
        in_specs=[SMEM] * len(scalars) + [VMEM] * len(arrays),
        out_specs=[VMEM] * len(outs) if many else out_spec,
        scratch_shapes=list(scratch),
    )(*scalars, *arrays)


def shape(dims, dtype):
    return pltpu.VMEM(dims, dtype)


def paired(n):
    return n & (n - 1) == 0


def source(n, z, step):
    return z ^ step if paired(n) else lax.rem(z - step + n, n)


def shifted(array, axis, step):
    n = lax.axis_size(axis)
    moves = [(i, i ^ step if paired(n) else (i + step) % n) for i in range(n)]
    return lax.ppermute(array, axis, moves)


def per_device(theta, target, kernels, dose, inst_owner, inst_local, inst_shift):
    n = lax.axis_size("cells")
    n_kern = lax.axis_size("kern")
    n_corners = lax.axis_size("corners")
    cells, cell = theta.shape[0], theta.shape[1]
    tiles = target.shape[0]
    slots = inst_local.shape[0] // tiles
    assert tiles == n_kern
    tabs = Tables(cell, kernels.shape[3])
    inst_owner = inst_owner[:, 0]
    rows, sent = tabs.rows, packing(tabs)[0]
    band = cell // (n_kern * n_corners)
    payload = call(
        functools.partial(first_body, tabs, slots),
        [inst_owner, inst_local, inst_shift],
        [theta, tabs.fy, tabs.fx],
        shape((cells * sent + INFO, LANES), BF),
        far=(0, 1, 2),
    )
    payloads = [payload]
    for k in range(1, n):
        payloads.append(shifted(payload, "cells", k))
    own = call(
        functools.partial(arrange_body, tabs),
        [dose],
        [kernels],
        shape((kernels.shape[2], 2 * rows, LANES), BF),
    )
    arranged = [own] + [shifted(own, "kern", k) for k in range(1, n_kern)]
    copies = n * n_corners * n_kern
    for iteration in range(ITERS):
        grads = call(
            functools.partial(tile_body, tabs, n, cells, tiles, copies),
            [inst_owner, inst_local, inst_shift],
            payloads
            + arranged
            + [target, tabs.ph, tabs.gyy, tabs.gyy_t, tabs.gx, tabs.gx_t, tabs.w, tabs.w_t],
            shape((copies, sent, LANES), BF),
            scratch=[
                pltpu.VMEM((n * cells, sent, LANES), BF),
                pltpu.VMEM((n_kern * kernels.shape[2] * 2 * rows, 2 * LANES), BF),
                pltpu.VMEM((n_kern * kernels.shape[2], 4 * rows, cell), BF),
                pltpu.VMEM((n_kern * kernels.shape[2], 2 * tabs.grid, cell), F32),
            ],
        )
        grads = lax.all_to_all(grads, ("cells", "corners", "kern"), 0, 0, tiled=True)
        if iteration == ITERS - 1:
            return call(
                functools.partial(last_body, tabs, slots, n_corners, n_kern),
                [],
                [theta, grads, sums, tabs.gy, tabs.ex],
                jax.ShapeDtypeStruct((cells, band, cell), F32),
                scratch=[
                    pltpu.VMEM((cells, cell, cell), F32),
                    pltpu.VMEM((cells, band, cell), F32),
                    pltpu.SemaphoreType.DMA((cells,)),
                ],
                out_far=True,
            )
        theta, sums, payload = call(
            functools.partial(update_body, tabs, slots, n_corners, n_kern, n),
            [],
            [theta, grads, tabs.ph_split, tabs.gy, tabs.ex, tabs.fy, tabs.fx] + payloads,
            [
                shape(theta.shape, F32),
                shape((n * tiles, cells, 2 * LANES), F32),
                shape((cells * sent, LANES), BF),
            ],
        )
        payloads = [payload]
        for k in range(1, n):
            payloads.append(shifted(payload, "cells", k))


def solution(mesh):
    in_specs = (
        P(("groups", "cells"), None, None),
        P(("groups", "cells"), None, None),
        P(None, "corners", "kern", None, None),
        P("corners"),
        P(("groups", "cells"), None),
        P(("groups", "cells")),
        P(("groups", "cells")),
    )
    out_specs = P(("groups", "cells"), ("corners", "kern"), None)
    return jax.shard_map(
        per_device, mesh=mesh, in_specs=in_specs, out_specs=out_specs, check_vma=False
    )
```

```python
import functools

import jax
import jax.numpy as jnp
import numpy as np
from jax import lax
from jax.experimental import pallas as pl
from jax.experimental.pallas import tpu as pltpu
from jax.sharding import PartitionSpec as P


ITERS = 2
LR = 0.25
EPS = 1e-06
STEEP = 3.0
LANES = 128
HALF = LANES // 2
INFO = 16
CHUNK = 8
BF = jnp.bfloat16
F32 = jnp.float32


def up(value, step):
    return -(-value // step) * step


def split(array):
    high = np.asarray(array, np.float32).astype(BF)
    low = (np.asarray(array, np.float32) - high.astype(np.float32)).astype(BF)
    return high, low


class Tables:
    def __init__(self, cell, freq):
        self.cell, self.freq = cell, freq
        self.mid = freq // 2
        self.rows = up(self.mid + 1, 8)
        self.grid = min(cell, up(4 * self.mid + 1, 8))
        rows, grid, mid = self.rows, self.grid, self.mid
        turn = 2.0 * np.pi / cell
        f = np.arange(mid + 1)
        g = np.arange(freq) - mid
        pixels = np.arange(cell)
        fy = np.zeros((cell, LANES))
        phase = (pixels[:, None] * g[None, :] % cell) * turn
        fy[:, :freq] = np.cos(phase)
        fy[:, HALF : HALF + freq] = -np.sin(phase)
        self.fy = np.concatenate(split(fy), axis=1)
        fx = np.zeros((2 * rows, cell))
        phase = (f[:, None] * pixels[None, :] % cell) * turn
        fx[: mid + 1] = np.cos(phase)
        fx[rows : rows + mid + 1] = np.sin(phase)
        self.fx = np.concatenate(split(fx), axis=0)
        ex = np.concatenate([fx[:rows].T, -fx[rows:].T], axis=1)
        self.ex = ex.astype(np.float32).astype(BF)
        gy = np.zeros((LANES, 2 * cell))
        phase = (g[:, None] * pixels[None, :] % cell) * turn
        gy[:freq, :cell] = np.cos(phase)
        gy[:freq, cell:] = np.sin(phase)
        gy[HALF : HALF + freq, :cell] = -np.sin(phase)
        gy[HALF : HALF + freq, cell:] = np.cos(phase)
        self.gy = gy.astype(np.float32).astype(BF)
        both = np.concatenate([gy, np.roll(gy, HALF, axis=0)], axis=0)
        self.gyy = both.astype(np.float32).astype(BF)
        self.gyy_t = self.gyy.T.copy()
        gx = np.zeros((2 * grid, 4 * rows))
        phase = (f[None, :] * np.arange(grid)[:, None] % grid) * (2.0 * np.pi / grid)
        cos, sin = np.zeros((grid, rows)), np.zeros((grid, rows))
        cos[:, : mid + 1], sin[:, : mid + 1] = np.cos(phase), np.sin(phase)
        gx[:grid] = np.concatenate([cos, cos, -sin, -sin], axis=1)
        gx[grid:] = np.concatenate([sin, -sin, cos, -cos], axis=1)
        self.gx = gx.astype(np.float32).astype(BF)
        self.gx_t = self.gx.T.copy()
        u = np.arange(-2 * mid, 2 * mid + 1)
        if grid == cell:
            weights = np.eye(cell)
        else:
            diff = pixels[:, None] / cell - np.arange(grid)[None, :] / grid
            weights = np.cos(2.0 * np.pi * diff[:, :, None] * u).sum(-1) / grid
        high, low = split(weights)
        self.w = np.zeros((cell, up(3 * grid, 16)), np.float32).astype(BF)
        self.w[:, : 3 * grid] = np.concatenate([high, high, low], axis=1)
        self.w_t = high.T.copy()
        ph = np.zeros((cell, 2 * LANES))
        phase = (pixels[:, None] * g[None, :] % cell) * turn
        ph[:, :freq] = ph[:, HALF : HALF + freq] = np.cos(phase)
        ph[:, LANES : LANES + freq] = np.sin(phase)
        ph[:, LANES + HALF : LANES + HALF + freq] = -np.sin(phase)
        self.ph = ph.astype(np.float32)
        self.ph_split = np.concatenate(split(ph), axis=1)


def packing(tabs):
    sent = tabs.rows - 8
    free = HALF - tabs.freq
    extra = tabs.mid + 1 - sent
    pieces = -(-tabs.freq // free) if free > 0 else 0
    if sent % 16 or free < 8 or extra < 1 or extra * pieces > 8:
        return up(tabs.rows, 16), []
    steps = []
    for p in range(pieces):
        begin = p * free
        steps.append((begin, min(free, tabs.freq - begin), p * extra, extra))
    return sent, steps


def inside(first, count, value):
    return (value >= first) & (value < first + count)


def pack(tabs, spec):
    sent, steps = packing(tabs)
    if not steps:
        return jnp.concatenate([spec, jnp.zeros((sent - tabs.rows, LANES), F32)], axis=0).astype(BF)
    row = lax.broadcasted_iota(jnp.int32, (8, LANES), 0)
    col = lane_of((8, LANES)) % HALF
    top, rest = spec[:8], spec[sent:]
    for begin, width, where, extra in steps:
        moved = pltpu.roll(rest, tabs.freq - begin, 1)
        if where:
            moved = pltpu.roll(moved, where, 0)
        here = inside(where, extra, row) & inside(tabs.freq, width, col)
        top = jnp.where(here, moved, top)
    return jnp.concatenate([top, spec[8:sent]], axis=0).astype(BF)


def unpack(tabs, sent_spec):
    _, steps = packing(tabs)
    if not steps:
        return sent_spec[: tabs.rows].astype(F32)
    spec = sent_spec.astype(F32)
    row = lax.broadcasted_iota(jnp.int32, (8, LANES), 0)
    col = lane_of((8, LANES)) % HALF
    rest = jnp.zeros((8, LANES), F32)
    for begin, width, where, extra in steps:
        moved = pltpu.roll(spec[:8], LANES - (tabs.freq - begin), 1)
        if where:
            moved = pltpu.roll(moved, 8 - where, 0)
        here = inside(0, extra, row) & inside(begin, width, col)
        rest = jnp.where(here, moved, rest)
    return jnp.concatenate([spec, rest], axis=0)


def dot(a, b, **kw):
    return jnp.dot(a, b, preferred_element_type=F32, **kw)


def swap(x):
    return pltpu.roll(x, HALF, 1)


def lane_of(shape):
    return lax.broadcasted_iota(jnp.int32, shape, len(shape) - 1)


def arrange_body(tabs, kern, out):
    freq, mid, rows = tabs.freq, tabs.mid, tabs.rows
    number, tall = out.shape[0], up(freq, 8)
    side = jnp.zeros((freq, HALF - freq), F32)
    below = jnp.zeros((tall - freq, LANES), F32)
    rights = []
    for k in range(number):
        both = jnp.concatenate([kern[0, 0, k], side, kern[1, 0, k], side], axis=1)
        rights.append(jnp.concatenate([both, below], axis=0))
    rights = jnp.concatenate(rights, axis=0).astype(BF)
    row = lax.broadcasted_iota(jnp.int32, (LANES, LANES), 0)
    col = lane_of((LANES, LANES))
    same = (row // HALF == col // HALF) & (row % HALF + col % HALF == freq - 1)
    turned = jnp.where(same, jnp.where(row < HALF, 1.0, -1.0), 0.0).astype(BF)
    lefts = dot(rights, turned)
    rights = rights.astype(F32)
    row = lax.broadcasted_iota(jnp.int32, (2 * rows, 2 * tall), 0)
    col = lane_of((2 * rows, 2 * tall))
    upper = (row <= mid) & (col == mid + row)
    lower = (row > rows) & (row <= rows + mid) & (col == tall + mid - (row - rows))
    pick = jnp.where(upper | lower, 1.0, 0.0).astype(BF)
    for k in range(0, number, 2):
        columns = [
            jnp.concatenate(
                [rights[m * tall : (m + 1) * tall], lefts[m * tall : (m + 1) * tall]], axis=0
            )
            for m in range(k, min(k + 2, number))
        ]
        res = dot(pick, jnp.concatenate(columns, axis=1).astype(BF)).astype(BF)
        for p in range(len(columns)):
            out[k + p] = res[:, p * LANES : (p + 1) * LANES]


def spectra(tabs, slots, theta, fy, fx, out):
    cells, cell, rows = theta.shape[0], tabs.cell, tabs.rows
    mask = jax.nn.sigmoid(theta).astype(BF).reshape(cells * cell, cell)
    along = dot(mask, fy[...])
    along = along[:, :LANES] + along[:, LANES:]
    sign = jnp.where(lane_of((rows, LANES)) < HALF, 1.0, -1.0)
    row_at = lax.broadcasted_iota(jnp.int32, (rows, LANES), 0)
    centre = jnp.where((row_at == 0) & (lane_of((rows, LANES)) == tabs.mid), 1.0 / slots, 0.0)
    scale = 2.0 / (slots * cell * cell)
    for c in range(cells):
        part = along[c * cell : (c + 1) * cell]
        high = part.astype(BF)
        low = (part - high.astype(F32)).astype(BF)
        res = dot(fx[...], jnp.concatenate([high, low], axis=1))
        res = res[: 2 * rows, :LANES] + res[: 2 * rows, LANES:] + res[2 * rows :, :LANES]
        spec = res[:rows] + swap(res[rows:]) * sign
        sent = packing(tabs)[0]
        out[c * sent : (c + 1) * sent] = pack(tabs, spec * scale - centre)


def first_body(tabs, slots, owner, local, shift, theta, fy, fx, out, table):
    spectra(tabs, slots, theta[...], fy, fx, out)
    base = theta.shape[0] * packing(tabs)[0]
    row = lax.broadcasted_iota(jnp.int32, (INFO, LANES), 0)
    col = lane_of((INFO, LANES))
    info = jnp.zeros((INFO, LANES), jnp.int32)
    for i in range(local.shape[0]):
        table[0, i] = owner[i]
        table[1, i] = local[i]
        table[2, i] = shift[i]
        value = jnp.where(row == 0, owner[i], jnp.where(row == 1, local[i], shift[i]))
        info = jnp.where((col == i) & (row < 3), value, info)
    out[base : base + INFO] = info.astype(F32).astype(BF)


def counts(tabs, n, tiles, cells, slots, ph, payload, out):
    z = lax.axis_index("cells")
    base = cells * packing(tabs)[0]
    row = lax.broadcasted_iota(jnp.int32, (tiles * cells, LANES), 0)
    col = lane_of((tiles * cells, LANES))
    shift_at = lax.broadcasted_iota(jnp.int32, (tabs.cell, LANES), 0)
    numbers = []
    for k in range(n):
        info = payload[k][base : base + INFO].astype(F32).astype(jnp.int32)
        owner, local, shift = info[0:1], info[1:2], info[2:3]
        mine = (owner == z) & (local == row % cells) & (col // slots == row // cells)
        mine = mine & (col < tiles * slots)
        chosen = jnp.where(mine, 1.0, 0.0).astype(BF)
        hot = jnp.where(shift == shift_at, 1.0, 0.0).astype(BF)
        numbers.append(
            lax.dot_general(chosen, hot, (((1,), (1,)), ((), ())), preferred_element_type=F32)
        )
    sums = dot(jnp.concatenate(numbers, axis=0).astype(BF), ph[...])
    sums = sums[:, : 2 * LANES] + sums[:, 2 * LANES :]
    for k in range(n):
        place = source(n, z, k)
        part = sums[k * tiles * cells : (k + 1) * tiles * cells]
        out[pl.ds(place * tiles, tiles)] = part.reshape(tiles, cells, 2 * LANES)


def tile_body(tabs, n, cells, tiles, copies, table, dose, *refs):
    payload, refs = refs[:n], refs[n:]
    arranged, refs = refs[:tiles], refs[tiles:]
    target, ph, gyy, gyy_t, gx, gx_t, w, w_t, out, held, wide, tall, near = refs
    rows, cell, grid = tabs.rows, tabs.cell, tabs.grid
    slots = table.shape[1] // tiles
    z, j = lax.axis_index("cells"), lax.axis_index("kern")
    for k in range(n):
        sent = packing(tabs)[0]
        held[pl.ds(k * cells, cells)] = payload[k][0 : cells * sent].reshape(cells, sent, LANES)
    spec = jnp.zeros((rows, LANES), F32)
    for s in range(slots):
        i = j * slots + s
        which = source(n, z, table[0, i]) * cells + table[1, i]
        one = unpack(tabs, held[which])
        turn = ph[pl.ds(table[2, i], 1)]
        spec = spec + one * turn[:, :LANES] + swap(one) * turn[:, LANES:]
    left = lane_of((rows, LANES)) < HALF
    other = swap(spec)
    real = jnp.where(left, spec, other)
    imag = jnp.where(left, other, -spec)
    real = jnp.concatenate([real, real], axis=0)
    imag = jnp.concatenate([imag, imag], axis=0)
    wanted = target[j].astype(F32)
    span = 2 * rows
    members = [(ref, k) for ref in arranged for k in range(ref.shape[0])]
    number = len(members)
    for m, (ref, k) in enumerate(members):
        kern = ref[k].astype(F32)
        wide[m * span : (m + 1) * span, :LANES] = (kern * real).astype(BF)
        wide[m * span : (m + 1) * span, LANES:] = (kern * imag).astype(BF)
    for first in range(0, number, CHUNK):
        last = min(first + CHUNK, number)
        res = dot(wide[first * span : last * span], gyy[...])
        for m in range(first, last):
            part = res[(m - first) * span : (m - first + 1) * span]
            tall[m] = jnp.concatenate([part[:, :cell], part[:, cell:]], axis=0).astype(BF)
    total = jnp.zeros((grid, cell), F32)
    for m in range(0, number, 2):
        pair = [tall[m + p] for p in range(min(2, number - m))]
        fields = dot(gx[...], jnp.concatenate(pair, axis=1))
        for p in range(len(pair)):
            one = fields[:, p * cell : (p + 1) * cell]
            near[m + p] = one
            total = total + (one[:grid] * one[:grid] + one[grid:] * one[grid:])
    high = total.astype(BF).astype(F32)
    stack = [high, total - high, high]
    if w.shape[1] > 3 * grid:
        stack.append(jnp.zeros((w.shape[1] - 3 * grid, cell), F32))
    image = dot(w[...], jnp.concatenate(stack, axis=0).astype(BF))
    resist = jax.nn.sigmoid(STEEP * (dose[0] * image - 1.0))
    pressure = 4.0 * STEEP * dose[0] * (resist - wanted) * resist * (1.0 - resist)
    push = dot(w_t[...], pressure.astype(BF))
    for m in range(0, number, 2):
        pair = []
        for p in range(min(2, number - m)):
            one = near[m + p]
            pair.append(jnp.concatenate([one[:grid] * push, one[grid:] * push], axis=0))
        back = dot(gx_t[...], jnp.concatenate(pair, axis=1).astype(BF)).astype(BF)
        for p in range(len(pair)):
            at_row = (m + p) * span
            wide[at_row : at_row + span, :LANES] = back[:span, p * cell : (p + 1) * cell]
            wide[at_row : at_row + span, LANES:] = back[span:, p * cell : (p + 1) * cell]
    sum_real = jnp.zeros((span, LANES), F32)
    sum_imag = jnp.zeros((span, LANES), F32)
    for first in range(0, number, CHUNK):
        last = min(first + CHUNK, number)
        res = dot(wide[first * span : last * span], gyy_t[...])
        for m in range(first, last):
            ref, k = members[m]
            kern = ref[k].astype(F32)
            part = res[(m - first) * span : (m - first + 1) * span]
            sum_real = sum_real + kern * part[:, :LANES]
            sum_imag = sum_imag + kern * part[:, LANES:]
    sum_real = sum_real[:rows] + sum_real[rows:]
    sum_imag = sum_imag[:rows] + sum_imag[rows:]
    grad = jnp.where(left, sum_real + swap(sum_real), swap(sum_imag - swap(sum_imag)))
    grad = pack(tabs, grad)
    for copy in range(copies):
        out[copy] = grad


def gradients(tabs, slots, corners, kern, theta, grads, sums, gy, ex):
    tiles, cells = sums.shape[0], theta.shape[0]
    rows, cell = tabs.rows, tabs.cell
    pieces = []
    own = []
    for t in range(tiles):
        z, j = t // kern, t % kern
        parts = [grads[(z * corners + x) * kern + j].astype(F32) for x in range(corners)]
        own.append(unpack(tabs, sum(parts[1:], parts[0])))
    swapped = [swap(grad) for grad in own]
    for c in range(cells):
        total = jnp.zeros((rows, LANES), F32)
        for t in range(tiles):
            turn = sums[t, c : c + 1]
            total = total + own[t] * turn[:, :LANES] - swapped[t] * turn[:, LANES:]
        pieces.append(total * (2.0 / (slots * cell * cell)))
    rowed = dot(jnp.concatenate(pieces, axis=0).astype(BF), gy[...])
    result = []
    for first in range(0, cells, 2):
        columns = []
        for c in range(first, min(first + 2, cells)):
            part = rowed[c * rows : (c + 1) * rows]
            columns.append(jnp.concatenate([part[:, :cell], part[:, cell:]], axis=0))
        planes = dot(ex[...], jnp.concatenate(columns, axis=1).astype(BF))
        for p in range(len(columns)):
            squash = jax.nn.sigmoid(theta[first + p])
            gradient = planes[:, p * cell : (p + 1) * cell] * squash * (1.0 - squash)
            power = jnp.sum(gradient * gradient, axis=0, keepdims=True)
            power = jnp.sum(power, axis=1, keepdims=True)
            result.append((gradient, LR * lax.rsqrt(power / (cell * cell) + EPS)))
    return result


def update_body(tabs, slots, corners, kern, n, theta, grads, ph, gy, ex, fy, fx, *refs):
    heard, (out, sums, payload) = refs[:n], refs[n:]
    counts(tabs, n, kern, theta.shape[0], slots, ph, heard, sums)
    for c, (gradient, rate) in enumerate(
        gradients(tabs, slots, corners, kern, theta, grads, sums, gy, ex)
    ):
        out[c] = theta[c] - rate * gradient
    spectra(tabs, slots, out[...], fy, fx, payload)


def last_body(tabs, slots, corners, kern, theta, grads, sums, gy, ex, out, held, ready, sem):
    band = out.shape[1]
    start = pl.multiple_of(lax.axis_index(("corners", "kern")) * band, band)
    copies = []
    for c, (gradient, rate) in enumerate(
        gradients(tabs, slots, corners, kern, theta, grads, sums, gy, ex)
    ):
        held[c] = rate * gradient
        ready[c] = theta[c, pl.ds(start, band)] - held[c, pl.ds(start, band)]
        copies.append(pltpu.make_async_copy(ready.at[c], out.at[c], sem.at[c]))
        copies[-1].start()
    for copy in copies:
        copy.wait()


VMEM = pl.BlockSpec(memory_space=pltpu.VMEM)
SMEM = pl.BlockSpec(memory_space=pltpu.SMEM)


def call(body, scalars, arrays, outs, scratch=(), name=None, far=(), out_far=False):
    many = isinstance(outs, list)
    if name == "tile":
        scalars = [pltpu.with_memory_space_constraint(array, pltpu.SMEM) for array in scalars]
    arrays = [
        array if place in far else pltpu.with_memory_space_constraint(array, pltpu.VMEM)
        for place, array in enumerate(arrays)
    ]
    out_spec = pl.BlockSpec(memory_space=pl.ANY) if out_far else VMEM
    return pl.pallas_call(
        body,
        out_shape=outs,
        in_specs=[SMEM] * len(scalars) + [VMEM] * len(arrays),
        out_specs=[
            SMEM if out.memory_space == pltpu.SMEM else VMEM for out in outs
        ] if many else out_spec,
        scratch_shapes=list(scratch),
    )(*scalars, *arrays)


def shape(dims, dtype):
    return pltpu.VMEM(dims, dtype)


def paired(n):
    return n & (n - 1) == 0


def source(n, z, step):
    return z ^ step if paired(n) else lax.rem(z - step + n, n)


def shifted(array, axis, step):
    n = lax.axis_size(axis)
    moves = [(i, i ^ step if paired(n) else (i + step) % n) for i in range(n)]
    return lax.ppermute(array, axis, moves)


def per_device(theta, target, kernels, dose, inst_owner, inst_local, inst_shift):
    n = lax.axis_size("cells")
    n_kern = lax.axis_size("kern")
    n_corners = lax.axis_size("corners")
    cells, cell = theta.shape[0], theta.shape[1]
    tiles = target.shape[0]
    slots = inst_local.shape[0] // tiles
    assert tiles == n_kern
    tabs = Tables(cell, kernels.shape[3])
    inst_owner = inst_owner[:, 0]
    rows, sent = tabs.rows, packing(tabs)[0]
    band = cell // (n_kern * n_corners)
    payload, table = call(
        functools.partial(first_body, tabs, slots),
        [inst_owner, inst_local, inst_shift],
        [theta, tabs.fy, tabs.fx],
        [
            shape((cells * sent + INFO, LANES), BF),
            pltpu.SMEM((3, inst_local.shape[0]), jnp.int32),
        ],
        name="first",
        far=(0, 1, 2),
    )
    payloads = [payload]
    for k in range(1, n):
        payloads.append(shifted(payload, "cells", k))
    own = call(
        functools.partial(arrange_body, tabs),
        [],
        [kernels],
        shape((kernels.shape[2], 2 * rows, LANES), BF),
        name="arrange",
    )
    arranged = [own]
    for k in range(1, n_kern):
        arranged.append(shifted(own, "kern", k))
    copies = n * n_corners * n_kern
    for iteration in range(ITERS):
        grads = call(
            functools.partial(tile_body, tabs, n, cells, tiles, copies),
            [table, dose],
            payloads
            + arranged
            + [target, tabs.ph, tabs.gyy, tabs.gyy_t, tabs.gx, tabs.gx_t, tabs.w, tabs.w_t],
            shape((copies, sent, LANES), BF),
            scratch=[
                pltpu.VMEM((n * cells, sent, LANES), BF),
                pltpu.VMEM((n_kern * kernels.shape[2] * 2 * rows, 2 * LANES), BF),
                pltpu.VMEM((n_kern * kernels.shape[2], 4 * rows, cell), BF),
                pltpu.VMEM((n_kern * kernels.shape[2], 2 * tabs.grid, cell), F32),
            ],
            name="tile",
        )
        grads = lax.all_to_all(grads, ("cells", "corners", "kern"), 0, 0, tiled=True)
        if iteration == ITERS - 1:
            return call(
                functools.partial(last_body, tabs, slots, n_corners, n_kern),
                [],
                [theta, grads, sums, tabs.gy, tabs.ex],
                jax.ShapeDtypeStruct((cells, band, cell), F32),
                scratch=[
                    pltpu.VMEM((cells, cell, cell), F32),
                    pltpu.VMEM((cells, band, cell), F32),
                    pltpu.SemaphoreType.DMA((cells,)),
                ],
                name="last",
                out_far=True,
            )
        theta, sums, payload = call(
            functools.partial(update_body, tabs, slots, n_corners, n_kern, n),
            [],
            [theta, grads, tabs.ph_split, tabs.gy, tabs.ex, tabs.fy, tabs.fx] + payloads,
            [
                shape(theta.shape, F32),
                shape((n * tiles, cells, 2 * LANES), F32),
                shape((cells * sent, LANES), BF),
            ],
            name="update",
        )
        payloads = [payload]
        for k in range(1, n):
            payloads.append(shifted(payload, "cells", k))


def solution(mesh):
    in_specs = (
        P(("groups", "cells"), None, None),
        P(("groups", "cells"), None, None),
        P(None, "corners", "kern", None, None),
        P("corners"),
        P(("groups", "cells"), None),
        P(("groups", "cells")),
        P(("groups", "cells")),
    )
    out_specs = P(("groups", "cells"), ("corners", "kern"), None)
    return jax.shard_map(
        per_device, mesh=mesh, in_specs=in_specs, out_specs=out_specs, check_vma=False
    )
```

```python
import functools

import jax
import jax.numpy as jnp
import numpy as np
from jax import lax
from jax.experimental import pallas as pl
from jax.experimental.pallas import tpu as pltpu
from jax.sharding import PartitionSpec as P


ITERS = 2
LR = 0.25
EPS = 1e-06
STEEP = 3.0
LANES = 128
HALF = LANES // 2
INFO = 16
CHUNK = 8
BF = jnp.bfloat16
F32 = jnp.float32


def up(value, step):
    return -(-value // step) * step


def split(array):
    high = np.asarray(array, np.float32).astype(BF)
    low = (np.asarray(array, np.float32) - high.astype(np.float32)).astype(BF)
    return high, low


class Tables:
    def __init__(self, cell, freq):
        self.cell, self.freq = cell, freq
        self.mid = freq // 2
        self.rows = up(self.mid + 1, 8)
        self.grid = min(cell, up(4 * self.mid + 1, 8))
        rows, grid, mid = self.rows, self.grid, self.mid
        turn = 2.0 * np.pi / cell
        f = np.arange(mid + 1)
        g = np.arange(freq) - mid
        pixels = np.arange(cell)
        fy = np.zeros((cell, LANES))
        phase = (pixels[:, None] * g[None, :] % cell) * turn
        fy[:, :freq] = np.cos(phase)
        fy[:, HALF : HALF + freq] = -np.sin(phase)
        self.fy = np.concatenate(split(fy), axis=1)
        fx = np.zeros((2 * rows, cell))
        phase = (f[:, None] * pixels[None, :] % cell) * turn
        fx[: mid + 1] = np.cos(phase)
        fx[rows : rows + mid + 1] = np.sin(phase)
        self.fx = np.concatenate(split(fx), axis=0)
        ex = np.concatenate([fx[:rows].T, -fx[rows:].T], axis=1)
        self.ex = ex.astype(np.float32).astype(BF)
        gy = np.zeros((LANES, 2 * cell))
        phase = (g[:, None] * pixels[None, :] % cell) * turn
        gy[:freq, :cell] = np.cos(phase)
        gy[:freq, cell:] = np.sin(phase)
        gy[HALF : HALF + freq, :cell] = -np.sin(phase)
        gy[HALF : HALF + freq, cell:] = np.cos(phase)
        self.gy = gy.astype(np.float32).astype(BF)
        both = np.concatenate([gy, np.roll(gy, HALF, axis=0)], axis=0)
        self.gyy = both.astype(np.float32).astype(BF)
        self.gyy_t = self.gyy.T.copy()
        gx = np.zeros((2 * grid, 4 * rows))
        phase = (f[None, :] * np.arange(grid)[:, None] % grid) * (2.0 * np.pi / grid)
        cos, sin = np.zeros((grid, rows)), np.zeros((grid, rows))
        cos[:, : mid + 1], sin[:, : mid + 1] = np.cos(phase), np.sin(phase)
        gx[:grid] = np.concatenate([cos, cos, -sin, -sin], axis=1)
        gx[grid:] = np.concatenate([sin, -sin, cos, -cos], axis=1)
        self.gx = gx.astype(np.float32).astype(BF)
        self.gx_t = self.gx.T.copy()
        u = np.arange(-2 * mid, 2 * mid + 1)
        if grid == cell:
            weights = np.eye(cell)
        else:
            diff = pixels[:, None] / cell - np.arange(grid)[None, :] / grid
            weights = np.cos(2.0 * np.pi * diff[:, :, None] * u).sum(-1) / grid
        high, low = split(weights)
        self.w = np.zeros((cell, up(3 * grid, 16)), np.float32).astype(BF)
        self.w[:, : 3 * grid] = np.concatenate([high, high, low], axis=1)
        self.w_t = high.T.copy()
        ph = np.zeros((cell, 2 * LANES))
        phase = (pixels[:, None] * g[None, :] % cell) * turn
        ph[:, :freq] = ph[:, HALF : HALF + freq] = np.cos(phase)
        ph[:, LANES : LANES + freq] = np.sin(phase)
        ph[:, LANES + HALF : LANES + HALF + freq] = -np.sin(phase)
        self.ph = ph.astype(np.float32)
        self.ph_split = np.concatenate(split(ph), axis=1)


def packing(tabs):
    sent = tabs.rows - 8
    free = HALF - tabs.freq
    extra = tabs.mid + 1 - sent
    pieces = -(-tabs.freq // free) if free > 0 else 0
    if sent % 16 or free < 8 or extra < 1 or extra * pieces > 8:
        return up(tabs.rows, 16), []
    steps = []
    for p in range(pieces):
        begin = p * free
        steps.append((begin, min(free, tabs.freq - begin), p * extra, extra))
    return sent, steps


def inside(first, count, value):
    return (value >= first) & (value < first + count)


def pack(tabs, spec):
    sent, steps = packing(tabs)
    if not steps:
        return jnp.concatenate([spec, jnp.zeros((sent - tabs.rows, LANES), F32)], axis=0).astype(BF)
    row = lax.broadcasted_iota(jnp.int32, (8, LANES), 0)
    col = lane_of((8, LANES)) % HALF
    top, rest = spec[:8], spec[sent:]
    for begin, width, where, extra in steps:
        moved = pltpu.roll(rest, tabs.freq - begin, 1)
        if where:
            moved = pltpu.roll(moved, where, 0)
        here = inside(where, extra, row) & inside(tabs.freq, width, col)
        top = jnp.where(here, moved, top)
    return jnp.concatenate([top, spec[8:sent]], axis=0).astype(BF)


def unpack(tabs, sent_spec):
    _, steps = packing(tabs)
    if not steps:
        return sent_spec[: tabs.rows].astype(F32)
    spec = sent_spec.astype(F32)
    row = lax.broadcasted_iota(jnp.int32, (8, LANES), 0)
    col = lane_of((8, LANES)) % HALF
    rest = jnp.zeros((8, LANES), F32)
    for begin, width, where, extra in steps:
        moved = pltpu.roll(spec[:8], LANES - (tabs.freq - begin), 1)
        if where:
            moved = pltpu.roll(moved, 8 - where, 0)
        here = inside(0, extra, row) & inside(begin, width, col)
        rest = jnp.where(here, moved, rest)
    return jnp.concatenate([spec, rest], axis=0)


def dot(a, b, **kw):
    return jnp.dot(a, b, preferred_element_type=F32, **kw)


def swap(x):
    return pltpu.roll(x, HALF, 1)


def lane_of(shape):
    return lax.broadcasted_iota(jnp.int32, shape, len(shape) - 1)


def arrange_body(tabs, kern, out):
    freq, mid, rows = tabs.freq, tabs.mid, tabs.rows
    number, tall = out.shape[0], up(freq, 8)
    side = jnp.zeros((freq, HALF - freq), F32)
    below = jnp.zeros((tall - freq, LANES), F32)
    rights = []
    for k in range(number):
        both = jnp.concatenate([kern[0, 0, k], side, kern[1, 0, k], side], axis=1)
        rights.append(jnp.concatenate([both, below], axis=0))
    rights = jnp.concatenate(rights, axis=0).astype(BF)
    row = lax.broadcasted_iota(jnp.int32, (LANES, LANES), 0)
    col = lane_of((LANES, LANES))
    same = (row // HALF == col // HALF) & (row % HALF + col % HALF == freq - 1)
    turned = jnp.where(same, jnp.where(row < HALF, 1.0, -1.0), 0.0).astype(BF)
    lefts = dot(rights, turned)
    rights = rights.astype(F32)
    row = lax.broadcasted_iota(jnp.int32, (2 * rows, 2 * tall), 0)
    col = lane_of((2 * rows, 2 * tall))
    upper = (row <= mid) & (col == mid + row)
    lower = (row > rows) & (row <= rows + mid) & (col == tall + mid - (row - rows))
    pick = jnp.where(upper | lower, 1.0, 0.0).astype(BF)
    for k in range(0, number, 2):
        columns = [
            jnp.concatenate(
                [rights[m * tall : (m + 1) * tall], lefts[m * tall : (m + 1) * tall]], axis=0
            )
            for m in range(k, min(k + 2, number))
        ]
        res = dot(pick, jnp.concatenate(columns, axis=1).astype(BF)).astype(BF)
        for p in range(len(columns)):
            out[k + p] = res[:, p * LANES : (p + 1) * LANES]


def spectra(tabs, slots, theta, fy, fx):
    cells, cell, rows = theta.shape[0], tabs.cell, tabs.rows
    mask = jax.nn.sigmoid(theta).astype(BF).reshape(cells * cell, cell)
    along = dot(mask, fy[...])
    along = along[:, :LANES] + along[:, LANES:]
    sign = jnp.where(lane_of((rows, LANES)) < HALF, 1.0, -1.0)
    row_at = lax.broadcasted_iota(jnp.int32, (rows, LANES), 0)
    centre = jnp.where((row_at == 0) & (lane_of((rows, LANES)) == tabs.mid), 1.0 / slots, 0.0)
    scale = 2.0 / (slots * cell * cell)
    specs = []
    for c in range(cells):
        part = along[c * cell : (c + 1) * cell]
        high = part.astype(BF)
        low = (part - high.astype(F32)).astype(BF)
        res = dot(fx[...], jnp.concatenate([high, low], axis=1))
        res = res[: 2 * rows, :LANES] + res[: 2 * rows, LANES:] + res[2 * rows :, :LANES]
        spec = res[:rows] + swap(res[rows:]) * sign
        specs.append(spec * scale - centre)
    return specs


def first_body(tabs, slots, owner, local, shift, theta, fy, fx, out, table):
    sent = packing(tabs)[0]
    for c, spec in enumerate(spectra(tabs, slots, theta[...], fy, fx)):
        out[c * sent : (c + 1) * sent] = pack(tabs, spec)
    base = theta.shape[0] * sent
    row = lax.broadcasted_iota(jnp.int32, (INFO, LANES), 0)
    col = lane_of((INFO, LANES))
    info = jnp.zeros((INFO, LANES), jnp.int32)
    for i in range(local.shape[0]):
        table[0, i] = owner[i]
        table[1, i] = local[i]
        table[2, i] = shift[i]
        value = jnp.where(row == 0, owner[i], jnp.where(row == 1, local[i], shift[i]))
        info = jnp.where((col == i) & (row < 3), value, info)
    out[base : base + INFO] = info.astype(F32).astype(BF)


def counts(tabs, n, tiles, cells, slots, ph, payload, out):
    z = lax.axis_index("cells")
    base = cells * packing(tabs)[0]
    row = lax.broadcasted_iota(jnp.int32, (tiles * cells, LANES), 0)
    col = lane_of((tiles * cells, LANES))
    shift_at = lax.broadcasted_iota(jnp.int32, (tabs.cell, LANES), 0)
    numbers = []
    for k in range(n):
        info = payload[k][base : base + INFO].astype(F32).astype(jnp.int32)
        owner, local, shift = info[0:1], info[1:2], info[2:3]
        mine = (owner == z) & (local == row % cells) & (col // slots == row // cells)
        mine = mine & (col < tiles * slots)
        chosen = jnp.where(mine, 1.0, 0.0).astype(BF)
        hot = jnp.where(shift == shift_at, 1.0, 0.0).astype(BF)
        numbers.append(
            lax.dot_general(chosen, hot, (((1,), (1,)), ((), ())), preferred_element_type=F32)
        )
    sums = dot(jnp.concatenate(numbers, axis=0).astype(BF), ph[...])
    sums = sums[:, : 2 * LANES] + sums[:, 2 * LANES :]
    for k in range(n):
        place = source(n, z, k)
        part = sums[k * tiles * cells : (k + 1) * tiles * cells]
        out[pl.ds(place * tiles, tiles)] = part.reshape(tiles, cells, 2 * LANES)


def tile_body(tabs, n, cells, tiles, copies, table, dose, *refs):
    payload, (ph, *rest, out, held, wide, tall, near) = refs[:n], refs[n:]
    slots = table.shape[1] // tiles
    z, j = lax.axis_index("cells"), lax.axis_index("kern")
    sent = packing(tabs)[0]
    for k in range(n):
        held[pl.ds(k * cells, cells)] = payload[k][0 : cells * sent].reshape(cells, sent, LANES)
    spec = jnp.zeros((tabs.rows, LANES), F32)
    for s in range(slots):
        i = j * slots + s
        which = source(n, z, table[0, i]) * cells + table[1, i]
        one = unpack(tabs, held[which])
        turn = ph[pl.ds(table[2, i], 1)]
        spec = spec + one * turn[:, :LANES] + swap(one) * turn[:, LANES:]
    tile_gradient(tabs, tiles, copies, spec, dose, rest, out, wide, tall, near)


def again_body(tabs, n, tiles, copies, dose, *refs):
    parts, (*rest, out, wide, tall, near) = refs[:n], refs[n:]
    total = parts[0][...].astype(F32)
    for k in range(1, n):
        total = total + parts[k][...].astype(F32)
    spec = unpack(tabs, total)
    tile_gradient(tabs, tiles, copies, spec, dose, rest, out, wide, tall, near)


def tile_gradient(tabs, tiles, copies, spec, dose, rest, out, wide, tall, near):
    arranged, (target, gyy, gyy_t, gx, gx_t, w, w_t) = rest[:tiles], rest[tiles:]
    rows, cell, grid = tabs.rows, tabs.cell, tabs.grid
    left = lane_of((rows, LANES)) < HALF
    other = swap(spec)
    real = jnp.where(left, spec, other)
    imag = jnp.where(left, other, -spec)
    real = jnp.concatenate([real, real], axis=0)
    imag = jnp.concatenate([imag, imag], axis=0)
    wanted = target[lax.axis_index("kern")].astype(F32)
    span = 2 * rows
    members = [(ref, k) for ref in arranged for k in range(ref.shape[0])]
    number = len(members)
    for m, (ref, k) in enumerate(members):
        kern = ref[k].astype(F32)
        wide[m * span : (m + 1) * span, :LANES] = (kern * real).astype(BF)
        wide[m * span : (m + 1) * span, LANES:] = (kern * imag).astype(BF)
    for first in range(0, number, CHUNK):
        last = min(first + CHUNK, number)
        res = dot(wide[first * span : last * span], gyy[...])
        for m in range(first, last):
            part = res[(m - first) * span : (m - first + 1) * span]
            tall[m] = jnp.concatenate([part[:, :cell], part[:, cell:]], axis=0).astype(BF)
    total = jnp.zeros((grid, cell), F32)
    for m in range(0, number, 2):
        pair = [tall[m + p] for p in range(min(2, number - m))]
        fields = dot(gx[...], jnp.concatenate(pair, axis=1))
        for p in range(len(pair)):
            one = fields[:, p * cell : (p + 1) * cell]
            near[m + p] = one
            total = total + (one[:grid] * one[:grid] + one[grid:] * one[grid:])
    high = total.astype(BF).astype(F32)
    stack = [high, total - high, high]
    if w.shape[1] > 3 * grid:
        stack.append(jnp.zeros((w.shape[1] - 3 * grid, cell), F32))
    image = dot(w[...], jnp.concatenate(stack, axis=0).astype(BF))
    resist = jax.nn.sigmoid(STEEP * (dose[0] * image - 1.0))
    pressure = 4.0 * STEEP * dose[0] * (resist - wanted) * resist * (1.0 - resist)
    push = dot(w_t[...], pressure.astype(BF))
    for m in range(0, number, 2):
        pair = []
        for p in range(min(2, number - m)):
            one = near[m + p]
            pair.append(jnp.concatenate([one[:grid] * push, one[grid:] * push], axis=0))
        back = dot(gx_t[...], jnp.concatenate(pair, axis=1).astype(BF)).astype(BF)
        for p in range(len(pair)):
            at_row = (m + p) * span
            wide[at_row : at_row + span, :LANES] = back[:span, p * cell : (p + 1) * cell]
            wide[at_row : at_row + span, LANES:] = back[span:, p * cell : (p + 1) * cell]
    sum_real = jnp.zeros((span, LANES), F32)
    sum_imag = jnp.zeros((span, LANES), F32)
    for first in range(0, number, CHUNK):
        last = min(first + CHUNK, number)
        res = dot(wide[first * span : last * span], gyy_t[...])
        for m in range(first, last):
            ref, k = members[m]
            kern = ref[k].astype(F32)
            part = res[(m - first) * span : (m - first + 1) * span]
            sum_real = sum_real + kern * part[:, :LANES]
            sum_imag = sum_imag + kern * part[:, LANES:]
    sum_real = sum_real[:rows] + sum_real[rows:]
    sum_imag = sum_imag[:rows] + sum_imag[rows:]
    grad = jnp.where(left, sum_real + swap(sum_real), swap(sum_imag - swap(sum_imag)))
    grad = pack(tabs, grad)
    for copy in range(copies):
        out[copy] = grad


def gradients(tabs, slots, corners, kern, theta, grads, sums, gy, ex):
    tiles, cells = sums.shape[0], theta.shape[0]
    rows, cell = tabs.rows, tabs.cell
    pieces = []
    own = []
    for t in range(tiles):
        z, j = t // kern, t % kern
        parts = [grads[(z * corners + x) * kern + j].astype(F32) for x in range(corners)]
        own.append(unpack(tabs, sum(parts[1:], parts[0])))
    swapped = [swap(grad) for grad in own]
    for c in range(cells):
        total = jnp.zeros((rows, LANES), F32)
        for t in range(tiles):
            turn = sums[t, c : c + 1]
            total = total + own[t] * turn[:, :LANES] - swapped[t] * turn[:, LANES:]
        pieces.append(total * (2.0 / (slots * cell * cell)))
    rowed = dot(jnp.concatenate(pieces, axis=0).astype(BF), gy[...])
    result = []
    for first in range(0, cells, 2):
        columns = []
        for c in range(first, min(first + 2, cells)):
            part = rowed[c * rows : (c + 1) * rows]
            columns.append(jnp.concatenate([part[:, :cell], part[:, cell:]], axis=0))
        planes = dot(ex[...], jnp.concatenate(columns, axis=1).astype(BF))
        for p in range(len(columns)):
            squash = jax.nn.sigmoid(theta[first + p])
            gradient = planes[:, p * cell : (p + 1) * cell] * squash * (1.0 - squash)
            power = jnp.sum(gradient * gradient, axis=0, keepdims=True)
            power = jnp.sum(power, axis=1, keepdims=True)
            result.append((gradient, LR * lax.rsqrt(power / (cell * cell) + EPS)))
    return result


def update_body(tabs, slots, corners, kern, n, theta, grads, ph, gy, ex, fy, fx, *refs):
    heard, (out, sums, *parts) = refs[:n], refs[n:]
    counts(tabs, n, kern, theta.shape[0], slots, ph, heard, sums)
    for c, (gradient, rate) in enumerate(
        gradients(tabs, slots, corners, kern, theta, grads, sums, gy, ex)
    ):
        out[c] = theta[c] - rate * gradient
    specs = spectra(tabs, slots, out[...], fy, fx)
    swapped = [swap(spec) for spec in specs]
    z, j = lax.axis_index("cells"), lax.axis_index("kern")
    for k in range(n):
        turns = sums[target_of(n, z, k) * kern + j]
        total = jnp.zeros((tabs.rows, LANES), F32)
        for c, spec in enumerate(specs):
            turn = turns[c : c + 1]
            total = total + spec * turn[:, :LANES] + swapped[c] * turn[:, LANES:]
        parts[k][...] = pack(tabs, total)


def last_body(tabs, slots, corners, kern, theta, grads, sums, gy, ex, out, held, ready, sem):
    band = out.shape[1]
    start = pl.multiple_of(lax.axis_index(("corners", "kern")) * band, band)
    copies = []
    for c, (gradient, rate) in enumerate(
        gradients(tabs, slots, corners, kern, theta, grads, sums, gy, ex)
    ):
        held[c] = rate * gradient
        ready[c] = theta[c, pl.ds(start, band)] - held[c, pl.ds(start, band)]
        copies.append(pltpu.make_async_copy(ready.at[c], out.at[c], sem.at[c]))
        copies[-1].start()
    for copy in copies:
        copy.wait()


VMEM = pl.BlockSpec(memory_space=pltpu.VMEM)
SMEM = pl.BlockSpec(memory_space=pltpu.SMEM)


def call(body, scalars, arrays, outs, scratch=(), name=None, far=(), out_far=False):
    many = isinstance(outs, list)
    if name in ("tile", "again"):
        scalars = [pltpu.with_memory_space_constraint(array, pltpu.SMEM) for array in scalars]
    arrays = [
        array if place in far else pltpu.with_memory_space_constraint(array, pltpu.VMEM)
        for place, array in enumerate(arrays)
    ]
    out_spec = pl.BlockSpec(memory_space=pl.ANY) if out_far else VMEM
    return pl.pallas_call(
        body,
        out_shape=outs,
        in_specs=[SMEM] * len(scalars) + [VMEM] * len(arrays),
        out_specs=[
            SMEM if out.memory_space == pltpu.SMEM else VMEM for out in outs
        ] if many else out_spec,
        scratch_shapes=list(scratch),
    )(*scalars, *arrays)


def shape(dims, dtype):
    return pltpu.VMEM(dims, dtype)


def paired(n):
    return n & (n - 1) == 0


def source(n, z, step):
    return z ^ step if paired(n) else lax.rem(z - step + n, n)


def target_of(n, z, step):
    return z ^ step if paired(n) else lax.rem(z + step, n)


def shifted(array, axis, step):
    n = lax.axis_size(axis)
    moves = [(i, i ^ step if paired(n) else (i + step) % n) for i in range(n)]
    return lax.ppermute(array, axis, moves)


def per_device(theta, target, kernels, dose, inst_owner, inst_local, inst_shift):
    n = lax.axis_size("cells")
    n_kern = lax.axis_size("kern")
    n_corners = lax.axis_size("corners")
    cells, cell = theta.shape[0], theta.shape[1]
    tiles = target.shape[0]
    slots = inst_local.shape[0] // tiles
    assert tiles == n_kern
    tabs = Tables(cell, kernels.shape[3])
    inst_owner = inst_owner[:, 0]
    rows, sent = tabs.rows, packing(tabs)[0]
    band = cell // (n_kern * n_corners)
    payload, table = call(
        functools.partial(first_body, tabs, slots),
        [inst_owner, inst_local, inst_shift],
        [theta, tabs.fy, tabs.fx],
        [
            shape((cells * sent + INFO, LANES), BF),
            pltpu.SMEM((3, inst_local.shape[0]), jnp.int32),
        ],
        name="first",
        far=(0, 1, 2),
    )
    payloads = [payload]
    for k in range(1, n):
        payloads.append(shifted(payload, "cells", k))
    own = call(
        functools.partial(arrange_body, tabs),
        [],
        [kernels],
        shape((kernels.shape[2], 2 * rows, LANES), BF),
        name="arrange",
    )
    arranged = [own]
    for k in range(1, n_kern):
        arranged.append(shifted(own, "kern", k))
    copies = n * n_corners * n_kern
    count = n_kern * kernels.shape[2]
    scratch = [
        pltpu.VMEM((count * 2 * rows, 2 * LANES), BF),
        pltpu.VMEM((count, 4 * rows, cell), BF),
        pltpu.VMEM((count, 2 * tabs.grid, cell), F32),
    ]
    common = arranged + [target, tabs.gyy, tabs.gyy_t, tabs.gx, tabs.gx_t, tabs.w, tabs.w_t]
    everyone = ("cells", "corners", "kern")
    grads = call(
        functools.partial(tile_body, tabs, n, cells, tiles, copies),
        [table, dose],
        payloads + [tabs.ph] + common,
        shape((copies, sent, LANES), BF),
        scratch=[pltpu.VMEM((n * cells, sent, LANES), BF)] + scratch,
        name="tile",
    )
    for _ in range(1, ITERS):
        grads = lax.all_to_all(grads, everyone, 0, 0, tiled=True)
        theta, sums, *parts = call(
            functools.partial(update_body, tabs, slots, n_corners, n_kern, n),
            [],
            [theta, grads, tabs.ph_split, tabs.gy, tabs.ex, tabs.fy, tabs.fx] + payloads,
            [shape(theta.shape, F32), shape((n * tiles, cells, 2 * LANES), F32)]
            + [shape((sent, LANES), BF)] * n,
            name="update",
        )
        for k in range(1, n):
            parts[k] = shifted(parts[k], "cells", k)
        grads = call(
            functools.partial(again_body, tabs, n, tiles, copies),
            [dose],
            parts + common,
            shape((copies, sent, LANES), BF),
            scratch=scratch,
            name="again",
        )
    grads = lax.all_to_all(grads, everyone, 0, 0, tiled=True)
    return call(
        functools.partial(last_body, tabs, slots, n_corners, n_kern),
        [],
        [theta, grads, sums, tabs.gy, tabs.ex],
        jax.ShapeDtypeStruct((cells, band, cell), F32),
        scratch=[
            pltpu.VMEM((cells, cell, cell), F32),
            pltpu.VMEM((cells, band, cell), F32),
            pltpu.SemaphoreType.DMA((cells,)),
        ],
        name="last",
        out_far=True,
    )


def solution(mesh):
    in_specs = (
        P(("groups", "cells"), None, None),
        P(("groups", "cells"), None, None),
        P(None, "corners", "kern", None, None),
        P("corners"),
        P(("groups", "cells"), None),
        P(("groups", "cells")),
        P(("groups", "cells")),
    )
    out_specs = P(("groups", "cells"), ("corners", "kern"), None)
    return jax.shard_map(
        per_device, mesh=mesh, in_specs=in_specs, out_specs=out_specs, check_vma=False
    )
```

```python
import functools

import jax
import jax.numpy as jnp
import numpy as np
from jax import lax
from jax.experimental import pallas as pl
from jax.experimental.pallas import tpu as pltpu
from jax.sharding import PartitionSpec as P


ITERS = 2
LR = 0.25
EPS = 1e-06
STEEP = 3.0
LANES = 128
HALF = LANES // 2
INFO = 16
CHUNK = 8
BF = jnp.bfloat16
F32 = jnp.float32


def up(value, step):
    return -(-value // step) * step


def split(array):
    high = np.asarray(array, np.float32).astype(BF)
    low = (np.asarray(array, np.float32) - high.astype(np.float32)).astype(BF)
    return high, low


class Tables:
    def __init__(self, cell, freq):
        self.cell, self.freq = cell, freq
        self.mid = freq // 2
        self.rows = up(self.mid + 1, 8)
        self.grid = min(cell, up(4 * self.mid + 1, 8))
        rows, grid, mid = self.rows, self.grid, self.mid
        turn = 2.0 * np.pi / cell
        f = np.arange(mid + 1)
        g = np.arange(freq) - mid
        pixels = np.arange(cell)
        fy = np.zeros((cell, LANES))
        phase = (pixels[:, None] * g[None, :] % cell) * turn
        fy[:, :freq] = np.cos(phase)
        fy[:, HALF : HALF + freq] = -np.sin(phase)
        self.fy = np.concatenate(split(fy), axis=1)
        fx = np.zeros((2 * rows, cell))
        phase = (f[:, None] * pixels[None, :] % cell) * turn
        fx[: mid + 1] = np.cos(phase)
        fx[rows : rows + mid + 1] = np.sin(phase)
        self.fx = np.concatenate(split(fx), axis=0)
        ex = np.concatenate([fx[:rows].T, -fx[rows:].T], axis=1)
        self.ex = ex.astype(np.float32).astype(BF)
        gy = np.zeros((LANES, 2 * cell))
        phase = (g[:, None] * pixels[None, :] % cell) * turn
        gy[:freq, :cell] = np.cos(phase)
        gy[:freq, cell:] = np.sin(phase)
        gy[HALF : HALF + freq, :cell] = -np.sin(phase)
        gy[HALF : HALF + freq, cell:] = np.cos(phase)
        self.gy = gy.astype(np.float32).astype(BF)
        both = np.concatenate([gy, np.roll(gy, HALF, axis=0)], axis=0)
        self.gyy = both.astype(np.float32).astype(BF)
        self.gyy_t = self.gyy.T.copy()
        self.span = up(2 * mid + 1, 8)
        phase = (f[None, :] * np.arange(grid)[:, None] % grid) * (2.0 * np.pi / grid)
        blank = np.zeros((grid, self.span - 2 * mid - 1))
        cos, sin = np.cos(phase), np.sin(phase)
        upper = [cos, cos[:, 1:], blank, -sin, -sin[:, 1:], blank]
        lower = [sin, -sin[:, 1:], blank, cos, -cos[:, 1:], blank]
        gx = np.concatenate([np.concatenate(r, axis=1) for r in (upper, lower)], axis=0)
        self.gx = gx.astype(np.float32).astype(BF)
        self.gx_t = self.gx.T.copy()
        u = np.arange(-2 * mid, 2 * mid + 1)
        if grid == cell:
            weights = np.eye(cell)
        else:
            diff = pixels[:, None] / cell - np.arange(grid)[None, :] / grid
            weights = np.cos(2.0 * np.pi * diff[:, :, None] * u).sum(-1) / grid
        high, low = split(weights)
        self.w = np.zeros((cell, up(3 * grid, 16)), np.float32).astype(BF)
        self.w[:, : 3 * grid] = np.concatenate([high, high, low], axis=1)
        self.w_t = high.T.copy()
        ph = np.zeros((cell, 2 * LANES))
        phase = (pixels[:, None] * g[None, :] % cell) * turn
        ph[:, :freq] = ph[:, HALF : HALF + freq] = np.cos(phase)
        ph[:, LANES : LANES + freq] = np.sin(phase)
        ph[:, LANES + HALF : LANES + HALF + freq] = -np.sin(phase)
        self.ph = ph.astype(np.float32)
        self.ph_split = np.concatenate(split(ph), axis=1)


def packing(tabs):
    sent = tabs.rows - 8
    free = HALF - tabs.freq
    extra = tabs.mid + 1 - sent
    pieces = -(-tabs.freq // free) if free > 0 else 0
    if sent % 16 or free < 8 or extra < 1 or extra * pieces > 8:
        return up(tabs.rows, 16), []
    steps = []
    for p in range(pieces):
        begin = p * free
        steps.append((begin, min(free, tabs.freq - begin), p * extra, extra))
    return sent, steps


def inside(first, count, value):
    return (value >= first) & (value < first + count)


def pack(tabs, spec):
    sent, steps = packing(tabs)
    if not steps:
        return jnp.concatenate([spec, jnp.zeros((sent - tabs.rows, LANES), F32)], axis=0).astype(BF)
    row = lax.broadcasted_iota(jnp.int32, (8, LANES), 0)
    col = lane_of((8, LANES)) % HALF
    top, rest = spec[:8], spec[sent:]
    for begin, width, where, extra in steps:
        moved = pltpu.roll(rest, tabs.freq - begin, 1)
        if where:
            moved = pltpu.roll(moved, where, 0)
        here = inside(where, extra, row) & inside(tabs.freq, width, col)
        top = jnp.where(here, moved, top)
    return jnp.concatenate([top, spec[8:sent]], axis=0).astype(BF)


def unpack(tabs, sent_spec):
    _, steps = packing(tabs)
    if not steps:
        return sent_spec[: tabs.rows].astype(F32)
    spec = sent_spec.astype(F32)
    row = lax.broadcasted_iota(jnp.int32, (8, LANES), 0)
    col = lane_of((8, LANES)) % HALF
    rest = jnp.zeros((8, LANES), F32)
    for begin, width, where, extra in steps:
        moved = pltpu.roll(spec[:8], LANES - (tabs.freq - begin), 1)
        if where:
            moved = pltpu.roll(moved, 8 - where, 0)
        here = inside(0, extra, row) & inside(begin, width, col)
        rest = jnp.where(here, moved, rest)
    return jnp.concatenate([spec, rest], axis=0)


def dot(a, b, **kw):
    return jnp.dot(a, b, preferred_element_type=F32, **kw)


def swap(x):
    return pltpu.roll(x, HALF, 1)


def lane_of(shape):
    return lax.broadcasted_iota(jnp.int32, shape, len(shape) - 1)


def arrange_body(tabs, kern, out):
    freq, mid, span = tabs.freq, tabs.mid, tabs.span
    number, tall = out.shape[0], up(freq, 8)
    side = jnp.zeros((freq, HALF - freq), F32)
    below = jnp.zeros((tall - freq, LANES), F32)
    rights = []
    for k in range(number):
        both = jnp.concatenate([kern[0, 0, k], side, kern[1, 0, k], side], axis=1)
        rights.append(jnp.concatenate([both, below], axis=0))
    rights = jnp.concatenate(rights, axis=0).astype(BF)
    row = lax.broadcasted_iota(jnp.int32, (LANES, LANES), 0)
    col = lane_of((LANES, LANES))
    same = (row // HALF == col // HALF) & (row % HALF + col % HALF == freq - 1)
    turned = jnp.where(same, jnp.where(row < HALF, 1.0, -1.0), 0.0).astype(BF)
    lefts = dot(rights, turned)
    rights = rights.astype(F32)
    row = lax.broadcasted_iota(jnp.int32, (span, 2 * tall), 0)
    col = lane_of((span, 2 * tall))
    upper = (row <= mid) & (col == mid + row)
    lower = (row > mid) & (row <= 2 * mid) & (col == tall + 2 * mid - row)
    pick = jnp.where(upper | lower, 1.0, 0.0).astype(BF)
    for k in range(0, number, 2):
        columns = [
            jnp.concatenate(
                [rights[m * tall : (m + 1) * tall], lefts[m * tall : (m + 1) * tall]], axis=0
            )
            for m in range(k, min(k + 2, number))
        ]
        res = dot(pick, jnp.concatenate(columns, axis=1).astype(BF))
        for p in range(len(columns)):
            out[k + p] = res[:, p * LANES : (p + 1) * LANES].astype(BF)


def spectra(tabs, slots, theta, fy, fx):
    cells, cell, rows = theta.shape[0], tabs.cell, tabs.rows
    mask = jax.nn.sigmoid(theta).astype(BF).reshape(cells * cell, cell)
    along = dot(mask, fy[...])
    along = along[:, :LANES] + along[:, LANES:]
    sign = jnp.where(lane_of((rows, LANES)) < HALF, 1.0, -1.0)
    row_at = lax.broadcasted_iota(jnp.int32, (rows, LANES), 0)
    centre = jnp.where((row_at == 0) & (lane_of((rows, LANES)) == tabs.mid), 1.0 / slots, 0.0)
    scale = 2.0 / (slots * cell * cell)
    specs = []
    for c in range(cells):
        part = along[c * cell : (c + 1) * cell]
        high = part.astype(BF)
        low = (part - high.astype(F32)).astype(BF)
        res = dot(fx[...], jnp.concatenate([high, low], axis=1))
        res = res[: 2 * rows, :LANES] + res[: 2 * rows, LANES:] + res[2 * rows :, :LANES]
        spec = res[:rows] + swap(res[rows:]) * sign
        specs.append(spec * scale - centre)
    return specs


def first_body(tabs, slots, owner, local, shift, theta, fy, fx, out, table):
    sent = packing(tabs)[0]
    for c, spec in enumerate(spectra(tabs, slots, theta[...], fy, fx)):
        out[c * sent : (c + 1) * sent] = pack(tabs, spec)
    base = theta.shape[0] * sent
    row = lax.broadcasted_iota(jnp.int32, (INFO, LANES), 0)
    col = lane_of((INFO, LANES))
    info = jnp.zeros((INFO, LANES), jnp.int32)
    for i in range(local.shape[0]):
        table[0, i] = owner[i]
        table[1, i] = local[i]
        table[2, i] = shift[i]
        value = jnp.where(row == 0, owner[i], jnp.where(row == 1, local[i], shift[i]))
        info = jnp.where((col == i) & (row < 3), value, info)
    out[base : base + INFO] = info.astype(F32).astype(BF)


def counts(tabs, n, tiles, cells, slots, ph, payload, out):
    z = lax.axis_index("cells")
    base = cells * packing(tabs)[0]
    row = lax.broadcasted_iota(jnp.int32, (tiles * cells, LANES), 0)
    col = lane_of((tiles * cells, LANES))
    shift_at = lax.broadcasted_iota(jnp.int32, (tabs.cell, LANES), 0)
    numbers = []
    for k in range(n):
        info = payload[k][base : base + INFO].astype(F32).astype(jnp.int32)
        owner, local, shift = info[0:1], info[1:2], info[2:3]
        mine = (owner == z) & (local == row % cells) & (col // slots == row // cells)
        mine = mine & (col < tiles * slots)
        chosen = jnp.where(mine, 1.0, 0.0).astype(BF)
        hot = jnp.where(shift == shift_at, 1.0, 0.0).astype(BF)
        numbers.append(
            lax.dot_general(chosen, hot, (((1,), (1,)), ((), ())), preferred_element_type=F32)
        )
    sums = dot(jnp.concatenate(numbers, axis=0).astype(BF), ph[...])
    sums = sums[:, : 2 * LANES] + sums[:, 2 * LANES :]
    for k in range(n):
        place = source(n, z, k)
        part = sums[k * tiles * cells : (k + 1) * tiles * cells]
        out[pl.ds(place * tiles, tiles)] = part.reshape(tiles, cells, 2 * LANES)


def tile_body(tabs, n, cells, tiles, copies, table, dose, *refs):
    payload, (ph, *rest, out, held, wide, tall, near) = refs[:n], refs[n:]
    slots = table.shape[1] // tiles
    z, j = lax.axis_index("cells"), lax.axis_index("kern")
    sent = packing(tabs)[0]
    for k in range(n):
        held[pl.ds(k * cells, cells)] = payload[k][0 : cells * sent].reshape(cells, sent, LANES)
    spec = jnp.zeros((tabs.rows, LANES), F32)
    for s in range(slots):
        i = j * slots + s
        which = source(n, z, table[0, i]) * cells + table[1, i]
        one = unpack(tabs, held[which])
        turn = ph[pl.ds(table[2, i], 1)]
        spec = spec + one * turn[:, :LANES] + swap(one) * turn[:, LANES:]
    tile_gradient(tabs, tiles, copies, spec, dose, rest, out, wide, tall, near)


def again_body(tabs, n, tiles, copies, dose, *refs):
    parts, (*rest, out, wide, tall, near) = refs[:n], refs[n:]
    total = parts[0][...].astype(F32)
    for k in range(1, n):
        total = total + parts[k][...].astype(F32)
    spec = unpack(tabs, total)
    tile_gradient(tabs, tiles, copies, spec, dose, rest, out, wide, tall, near)


def tile_gradient(tabs, tiles, copies, spec, dose, rest, out, wide, tall, near):
    arranged, (target, gyy, gyy_t, gx, gx_t, w, w_t) = rest[:tiles], rest[tiles:]
    rows, cell, grid = tabs.rows, tabs.cell, tabs.grid
    left = lane_of((rows, LANES)) < HALF
    other = swap(spec)
    real = jnp.where(left, spec, other)
    imag = jnp.where(left, other, -spec)
    span, mid = tabs.span, tabs.mid
    rest = jnp.zeros((span - rows, LANES), F32)
    upper = lax.broadcasted_iota(jnp.int32, (span, LANES), 0) <= mid
    real, imag = [jnp.concatenate([part, rest], axis=0) for part in (real, imag)]
    real, imag = [jnp.where(upper, part, pltpu.roll(part, mid, 0)) for part in (real, imag)]
    wanted = target[lax.axis_index("kern")].astype(F32)
    members = [(ref, k) for ref in arranged for k in range(ref.shape[0])]
    number = len(members)
    for m in range(0, number, 2):
        kerns = [ref[k].astype(F32) for ref, k in members[m : m + 2]]
        lines = slice(m * span, (m + len(kerns)) * span)
        wide[lines, :LANES] = jnp.concatenate([k * real for k in kerns], axis=0).astype(BF)
        wide[lines, LANES:] = jnp.concatenate([k * imag for k in kerns], axis=0).astype(BF)
    for first in range(0, number, CHUNK):
        last = min(first + CHUNK, number)
        res = dot(wide[first * span : last * span], gyy[...])
        for m in range(first, last):
            part = res[(m - first) * span : (m - first + 1) * span]
            tall[m] = jnp.concatenate([part[:, :cell], part[:, cell:]], axis=0).astype(BF)
    total = jnp.zeros((grid, cell), F32)
    for m in range(0, number, 2):
        pair = [tall[m + p] for p in range(min(2, number - m))]
        fields = dot(gx[...], jnp.concatenate(pair, axis=1))
        for p in range(len(pair)):
            one = fields[:, p * cell : (p + 1) * cell]
            near[m + p] = one
            total = total + (one[:grid] * one[:grid] + one[grid:] * one[grid:])
    high = total.astype(BF).astype(F32)
    stack = [high, total - high, high]
    if w.shape[1] > 3 * grid:
        stack.append(jnp.zeros((w.shape[1] - 3 * grid, cell), F32))
    image = dot(w[...], jnp.concatenate(stack, axis=0).astype(BF))
    resist = jax.nn.sigmoid(STEEP * (dose[0] * image - 1.0))
    pressure = 4.0 * STEEP * dose[0] * (resist - wanted) * resist * (1.0 - resist)
    push = dot(w_t[...], pressure.astype(BF))
    for m in range(0, number, 2):
        pair = []
        for p in range(min(2, number - m)):
            one = near[m + p]
            pair.append(jnp.concatenate([one[:grid] * push, one[grid:] * push], axis=0))
        back = dot(gx_t[...], jnp.concatenate(pair, axis=1).astype(BF))
        lines = slice(m * span, (m + len(pair)) * span)
        halves = [back[:, p * cell : (p + 1) * cell] for p in range(len(pair))]
        wide[lines, :LANES] = jnp.concatenate([h[:span] for h in halves], axis=0).astype(BF)
        wide[lines, LANES:] = jnp.concatenate([h[span:] for h in halves], axis=0).astype(BF)
    sum_real = jnp.zeros((span, LANES), F32)
    sum_imag = jnp.zeros((span, LANES), F32)
    for first in range(0, number, CHUNK):
        last = min(first + CHUNK, number)
        res = dot(wide[first * span : last * span], gyy_t[...])
        for m in range(first, last):
            ref, k = members[m]
            kern = ref[k].astype(F32)
            part = res[(m - first) * span : (m - first + 1) * span]
            sum_real = sum_real + kern * part[:, :LANES]
            sum_imag = sum_imag + kern * part[:, LANES:]
    sums = []
    for part in (sum_real, sum_imag):
        below = pltpu.roll(jnp.where(upper, 0.0, part), span - mid, 0)
        sums.append((jnp.where(upper, part, 0.0) + below)[:rows])
    sum_real, sum_imag = sums
    grad = jnp.where(left, sum_real + swap(sum_real), swap(sum_imag - swap(sum_imag)))
    grad = pack(tabs, grad)
    for copy in range(copies):
        out[copy] = grad


def gradients(tabs, slots, corners, kern, theta, grads, sums, gy, ex):
    tiles, cells = sums.shape[0], theta.shape[0]
    rows, cell = tabs.rows, tabs.cell
    pieces = []
    own = []
    for t in range(tiles):
        z, j = t // kern, t % kern
        parts = [grads[(z * corners + x) * kern + j].astype(F32) for x in range(corners)]
        own.append(unpack(tabs, sum(parts[1:], parts[0])))
    swapped = [swap(grad) for grad in own]
    for c in range(cells):
        total = jnp.zeros((rows, LANES), F32)
        for t in range(tiles):
            turn = sums[t, c : c + 1]
            total = total + own[t] * turn[:, :LANES] - swapped[t] * turn[:, LANES:]
        pieces.append(total * (2.0 / (slots * cell * cell)))
    rowed = dot(jnp.concatenate(pieces, axis=0).astype(BF), gy[...])
    result = []
    for first in range(0, cells, 2):
        columns = []
        for c in range(first, min(first + 2, cells)):
            part = rowed[c * rows : (c + 1) * rows]
            columns.append(jnp.concatenate([part[:, :cell], part[:, cell:]], axis=0))
        planes = dot(ex[...], jnp.concatenate(columns, axis=1).astype(BF))
        for p in range(len(columns)):
            squash = jax.nn.sigmoid(theta[first + p])
            gradient = planes[:, p * cell : (p + 1) * cell] * squash * (1.0 - squash)
            power = jnp.sum(gradient * gradient, axis=0, keepdims=True)
            power = jnp.sum(power, axis=1, keepdims=True)
            result.append((gradient, LR * lax.rsqrt(power / (cell * cell) + EPS)))
    return result


def update_body(tabs, slots, corners, kern, n, theta, grads, ph, gy, ex, fy, fx, *refs):
    heard, (out, sums, *parts) = refs[:n], refs[n:]
    counts(tabs, n, kern, theta.shape[0], slots, ph, heard, sums)
    for c, (gradient, rate) in enumerate(
        gradients(tabs, slots, corners, kern, theta, grads, sums, gy, ex)
    ):
        out[c] = theta[c] - rate * gradient
    specs = spectra(tabs, slots, out[...], fy, fx)
    swapped = [swap(spec) for spec in specs]
    z, j = lax.axis_index("cells"), lax.axis_index("kern")
    for k in range(n):
        turns = sums[target_of(n, z, k) * kern + j]
        total = jnp.zeros((tabs.rows, LANES), F32)
        for c, spec in enumerate(specs):
            turn = turns[c : c + 1]
            total = total + spec * turn[:, :LANES] + swapped[c] * turn[:, LANES:]
        parts[k][...] = pack(tabs, total)


def last_body(tabs, slots, corners, kern, theta, grads, sums, gy, ex, out, held, ready, sem):
    band = out.shape[1]
    start = pl.multiple_of(lax.axis_index(("corners", "kern")) * band, band)
    copies = []
    for c, (gradient, rate) in enumerate(
        gradients(tabs, slots, corners, kern, theta, grads, sums, gy, ex)
    ):
        held[c] = rate * gradient
        ready[c] = theta[c, pl.ds(start, band)] - held[c, pl.ds(start, band)]
        copies.append(pltpu.make_async_copy(ready.at[c], out.at[c], sem.at[c]))
        copies[-1].start()
    for copy in copies:
        copy.wait()


VMEM = pl.BlockSpec(memory_space=pltpu.VMEM)
SMEM = pl.BlockSpec(memory_space=pltpu.SMEM)


def call(body, scalars, arrays, outs, scratch=(), name=None, far=(), out_far=False):
    many = isinstance(outs, list)
    if name in ("tile", "again"):
        scalars = [pltpu.with_memory_space_constraint(array, pltpu.SMEM) for array in scalars]
    arrays = [
        array if place in far else pltpu.with_memory_space_constraint(array, pltpu.VMEM)
        for place, array in enumerate(arrays)
    ]
    out_spec = pl.BlockSpec(memory_space=pl.ANY) if out_far else VMEM
    return pl.pallas_call(
        body,
        out_shape=outs,
        in_specs=[SMEM] * len(scalars) + [VMEM] * len(arrays),
        out_specs=[
            SMEM if out.memory_space == pltpu.SMEM else VMEM for out in outs
        ] if many else out_spec,
        scratch_shapes=list(scratch),
    )(*scalars, *arrays)


def shape(dims, dtype):
    return pltpu.VMEM(dims, dtype)


def paired(n):
    return n & (n - 1) == 0


def source(n, z, step):
    return z ^ step if paired(n) else lax.rem(z - step + n, n)


def target_of(n, z, step):
    return z ^ step if paired(n) else lax.rem(z + step, n)


def shifted(array, axis, step):
    n = lax.axis_size(axis)
    moves = [(i, i ^ step if paired(n) else (i + step) % n) for i in range(n)]
    return lax.ppermute(array, axis, moves)


def per_device(theta, target, kernels, dose, inst_owner, inst_local, inst_shift):
    n = lax.axis_size("cells")
    n_kern = lax.axis_size("kern")
    n_corners = lax.axis_size("corners")
    cells, cell = theta.shape[0], theta.shape[1]
    tiles = target.shape[0]
    slots = inst_local.shape[0] // tiles
    assert tiles == n_kern
    tabs = Tables(cell, kernels.shape[3])
    inst_owner = inst_owner[:, 0]
    sent = packing(tabs)[0]
    band = cell // (n_kern * n_corners)
    payload, table = call(
        functools.partial(first_body, tabs, slots),
        [inst_owner, inst_local, inst_shift],
        [theta, tabs.fy, tabs.fx],
        [
            shape((cells * sent + INFO, LANES), BF),
            pltpu.SMEM((3, inst_local.shape[0]), jnp.int32),
        ],
        name="first",
        far=(0, 1, 2),
    )
    payloads = [payload]
    for k in range(1, n):
        payloads.append(shifted(payload, "cells", k))
    own = call(
        functools.partial(arrange_body, tabs),
        [],
        [kernels],
        shape((kernels.shape[2], tabs.span, LANES), BF),
        name="arrange",
    )
    arranged = [own]
    for k in range(1, n_kern):
        arranged.append(shifted(own, "kern", k))
    copies = n * n_corners * n_kern
    count = n_kern * kernels.shape[2]
    scratch = [
        pltpu.VMEM((up(count, 2) * tabs.span, 2 * LANES), BF),
        pltpu.VMEM((count, 2 * tabs.span, cell), BF),
        pltpu.VMEM((count, 2 * tabs.grid, cell), F32),
    ]
    common = arranged + [target, tabs.gyy, tabs.gyy_t, tabs.gx, tabs.gx_t, tabs.w, tabs.w_t]
    everyone = ("cells", "corners", "kern")
    grads = call(
        functools.partial(tile_body, tabs, n, cells, tiles, copies),
        [table, dose],
        payloads + [tabs.ph] + common,
        shape((copies, sent, LANES), BF),
        scratch=[pltpu.VMEM((n * cells, sent, LANES), BF)] + scratch,
        name="tile",
    )
    for _ in range(1, ITERS):
        grads = lax.all_to_all(grads, everyone, 0, 0, tiled=True)
        theta, sums, *parts = call(
            functools.partial(update_body, tabs, slots, n_corners, n_kern, n),
            [],
            [theta, grads, tabs.ph_split, tabs.gy, tabs.ex, tabs.fy, tabs.fx] + payloads,
            [shape(theta.shape, F32), shape((n * tiles, cells, 2 * LANES), F32)]
            + [shape((sent, LANES), BF)] * n,
            name="update",
        )
        for k in range(1, n):
            parts[k] = shifted(parts[k], "cells", k)
        grads = call(
            functools.partial(again_body, tabs, n, tiles, copies),
            [dose],
            parts + common,
            shape((copies, sent, LANES), BF),
            scratch=scratch,
            name="again",
        )
    grads = lax.all_to_all(grads, everyone, 0, 0, tiled=True)
    return call(
        functools.partial(last_body, tabs, slots, n_corners, n_kern),
        [],
        [theta, grads, sums, tabs.gy, tabs.ex],
        jax.ShapeDtypeStruct((cells, band, cell), F32),
        scratch=[
            pltpu.VMEM((cells, cell, cell), F32),
            pltpu.VMEM((cells, band, cell), F32),
            pltpu.SemaphoreType.DMA((cells,)),
        ],
        name="last",
        out_far=True,
    )


def solution(mesh):
    in_specs = (
        P(("groups", "cells"), None, None),
        P(("groups", "cells"), None, None),
        P(None, "corners", "kern", None, None),
        P("corners"),
        P(("groups", "cells"), None),
        P(("groups", "cells")),
        P(("groups", "cells")),
    )
    out_specs = P(("groups", "cells"), ("corners", "kern"), None)
    return jax.shard_map(
        per_device, mesh=mesh, in_specs=in_specs, out_specs=out_specs, check_vma=False
    )
```

```python
import functools

import jax
import jax.numpy as jnp
import numpy as np
from jax import lax
from jax.experimental import pallas as pl
from jax.experimental.pallas import tpu as pltpu
from jax.sharding import PartitionSpec as P


ITERS = 2
LR = 0.25
EPS = 1e-06
STEEP = 3.0
LANES = 128
HALF = LANES // 2
INFO = 16
CHUNK = 6
BF = jnp.bfloat16
F32 = jnp.float32


def up(value, step):
    return -(-value // step) * step


def split(array):
    high = np.asarray(array, np.float32).astype(BF)
    low = (np.asarray(array, np.float32) - high.astype(np.float32)).astype(BF)
    return high, low


class Tables:
    def __init__(self, cell, freq):
        self.cell, self.freq = cell, freq
        self.mid = freq // 2
        self.rows = up(self.mid + 1, 8)
        self.grid = min(cell, up(4 * self.mid + 1, 8))
        rows, grid, mid = self.rows, self.grid, self.mid
        turn = 2.0 * np.pi / cell
        f = np.arange(mid + 1)
        g = np.arange(freq) - mid
        pixels = np.arange(cell)
        fy = np.zeros((cell, LANES))
        phase = (pixels[:, None] * g[None, :] % cell) * turn
        fy[:, :freq] = np.cos(phase)
        fy[:, HALF : HALF + freq] = -np.sin(phase)
        self.fy = np.concatenate(split(fy), axis=1)
        fx = np.zeros((2 * rows, cell))
        phase = (f[:, None] * pixels[None, :] % cell) * turn
        fx[: mid + 1] = np.cos(phase)
        fx[rows : rows + mid + 1] = np.sin(phase)
        self.fx = np.concatenate(split(fx), axis=0)
        ex = np.concatenate([fx[:rows].T, -fx[rows:].T], axis=1)
        self.ex = ex.astype(np.float32).astype(BF)
        gy = np.zeros((LANES, 2 * cell))
        phase = (g[:, None] * pixels[None, :] % cell) * turn
        gy[:freq, :cell] = np.cos(phase)
        gy[:freq, cell:] = np.sin(phase)
        gy[HALF : HALF + freq, :cell] = -np.sin(phase)
        gy[HALF : HALF + freq, cell:] = np.cos(phase)
        self.gy = gy.astype(np.float32).astype(BF)
        both = np.concatenate([gy, np.roll(gy, HALF, axis=0)], axis=0)
        self.gyy = both.astype(np.float32).astype(BF)
        self.gyy_t = self.gyy.T.copy()
        self.span = up(2 * mid + 1, 8)
        phase = (f[None, :] * np.arange(grid)[:, None] % grid) * (2.0 * np.pi / grid)
        blank = np.zeros((grid, self.span - 2 * mid - 1))
        cos, sin = np.cos(phase), np.sin(phase)
        upper = [cos, cos[:, 1:], blank, -sin, -sin[:, 1:], blank]
        lower = [sin, -sin[:, 1:], blank, cos, -cos[:, 1:], blank]
        gx = np.concatenate([np.concatenate(r, axis=1) for r in (upper, lower)], axis=0)
        self.gx = gx.astype(np.float32).astype(BF)
        self.gx_t = self.gx.T.copy()
        u = np.arange(-2 * mid, 2 * mid + 1)
        if grid == cell:
            weights = np.eye(cell)
        else:
            diff = pixels[:, None] / cell - np.arange(grid)[None, :] / grid
            weights = np.cos(2.0 * np.pi * diff[:, :, None] * u).sum(-1) / grid
        high, low = split(weights)
        self.w = np.zeros((cell, up(3 * grid, 16)), np.float32).astype(BF)
        self.w[:, : 3 * grid] = np.concatenate([high, high, low], axis=1)
        self.w_t = high.T.copy()
        ph = np.zeros((cell, 2 * LANES))
        phase = (pixels[:, None] * g[None, :] % cell) * turn
        ph[:, :freq] = ph[:, HALF : HALF + freq] = np.cos(phase)
        ph[:, LANES : LANES + freq] = np.sin(phase)
        ph[:, LANES + HALF : LANES + HALF + freq] = -np.sin(phase)
        self.ph = ph.astype(np.float32)
        self.ph_split = np.concatenate(split(ph), axis=1)


def packing(tabs):
    sent = tabs.rows - 8
    free = HALF - tabs.freq
    extra = tabs.mid + 1 - sent
    pieces = -(-tabs.freq // free) if free > 0 else 0
    if sent % 16 or free < 8 or extra < 1 or extra * pieces > 8:
        return up(tabs.rows, 16), []
    steps = []
    for p in range(pieces):
        begin = p * free
        steps.append((begin, min(free, tabs.freq - begin), p * extra, extra))
    return sent, steps


def inside(first, count, value):
    return (value >= first) & (value < first + count)


def pack(tabs, spec):
    sent, steps = packing(tabs)
    if not steps:
        return jnp.concatenate([spec, jnp.zeros((sent - tabs.rows, LANES), F32)], axis=0).astype(BF)
    row = lax.broadcasted_iota(jnp.int32, (8, LANES), 0)
    col = lane_of((8, LANES)) % HALF
    top, rest = spec[:8], spec[sent:]
    for begin, width, where, extra in steps:
        moved = pltpu.roll(rest, tabs.freq - begin, 1)
        if where:
            moved = pltpu.roll(moved, where, 0)
        here = inside(where, extra, row) & inside(tabs.freq, width, col)
        top = jnp.where(here, moved, top)
    return jnp.concatenate([top, spec[8:sent]], axis=0).astype(BF)


def unpack(tabs, sent_spec):
    _, steps = packing(tabs)
    if not steps:
        return sent_spec[: tabs.rows].astype(F32)
    spec = sent_spec.astype(F32)
    row = lax.broadcasted_iota(jnp.int32, (8, LANES), 0)
    col = lane_of((8, LANES)) % HALF
    rest = jnp.zeros((8, LANES), F32)
    for begin, width, where, extra in steps:
        moved = pltpu.roll(spec[:8], LANES - (tabs.freq - begin), 1)
        if where:
            moved = pltpu.roll(moved, 8 - where, 0)
        here = inside(0, extra, row) & inside(begin, width, col)
        rest = jnp.where(here, moved, rest)
    return jnp.concatenate([spec, rest], axis=0)


def dot(a, b, **kw):
    return jnp.dot(a, b, preferred_element_type=F32, **kw)


def swap(x):
    return pltpu.roll(x, HALF, 1)


def lane_of(shape):
    return lax.broadcasted_iota(jnp.int32, shape, len(shape) - 1)


def arrange_body(tabs, kern, out):
    freq, mid, span = tabs.freq, tabs.mid, tabs.span
    number, tall = out.shape[0], up(freq, 8)
    side = jnp.zeros((freq, HALF - freq), F32)
    below = jnp.zeros((tall - freq, LANES), F32)
    rights = []
    for k in range(number):
        both = jnp.concatenate([kern[0, 0, k], side, kern[1, 0, k], side], axis=1)
        rights.append(jnp.concatenate([both, below], axis=0))
    rights = jnp.concatenate(rights, axis=0).astype(BF)
    row = lax.broadcasted_iota(jnp.int32, (LANES, LANES), 0)
    col = lane_of((LANES, LANES))
    same = (row // HALF == col // HALF) & (row % HALF + col % HALF == freq - 1)
    turned = jnp.where(same, jnp.where(row < HALF, 1.0, -1.0), 0.0).astype(BF)
    lefts = dot(rights, turned)
    rights = rights.astype(F32)
    row = lax.broadcasted_iota(jnp.int32, (span, 2 * tall), 0)
    col = lane_of((span, 2 * tall))
    upper = (row <= mid) & (col == mid + row)
    lower = (row > mid) & (row <= 2 * mid) & (col == tall + 2 * mid - row)
    pick = jnp.where(upper | lower, 1.0, 0.0).astype(BF)
    for k in range(0, number, 2):
        columns = [
            jnp.concatenate(
                [rights[m * tall : (m + 1) * tall], lefts[m * tall : (m + 1) * tall]], axis=0
            )
            for m in range(k, min(k + 2, number))
        ]
        res = dot(pick, jnp.concatenate(columns, axis=1).astype(BF))
        for p in range(len(columns)):
            out[k + p] = res[:, p * LANES : (p + 1) * LANES].astype(BF)


def spectra(tabs, slots, theta, fy, fx):
    cells, cell, rows = theta.shape[0], tabs.cell, tabs.rows
    mask = jax.nn.sigmoid(theta).astype(BF).reshape(cells * cell, cell)
    along = dot(mask, fy[...])
    along = along[:, :LANES] + along[:, LANES:]
    sign = jnp.where(lane_of((rows, LANES)) < HALF, 1.0, -1.0)
    row_at = lax.broadcasted_iota(jnp.int32, (rows, LANES), 0)
    centre = jnp.where((row_at == 0) & (lane_of((rows, LANES)) == tabs.mid), 1.0 / slots, 0.0)
    scale = 2.0 / (slots * cell * cell)
    specs = []
    for c in range(cells):
        part = along[c * cell : (c + 1) * cell]
        high = part.astype(BF)
        low = (part - high.astype(F32)).astype(BF)
        res = dot(fx[...], jnp.concatenate([high, low], axis=1))
        res = res[: 2 * rows, :LANES] + res[: 2 * rows, LANES:] + res[2 * rows :, :LANES]
        spec = res[:rows] + swap(res[rows:]) * sign
        specs.append(spec * scale - centre)
    return specs


def first_body(tabs, slots, owner, local, shift, theta, fy, fx, out, table):
    sent = packing(tabs)[0]
    for c, spec in enumerate(spectra(tabs, slots, theta[...], fy, fx)):
        out[c * sent : (c + 1) * sent] = pack(tabs, spec)
    base = theta.shape[0] * sent
    row = lax.broadcasted_iota(jnp.int32, (INFO, LANES), 0)
    col = lane_of((INFO, LANES))
    info = jnp.zeros((INFO, LANES), jnp.int32)
    for i in range(local.shape[0]):
        table[0, i] = owner[i]
        table[1, i] = local[i]
        table[2, i] = shift[i]
        value = jnp.where(row == 0, owner[i], jnp.where(row == 1, local[i], shift[i]))
        info = jnp.where((col == i) & (row < 3), value, info)
    out[base : base + INFO] = info.astype(F32).astype(BF)


def counts(tabs, n, tiles, cells, slots, ph, payload, out):
    z = lax.axis_index("cells")
    base = cells * packing(tabs)[0]
    row = lax.broadcasted_iota(jnp.int32, (tiles * cells, LANES), 0)
    col = lane_of((tiles * cells, LANES))
    shift_at = lax.broadcasted_iota(jnp.int32, (tabs.cell, LANES), 0)
    numbers = []
    for k in range(n):
        info = payload[k][base : base + INFO].astype(F32).astype(jnp.int32)
        owner, local, shift = info[0:1], info[1:2], info[2:3]
        mine = (owner == z) & (local == row % cells) & (col // slots == row // cells)
        mine = mine & (col < tiles * slots)
        chosen = jnp.where(mine, 1.0, 0.0).astype(BF)
        hot = jnp.where(shift == shift_at, 1.0, 0.0).astype(BF)
        numbers.append(
            lax.dot_general(chosen, hot, (((1,), (1,)), ((), ())), preferred_element_type=F32)
        )
    sums = dot(jnp.concatenate(numbers, axis=0).astype(BF), ph[...])
    sums = sums[:, : 2 * LANES] + sums[:, 2 * LANES :]
    for k in range(n):
        place = source(n, z, k)
        part = sums[k * tiles * cells : (k + 1) * tiles * cells]
        out[pl.ds(place * tiles, tiles)] = part.reshape(tiles, cells, 2 * LANES)


def tile_body(tabs, n, cells, tiles, copies, table, dose, *refs):
    payload, (ph, *rest, out, held, wide, tall, near) = refs[:n], refs[n:]
    slots = table.shape[1] // tiles
    z, j = lax.axis_index("cells"), lax.axis_index("kern")
    sent = packing(tabs)[0]
    for k in range(n):
        held[pl.ds(k * cells, cells)] = payload[k][0 : cells * sent].reshape(cells, sent, LANES)
    spec = jnp.zeros((tabs.rows, LANES), F32)
    cross = spec
    for s in range(slots):
        i = j * slots + s
        which = source(n, z, table[0, i]) * cells + table[1, i]
        one = unpack(tabs, held[which])
        turn = ph[pl.ds(table[2, i], 1)]
        spec = spec + one * turn[:, :LANES]
        cross = cross + one * turn[:, LANES:]
    spec = spec - swap(cross)
    tile_gradient(tabs, tiles, copies, spec, dose, rest, out, wide, tall, near)


def again_body(tabs, n, tiles, copies, dose, *refs):
    parts, (*rest, out, wide, tall, near) = refs[:n], refs[n:]
    total = parts[0][...].astype(F32)
    for k in range(1, n):
        total = total + parts[k][...].astype(F32)
    spec = unpack(tabs, total)
    tile_gradient(tabs, tiles, copies, spec, dose, rest, out, wide, tall, near)


def tile_gradient(tabs, tiles, copies, spec, dose, rest, out, wide, tall, near):
    arranged, (target, gyy, gyy_t, gx, gx_t, w, w_t) = rest[:tiles], rest[tiles:]
    rows, cell, grid = tabs.rows, tabs.cell, tabs.grid
    left = lane_of((rows, LANES)) < HALF
    other = swap(spec)
    real = jnp.where(left, spec, other)
    imag = jnp.where(left, other, -spec)
    span, mid = tabs.span, tabs.mid
    rest = jnp.zeros((span - rows, LANES), F32)
    upper = lax.broadcasted_iota(jnp.int32, (span, LANES), 0) <= mid
    real, imag = [jnp.concatenate([part, rest], axis=0) for part in (real, imag)]
    real, imag = [jnp.where(upper, part, pltpu.roll(part, mid, 0)) for part in (real, imag)]
    wanted = target[lax.axis_index("kern")].astype(F32)
    members = [(ref, k) for ref in arranged for k in range(ref.shape[0])]
    number = len(members)
    for m in range(0, number, 2):
        kerns = [ref[k].astype(F32) for ref, k in members[m : m + 2]]
        lines = slice(m * span, (m + len(kerns)) * span)
        wide[lines, :LANES] = jnp.concatenate([k * real for k in kerns], axis=0).astype(BF)
        wide[lines, LANES:] = jnp.concatenate([k * imag for k in kerns], axis=0).astype(BF)
    for first in range(0, number, CHUNK):
        last = min(first + CHUNK, number)
        res = dot(wide[first * span : last * span], gyy[...])
        for m in range(first, last):
            part = res[(m - first) * span : (m - first + 1) * span]
            tall[m] = jnp.concatenate([part[:, :cell], part[:, cell:]], axis=0).astype(BF)
    total = jnp.zeros((grid, cell), F32)
    for m in range(0, number, 2):
        pair = [tall[m + p] for p in range(min(2, number - m))]
        fields = dot(gx[...], jnp.concatenate(pair, axis=1))
        for p in range(len(pair)):
            one = fields[:, p * cell : (p + 1) * cell]
            near[m + p] = one
            total = total + (one[:grid] * one[:grid] + one[grid:] * one[grid:])
    high = total.astype(BF).astype(F32)
    stack = [high, total - high, high]
    if w.shape[1] > 3 * grid:
        stack.append(jnp.zeros((w.shape[1] - 3 * grid, cell), F32))
    image = dot(w[...], jnp.concatenate(stack, axis=0).astype(BF))
    resist = jax.nn.sigmoid(STEEP * (dose[0] * image - 1.0))
    pressure = 4.0 * STEEP * dose[0] * (resist - wanted) * resist * (1.0 - resist)
    push = dot(w_t[...], pressure.astype(BF))
    for m in range(0, number, 2):
        pair = []
        for p in range(min(2, number - m)):
            one = near[m + p]
            pair.append(jnp.concatenate([one[:grid] * push, one[grid:] * push], axis=0))
        back = dot(gx_t[...], jnp.concatenate(pair, axis=1).astype(BF))
        lines = slice(m * span, (m + len(pair)) * span)
        halves = [back[:, p * cell : (p + 1) * cell] for p in range(len(pair))]
        wide[lines, :LANES] = jnp.concatenate([h[:span] for h in halves], axis=0).astype(BF)
        wide[lines, LANES:] = jnp.concatenate([h[span:] for h in halves], axis=0).astype(BF)
    sum_real = jnp.zeros((span, LANES), F32)
    sum_imag = jnp.zeros((span, LANES), F32)
    for first in range(0, number, CHUNK):
        last = min(first + CHUNK, number)
        res = dot(wide[first * span : last * span], gyy_t[...])
        for m in range(first, last):
            ref, k = members[m]
            kern = ref[k].astype(F32)
            part = res[(m - first) * span : (m - first + 1) * span]
            sum_real = sum_real + kern * part[:, :LANES]
            sum_imag = sum_imag + kern * part[:, LANES:]
    sums = []
    for part in (sum_real, sum_imag):
        below = pltpu.roll(jnp.where(upper, 0.0, part), span - mid, 0)
        sums.append((jnp.where(upper, part, 0.0) + below)[:rows])
    sum_real, sum_imag = sums
    grad = jnp.where(left, sum_real + swap(sum_real), swap(sum_imag - swap(sum_imag)))
    grad = pack(tabs, grad)
    for copy in range(copies):
        out[copy] = grad


def gradients(tabs, slots, corners, kern, theta, grads, sums, gy, ex):
    tiles, cells = sums.shape[0], theta.shape[0]
    rows, cell = tabs.rows, tabs.cell
    pieces = []
    own = []
    for t in range(tiles):
        z, j = t // kern, t % kern
        parts = [grads[(z * corners + x) * kern + j].astype(F32) for x in range(corners)]
        own.append(unpack(tabs, sum(parts[1:], parts[0])))
    for c in range(cells):
        total, cross = jnp.zeros((rows, LANES), F32), jnp.zeros((rows, LANES), F32)
        for t in range(tiles):
            turn = sums[t, c : c + 1]
            total = total + own[t] * turn[:, :LANES]
            cross = cross + own[t] * turn[:, LANES:]
        pieces.append((total + swap(cross)) * (2.0 / (slots * cell * cell)))
    rowed = dot(jnp.concatenate(pieces, axis=0).astype(BF), gy[...])
    result = []
    for first in range(0, cells, 2):
        columns = []
        for c in range(first, min(first + 2, cells)):
            part = rowed[c * rows : (c + 1) * rows]
            columns.append(jnp.concatenate([part[:, :cell], part[:, cell:]], axis=0))
        planes = dot(ex[...], jnp.concatenate(columns, axis=1).astype(BF))
        for p in range(len(columns)):
            squash = jax.nn.sigmoid(theta[first + p])
            gradient = planes[:, p * cell : (p + 1) * cell] * squash * (1.0 - squash)
            power = jnp.sum(gradient * gradient, axis=0, keepdims=True)
            power = jnp.sum(power, axis=1, keepdims=True)
            result.append((gradient, LR * lax.rsqrt(power / (cell * cell) + EPS)))
    return result


def update_body(tabs, slots, corners, kern, n, theta, grads, ph, gy, ex, fy, fx, *refs):
    heard, (out, sums, *parts) = refs[:n], refs[n:]
    counts(tabs, n, kern, theta.shape[0], slots, ph, heard, sums)
    for c, (gradient, rate) in enumerate(
        gradients(tabs, slots, corners, kern, theta, grads, sums, gy, ex)
    ):
        out[c] = theta[c] - rate * gradient
    specs = spectra(tabs, slots, out[...], fy, fx)
    z, j = lax.axis_index("cells"), lax.axis_index("kern")
    for k in range(n):
        turns = sums[target_of(n, z, k) * kern + j]
        total = jnp.zeros((tabs.rows, LANES), F32)
        cross = total
        for c, spec in enumerate(specs):
            turn = turns[c : c + 1]
            total = total + spec * turn[:, :LANES]
            cross = cross + spec * turn[:, LANES:]
        total = total - swap(cross)
        parts[k][...] = pack(tabs, total)


def last_body(tabs, slots, corners, kern, theta, grads, sums, gy, ex, out, held, ready, sem):
    band = out.shape[1]
    start = pl.multiple_of(lax.axis_index(("corners", "kern")) * band, band)
    copies = []
    for c, (gradient, rate) in enumerate(
        gradients(tabs, slots, corners, kern, theta, grads, sums, gy, ex)
    ):
        held[c] = rate * gradient
        ready[c] = theta[c, pl.ds(start, band)] - held[c, pl.ds(start, band)]
        copies.append(pltpu.make_async_copy(ready.at[c], out.at[c], sem.at[c]))
        copies[-1].start()
    for copy in copies:
        copy.wait()


VMEM = pl.BlockSpec(memory_space=pltpu.VMEM)
SMEM = pl.BlockSpec(memory_space=pltpu.SMEM)


def call(body, scalars, arrays, outs, scratch=(), name=None, far=(), out_far=False):
    many = isinstance(outs, list)
    if name in ("tile", "again"):
        scalars = [pltpu.with_memory_space_constraint(array, pltpu.SMEM) for array in scalars]
    arrays = [
        array if place in far else pltpu.with_memory_space_constraint(array, pltpu.VMEM)
        for place, array in enumerate(arrays)
    ]
    out_spec = pl.BlockSpec(memory_space=pl.ANY) if out_far else VMEM
    return pl.pallas_call(
        body,
        out_shape=outs,
        in_specs=[SMEM] * len(scalars) + [VMEM] * len(arrays),
        out_specs=[
            SMEM if out.memory_space == pltpu.SMEM else VMEM for out in outs
        ] if many else out_spec,
        scratch_shapes=list(scratch),
    )(*scalars, *arrays)


def shape(dims, dtype):
    return pltpu.VMEM(dims, dtype)


def paired(n):
    return n & (n - 1) == 0


def source(n, z, step):
    return z ^ step if paired(n) else lax.rem(z - step + n, n)


def target_of(n, z, step):
    return z ^ step if paired(n) else lax.rem(z + step, n)


def shifted(array, axis, step):
    n = lax.axis_size(axis)
    moves = [(i, i ^ step if paired(n) else (i + step) % n) for i in range(n)]
    return lax.ppermute(array, axis, moves)


def per_device(theta, target, kernels, dose, inst_owner, inst_local, inst_shift):
    n = lax.axis_size("cells")
    n_kern = lax.axis_size("kern")
    n_corners = lax.axis_size("corners")
    cells, cell = theta.shape[0], theta.shape[1]
    tiles = target.shape[0]
    slots = inst_local.shape[0] // tiles
    assert tiles == n_kern
    tabs = Tables(cell, kernels.shape[3])
    inst_owner = inst_owner[:, 0]
    sent = packing(tabs)[0]
    band = cell // (n_kern * n_corners)
    payload, table = call(
        functools.partial(first_body, tabs, slots),
        [inst_owner, inst_local, inst_shift],
        [theta, tabs.fy, tabs.fx],
        [
            shape((cells * sent + INFO, LANES), BF),
            pltpu.SMEM((3, inst_local.shape[0]), jnp.int32),
        ],
        name="first",
        far=(0, 1, 2),
    )
    payloads = [payload]
    for k in range(1, n):
        payloads.append(shifted(payload, "cells", k))
    own = call(
        functools.partial(arrange_body, tabs),
        [],
        [kernels],
        shape((kernels.shape[2], tabs.span, LANES), BF),
        name="arrange",
    )
    arranged = [own]
    for k in range(1, n_kern):
        arranged.append(shifted(own, "kern", k))
    copies = n * n_corners * n_kern
    count = n_kern * kernels.shape[2]
    scratch = [
        pltpu.VMEM((up(count, 2) * tabs.span, 2 * LANES), BF),
        pltpu.VMEM((count, 2 * tabs.span, cell), BF),
        pltpu.VMEM((count, 2 * tabs.grid, cell), F32),
    ]
    common = arranged + [target, tabs.gyy, tabs.gyy_t, tabs.gx, tabs.gx_t, tabs.w, tabs.w_t]
    everyone = ("cells", "corners", "kern")
    grads = call(
        functools.partial(tile_body, tabs, n, cells, tiles, copies),
        [table, dose],
        payloads + [tabs.ph] + common,
        shape((copies, sent, LANES), BF),
        scratch=[pltpu.VMEM((n * cells, sent, LANES), BF)] + scratch,
        name="tile",
    )
    for _ in range(1, ITERS):
        grads = lax.all_to_all(grads, everyone, 0, 0, tiled=True)
        theta, sums, *parts = call(
            functools.partial(update_body, tabs, slots, n_corners, n_kern, n),
            [],
            [theta, grads, tabs.ph_split, tabs.gy, tabs.ex, tabs.fy, tabs.fx] + payloads,
            [shape(theta.shape, F32), shape((n * tiles, cells, 2 * LANES), F32)]
            + [shape((sent, LANES), BF)] * n,
            name="update",
        )
        for k in range(1, n):
            parts[k] = shifted(parts[k], "cells", k)
        grads = call(
            functools.partial(again_body, tabs, n, tiles, copies),
            [dose],
            parts + common,
            shape((copies, sent, LANES), BF),
            scratch=scratch,
            name="again",
        )
    grads = lax.all_to_all(grads, everyone, 0, 0, tiled=True)
    return call(
        functools.partial(last_body, tabs, slots, n_corners, n_kern),
        [],
        [theta, grads, sums, tabs.gy, tabs.ex],
        jax.ShapeDtypeStruct((cells, band, cell), F32),
        scratch=[
            pltpu.VMEM((cells, cell, cell), F32),
            pltpu.VMEM((cells, band, cell), F32),
            pltpu.SemaphoreType.DMA((cells,)),
        ],
        name="last",
        out_far=True,
    )


def solution(mesh):
    in_specs = (
        P(("groups", "cells"), None, None),
        P(("groups", "cells"), None, None),
        P(None, "corners", "kern", None, None),
        P("corners"),
        P(("groups", "cells"), None),
        P(("groups", "cells")),
        P(("groups", "cells")),
    )
    out_specs = P(("groups", "cells"), ("corners", "kern"), None)
    return jax.shard_map(
        per_device, mesh=mesh, in_specs=in_specs, out_specs=out_specs, check_vma=False
    )
```
